32 devices in a mesh: gx: 2 (over core), gy: 4 (over y, x), gz: 4 (over z).
Axes of the slice: x: 2, y: 2, z: 4, core: 2. Of those that a mesh axis runs over, the one named last changes fastest.
Arguments:
- flow: float32 [4, 64, 64, 1024], P(None, 'gx', 'gz', 'gy'), may hold values from -6 to 6
- positions: float32 [3, 3, 8, 128], P(None, None, ('gx', 'gy'), 'gz'), may hold values from 0 to 1024
- loads: float32 [3, 3, 8, 128], P(None, None, ('gx', 'gy'), 'gz'), may hold values from -120 to 120
- block_list: int32 [2, 4, 4, 2], P('gx', 'gy', 'gz'), may hold values from 0 to 8, as said below
Outputs:
- flow_out: float32 [4, 64, 64, 1024], P(None, 'gx', 'gz', 'gy')
- sampled: float32 [3, 3, 8, 128], P(None, None, ('gx', 'gy'), 'gz')
The draws below stay inside these ranges and needn't reach their ends.
Inputs may be any that keep to these rules, and one draw needn't show every extreme that they name: `block_list`: an entry names a turbine whose rotor reaches that device's cells, or is 8 for an empty slot. No turbine appears twice in one list. Each turbine is named by exactly four devices with one gy index: two neighbours along gx, each with gz index 0 and 1; these four lists hold the same set of turbines. Every list is either full or empty.
All inputs are finite; a program needn't handle non-finite values.
Results may differ from the reference program's by a relative error of at most 0.0003.
Values sent between devices are 32-bit elements; how exact they have to be, the bound alone decides.
No kernel may reach another device: no remote copies, remote signals or barrier semaphores. Data moves between devices by JAX's collectives and lax.ppermute only.
A program may use at most 128 MiB of HBM per device.

```python
import math
import jax
import jax.numpy as jnp
from jax import lax

CX = 32
CY = 256
CZ = 16
P_SIZE = 128
STEPS = 3
ROWS = 1
CAP = 2
TURB = 8
NX = 64
NY = 1024
NZ = 64
N_GX = 2
N_GY = 4
N_GZ = 4


rotation_rate = 0.4


def farm_layout(key):
    base = jax.random.fold_in(key, 4242)
    key_order, key_roll = jax.random.split(base, 2)
    turbine_order = jax.random.permutation(key_order, TURB).astype(jnp.int32)
    slot_table = turbine_order.reshape(ROWS, N_GY, CAP)
    slot_of = jnp.zeros((TURB,), jnp.int32).at[turbine_order].set(jnp.arange(TURB, dtype=jnp.int32))
    roll_amount = jax.random.randint(key_roll, (ROWS, N_GY), 0, CAP).astype(jnp.int32)
    return (slot_table, slot_of, roll_amount)


def draw_block_list(key, part):
    slot_table, slot_of, roll_amount = farm_layout(key)
    grid_x = jnp.arange(N_GX, dtype=jnp.int32)[:, None, None]
    grid_y = jnp.arange(N_GY, dtype=jnp.int32)[None, :, None]
    grid_z = jnp.arange(N_GZ, dtype=jnp.int32)[None, None, :]
    row_index = jnp.minimum(grid_x // 4, ROWS - 1) + 0 * grid_y + 0 * grid_z
    column_y = grid_y + 0 * grid_x + 0 * grid_z
    rows = slot_table[row_index, column_y]
    shift = roll_amount[row_index, column_y] * (grid_x % 2 + 2 * jnp.minimum(grid_z, 1))
    places = (jnp.arange(CAP, dtype=jnp.int32) + shift[..., None]) % CAP
    rolled = jnp.take_along_axis(rows, places, axis=-1)
    listing = ((grid_x % 4 < 2) & (grid_z < 2))[..., None]
    return jnp.where(listing, rolled, TURB).astype(jnp.int32)


def draw_positions(key, part):
    slot_table, slot_of, roll_amount = farm_layout(key)
    local = jax.random.fold_in(key, 99)
    key_x, key_y, key_z, key_phase, key_jitter = jax.random.split(local, 5)
    row_of = (slot_of // (N_GY * CAP)).astype(jnp.float32)
    block_y = (slot_of // CAP % N_GY).astype(jnp.float32)
    place_y = (slot_of % CAP).astype(jnp.float32)
    radius = CZ / 2.0 - 1.0
    pitch_y = CY / CAP
    hub_x = (4.0 * row_of + 1.0) * CX - 0.5 + jax.random.uniform(key_x, (TURB,), jnp.float32, -0.5, 0.5)
    hub_y = block_y * CY + (place_y + 0.5) * pitch_y + jax.random.uniform(key_y, (TURB,), jnp.float32, -1.0, 1.0) * (pitch_y / 2.0 - radius - 3.0)
    hub_z = CZ - 0.5 + jax.random.uniform(key_z, (TURB,), jnp.float32, -0.5, 0.5)
    phase = jax.random.uniform(key_phase, (TURB,), jnp.float32, 0.0, 2.0 * math.pi)
    point_index = jnp.arange(P_SIZE, dtype=jnp.int32)
    blade = (point_index % 3).astype(jnp.float32)
    span = radius * ((point_index // 3).astype(jnp.float32) + 0.5) / ((P_SIZE + 2) // 3)
    step_angle = rotation_rate * jnp.arange(STEPS, dtype=jnp.float32)
    angle = phase[None, :, None] + step_angle[:, None, None] + 2.0 * math.pi / 3.0 * blade[None, None, :]
    jitter = jax.random.uniform(key_jitter, (STEPS, 3, TURB, P_SIZE), jnp.float32, -0.3, 0.3)
    pos_x = hub_x[None, :, None] + 0.0 * angle + jitter[:, 0]
    pos_y = hub_y[None, :, None] + span[None, None, :] * jnp.sin(angle) + jitter[:, 1]
    pos_z = hub_z[None, :, None] + span[None, None, :] * jnp.cos(angle) + jitter[:, 2]
    return jnp.stack([pos_x, pos_y, pos_z], axis=1).astype(jnp.float32)


def block_levels(key, shape, cuts, low, largest):
    loudness = 1.0
    for position, parts in cuts:
        steps = jax.random.uniform(jax.random.fold_in(jax.random.fold_in(key, 6), position), (parts,), jnp.float32, low / len(cuts), largest / len(cuts))
        loudness = loudness * jnp.repeat(jnp.exp(steps), shape[position] // parts).reshape((-1,) + (1,) * (len(shape) - 1 - position))
    return loudness


def gaussian(stream_key, dims, scale, bound, cuts=(), held_as=jnp.bfloat16):
    drawn = scale * jax.random.normal(stream_key, dims, jnp.float32)
    if cuts:
        drawn = drawn * block_levels(stream_key, dims, cuts, -0.22, 0.18)
    return jnp.clip(drawn, -bound, bound).astype(held_as)


def setup_inputs(seed: int = 0) -> dict:
    arg_keys = jax.random.split(jax.random.key(seed), 5)
    flow = gaussian(arg_keys[0], (4, NX, NZ, NY), 1.0, 6.0, ((1, 2), (2, 4), (3, 4)), jnp.float32)
    positions = draw_positions(jax.random.fold_in(arg_keys[4], 71), 0)
    loads = gaussian(arg_keys[2], (STEPS, 3, TURB, P_SIZE), 20.0, 120.0, ((2, 8), (3, 4)), jnp.float32)
    block_list = draw_block_list(jax.random.fold_in(arg_keys[4], 71), 0)
    return {"flow": flow, "positions": positions, "loads": loads, "block_list": block_list}


kernel_width = 2.0
kernel_norm = 1.0 / (math.pi ** 1.5 * kernel_width ** 3)
time_step = 0.1
smag_coef = 0.17
viscosity = 0.02
diffusivity = 0.02
prandtl = 0.4

def kernel_factors(points, start_x, start_z, start_y, count_x, count_z, count_y):
    cells_x = start_x + jnp.arange(count_x, dtype=jnp.float32)
    cells_y = start_y + jnp.arange(count_y, dtype=jnp.float32)
    cells_z = start_z + jnp.arange(count_z, dtype=jnp.float32)
    factor_x = jnp.exp(-(cells_x[None, :] - points[0][:, None]) ** 2 / kernel_width ** 2)
    factor_y = jnp.exp(-(cells_y[None, :] - points[1][:, None]) ** 2 / kernel_width ** 2)
    factor_z = jnp.exp(-(cells_z[None, :] - points[2][:, None]) ** 2 / kernel_width ** 2)
    return (factor_x, factor_y, factor_z)

def block_terms(velocity, points, loadings, start_x, start_z, start_y):
    count_x, count_z, count_y = (velocity.shape[1], velocity.shape[2], velocity.shape[3])
    width_k = points.shape[1]
    factor_x, factor_y, factor_z = kernel_factors(points, start_x, start_z, start_y, count_x, count_z, count_y)
    weights = jnp.einsum('kx,kz->xzk', factor_x, factor_z, precision=lax.Precision.HIGHEST) * kernel_norm
    spread = loadings[:, None, None, :] * weights[None]
    forcing = jnp.dot(spread.reshape(-1, width_k), factor_y, precision=lax.Precision.HIGHEST)
    forcing = forcing.reshape(3, count_x, count_z, count_y)
    along_y = jnp.dot(velocity.reshape(-1, count_y), factor_y.T, precision=lax.Precision.HIGHEST)
    along_y = along_y.reshape(3, count_x, count_z, width_k)
    samples = lax.optimization_barrier(jnp.sum(along_y * weights[None], axis=(1, 2)))
    return (forcing, samples)

def advance(padded, forcing):
    centre = padded[:, 1:-1, 1:-1, 1:-1]
    plus_x = padded[:, 2:, 1:-1, 1:-1]
    minus_x = padded[:, :-2, 1:-1, 1:-1]
    plus_z = padded[:, 1:-1, 2:, 1:-1]
    minus_z = padded[:, 1:-1, :-2, 1:-1]
    plus_y = padded[:, 1:-1, 1:-1, 2:]
    minus_y = padded[:, 1:-1, 1:-1, :-2]
    grad_x = 0.5 * (plus_x - minus_x)
    grad_y = 0.5 * (plus_y - minus_y)
    grad_z = 0.5 * (plus_z - minus_z)
    laplace = plus_x + minus_x + plus_y + minus_y + plus_z + minus_z - 6.0 * centre
    grads = (grad_x, grad_y, grad_z)
    strain = jnp.zeros_like(centre[0])
    for first in range(3):
        for second in range(3):
            entry = 0.5 * (grads[first][second] + grads[second][first])
            strain = strain + entry * entry
    eddy_visc = smag_coef ** 2 * jnp.sqrt(2.0 * strain)
    velocity = centre[:3]
    transport = velocity[0] * grad_x + velocity[1] * grad_y + velocity[2] * grad_z
    momentum = (viscosity + eddy_visc)[None] * laplace[:3]
    scalar_part = ((diffusivity + eddy_visc / prandtl) * laplace[3])[None]
    diffuse = jnp.concatenate([momentum, scalar_part], axis=0)
    source = jnp.concatenate([forcing, jnp.zeros_like(forcing[:1])], axis=0)
    return centre + time_step * (-transport + diffuse + source)

def reference(flow, positions, loads, block_list):
    device_count = N_GX * N_GY * N_GZ
    lists_flat = block_list.reshape(device_count, CAP)
    zero_index = jnp.zeros((), jnp.int32)
    positions_ext = jnp.concatenate([positions, jnp.zeros((STEPS, 3, 1, P_SIZE), positions.dtype)], axis=2)
    loads_ext = jnp.concatenate([loads, jnp.zeros((STEPS, 3, 1, P_SIZE), loads.dtype)], axis=2)
    sampled_list = []
    fields = flow
    for step_index in range(STEPS):

        def per_device(index):
            block_x = index // (N_GY * N_GZ)
            block_y = index // N_GZ % N_GY
            block_z = index % N_GZ
            starts = (zero_index, (block_x * CX).astype(jnp.int32), (block_z * CZ).astype(jnp.int32), (block_y * CY).astype(jnp.int32))
            velocity = lax.dynamic_slice(fields, starts, (3, CX, CZ, CY))
            turbines = lists_flat[index]
            points = positions_ext[step_index][:, turbines, :].reshape(3, CAP * P_SIZE)
            loadings = loads_ext[step_index][:, turbines, :].reshape(3, CAP * P_SIZE)
            start_x = (block_x * CX).astype(jnp.float32)
            start_z = (block_z * CZ).astype(jnp.float32)
            start_y = (block_y * CY).astype(jnp.float32)
            forcing, samples = block_terms(velocity, points, loadings, start_x, start_z, start_y)
            return (forcing, samples.reshape(3, CAP, P_SIZE))
        forces, pieces = lax.map(per_device, jnp.arange(device_count, dtype=jnp.int32))
        forces = forces.reshape(N_GX, N_GY, N_GZ, 3, CX, CZ, CY).transpose(3, 0, 4, 2, 5, 1, 6).reshape(3, NX, NZ, NY)
        data = pieces.transpose(0, 2, 1, 3).reshape(device_count * CAP, 3, P_SIZE)
        totals = jax.ops.segment_sum(data, lists_flat.reshape(-1), num_segments=TURB + 1)[:TURB]
        sampled_list.append(totals.transpose(1, 0, 2))
        padded = jnp.pad(fields, ((0, 0), (1, 1), (1, 1), (1, 1)))

        def per_slab(block_x):
            start = (block_x * CX).astype(jnp.int32)
            slab = lax.dynamic_slice(padded, (zero_index, start, zero_index, zero_index), (4, CX + 2, NZ + 2, NY + 2))
            pushed = lax.dynamic_slice(forces, (zero_index, start, zero_index, zero_index), (3, CX, NZ, NY))
            return advance(slab, pushed)
        slabs = lax.map(per_slab, jnp.arange(N_GX, dtype=jnp.int32))
        fields = slabs.transpose(1, 0, 2, 3, 4).reshape(4, NX, NZ, NY)
    return (fields, jnp.stack(sampled_list))
```

```python
import functools
import math

import jax
import jax.numpy as jnp
from jax import lax
from jax.experimental import pallas as pl
from jax.experimental.pallas import tpu as pltpu
from jax.sharding import PartitionSpec as P

kernel_width = 2.0
kernel_norm = 1.0 / (math.pi**1.5 * kernel_width**3)
time_step = 0.1
smag_coef = 0.17
viscosity = 0.02
diffusivity = 0.02
prandtl = 0.4
vmem_limit = 48 << 20


def swap_pairs(count, first):
    pairs = []
    for low in range(first, count - 1, 2):
        pairs += [(low, low + 1), (low + 1, low)]
    return pairs


def swap(value, axis, first):
    pairs = swap_pairs(lax.axis_size(axis), first)
    if not pairs:
        return jnp.zeros_like(value)
    return lax.ppermute(value, axis, pairs)


def from_distance(value, axis, distance):
    count = lax.axis_size(axis)
    return lax.ppermute(value, axis, [(i, i ^ distance) for i in range(count)])


def gather_relative(value, axis):
    distance = 1
    while distance < lax.axis_size(axis):
        value = jnp.concatenate([value, from_distance(value, axis, distance)], axis=0)
        distance *= 2
    return value


def pick(flag, first, second):
    return jnp.where(flag, first, second)


def is_even(axis):
    return lax.rem(lax.axis_index(axis), 2) == 0


def write_faces(q_ref, face_refs, shape):
    count_x, count_z, count_y = shape
    xa_ref, xb_ref, za_ref, zb_ref, ya_ref, yb_ref = face_refs
    even_x, even_z, even_y = is_even("gx"), is_even("gz"), is_even("gy")
    low, high = q_ref[:, 0], q_ref[:, count_x - 1]
    xa_ref[...] = pick(even_x, high, low)
    xb_ref[...] = pick(even_x, low, high)
    for comp in range(4):
        low = q_ref[comp, :, 0, :]
        high = q_ref[comp, :, count_z - 1, :]
        za_ref[comp] = pick(even_z, high, low)
        zb_ref[comp] = pick(even_z, low, high)
    lane = lax.broadcasted_iota(jnp.int32, (count_z, 128), 1)
    for comp in range(4):
        low = jnp.zeros((count_z, 128), jnp.float32)
        high = jnp.zeros((count_z, 128), jnp.float32)
        for x in range(count_x):
            first = q_ref[comp, x, :, :128]
            last = q_ref[comp, x, :, count_y - 128 :]
            low = jnp.where(lane == x, pltpu.roll(first, x, 1), low)
            high = jnp.where(lane == x, pltpu.roll(last, (x + 1) % 128, 1), high)
        ya_ref[comp] = pick(even_y, high, low)
        yb_ref[comp] = pick(even_y, low, high)


def faces_body(q_ref, *face_refs, shape):
    write_faces(q_ref, face_refs, shape)


def sorted_slots(list_ref, capacity):
    slots = [list_ref[j] for j in range(capacity)]
    for first in range(capacity):
        for second in range(first + 1, capacity):
            a, b = slots[first], slots[second]
            slots[first], slots[second] = jnp.minimum(a, b), jnp.maximum(a, b)
    return slots


def plane_update(centre, minus_x, plus_x, rows_z, cols_y, pushed, shape):
    count_x, count_z, count_y = shape
    sub = lax.broadcasted_iota(jnp.int32, (count_z, count_y), 0)
    lane = lax.broadcasted_iota(jnp.int32, (count_z, count_y), 1)
    diffs, laplace = [], []
    for comp in range(4):
        c = centre[comp]
        low_z, high_z = rows_z[comp]
        low_y, high_y = cols_y[comp]
        minus_z = jnp.where(sub == 0, low_z, pltpu.roll(c, 1, 0))
        plus_z = jnp.where(sub == count_z - 1, high_z, pltpu.roll(c, count_z - 1, 0))
        minus_y = jnp.where(lane == 0, low_y, pltpu.roll(c, 1, 1))
        plus_y = jnp.where(lane == count_y - 1, high_y, pltpu.roll(c, count_y - 1, 1))
        diffs.append((plus_x[comp] - minus_x[comp], plus_y - minus_y, plus_z - minus_z))
        total = (plus_x[comp] + minus_x[comp]) + (plus_y + minus_y) + (plus_z + minus_z)
        laplace.append(total - 6.0 * c)
    diagonal = diffs[0][0] * diffs[0][0] + diffs[1][1] * diffs[1][1] + diffs[2][2] * diffs[2][2]
    xy = diffs[0][1] + diffs[1][0]
    xz = diffs[0][2] + diffs[2][0]
    yz = diffs[1][2] + diffs[2][1]
    doubled = 0.5 * diagonal + 0.25 * (xy * xy + xz * xz + yz * yz)
    eddy = smag_coef**2 * jnp.sqrt(doubled)
    half = [0.5 * time_step * centre[a] for a in range(3)]
    scale_u = time_step * (viscosity + eddy)
    scale_t = time_step * (diffusivity + eddy / prandtl)
    out = []
    for comp in range(4):
        d = diffs[comp]
        moved = half[0] * d[0] + half[1] * d[1] + half[2] * d[2]
        value = centre[comp] - moved + (scale_u if comp < 3 else scale_t) * laplace[comp]
        if comp < 3:
            value = value + time_step * pushed[comp]
        out.append(value)
    return out


def step_body(
    list_ref, table_ref, q_ref, xa_ref, xb_ref, za_ref, zb_ref, ya_ref, yb_ref, *rest, shape, points, capacity, step, last
):
    count_x, count_z, count_y = shape
    out_ref, sample_ref = rest[:2]
    face_refs = rest[2:-8]
    force_ref, rows_ref, low_ref, high_ref, low_z_ref, high_z_ref, low_y_ref, high_y_ref = rest[-8:]
    index_x, index_y, index_z = lax.axis_index("gx"), lax.axis_index("gy"), lax.axis_index("gz")
    size_x, size_y, size_z = lax.axis_size("gx"), lax.axis_size("gy"), lax.axis_size("gz")
    turbines = size_x * size_y
    slots = sorted_slots(list_ref, capacity)
    listed = slots[0] < turbines
    part = points // size_z

    @pl.when(listed)
    def _():
        for j in range(capacity):
            t = jnp.minimum(slots[j], turbines - 1)
            place_x = lax.bitwise_xor(lax.div(t, size_y), index_x)
            place_y = lax.bitwise_xor(lax.rem(t, size_y), index_y)
            for c in range(size_z):
                place_z = lax.bitwise_xor(index_z, c)
                entry = (place_x * size_y + place_y) * size_z + place_z
                offset = j * points + c * part
                rows_ref[:, offset : offset + part] = table_ref[entry, 8 * step : 8 * step + 8, :]
        rows = rows_ref[...]
        lanes = capacity * points
        start_x = (index_x * count_x).astype(jnp.float32)
        start_z = (index_z * count_z).astype(jnp.float32)
        start_y = (index_y * count_y).astype(jnp.float32)

        def factor(row, start, count):
            cells = lax.broadcasted_iota(jnp.int32, (count, lanes), 0).astype(jnp.float32) + start
            gap = cells - row
            return jnp.exp(-(gap * gap) / kernel_width**2)

        factor_x = factor(rows[0:1], start_x, count_x)
        factor_y = factor(rows[1:2], start_y, count_y)
        factor_z = factor(rows[2:3], start_z, count_z) * kernel_norm
        weights = (factor_x[:, None, :] * factor_z[None, :, :]).reshape(count_x * count_z, lanes)
        for comp in range(3):
            spread = weights * rows[3 + comp : 4 + comp]
            pushed = lax.dot_general(
                spread,
                factor_y,
                (((1,), (1,)), ((), ())),
                precision=lax.Precision.HIGHEST,
                preferred_element_type=jnp.float32,
            )
            force_ref[comp] = pushed.reshape(shape)
            along = jnp.dot(
                q_ref[comp].reshape(count_x * count_z, count_y), factor_y, precision=lax.Precision.HIGHEST, preferred_element_type=jnp.float32
            )
            sample_ref[comp : comp + 1, :] = jnp.sum(along * weights, axis=0, keepdims=True)

    @pl.when(jnp.logical_not(listed))
    def _():
        force_ref[...] = jnp.zeros(force_ref.shape, jnp.float32)
        sample_ref[...] = jnp.zeros(sample_ref.shape, jnp.float32)

    even_x, even_z, even_y = is_even("gx"), is_even("gz"), is_even("gy")
    low_ref[...] = pick(even_x, xb_ref[...], xa_ref[...])
    high_ref[...] = pick(even_x, xa_ref[...], xb_ref[...])
    low_z_ref[...] = pick(even_z, zb_ref[...], za_ref[...])
    high_z_ref[...] = pick(even_z, za_ref[...], zb_ref[...])
    low_y_ref[...] = pick(even_y, yb_ref[...], ya_ref[...])
    high_y_ref[...] = pick(even_y, ya_ref[...], yb_ref[...])

    def plane(x, minus_x, plus_x):
        centre = planes(q_ref, x)
        rows_z, cols_y = [], []
        for comp in range(4):
            rows_z.append((low_z_ref[comp, pl.ds(x, 1), :], high_z_ref[comp, pl.ds(x, 1), :]))
            low_y = pltpu.roll(low_y_ref[comp], (128 - x) % 128 if isinstance(x, int) else 128 - x, 1)
            high_y = pltpu.roll(high_y_ref[comp], 127 - x, 1)
            cols_y.append((jnp.concatenate([low_y, low_y], 1), jnp.concatenate([high_y, high_y], 1)))
        pushed = [force_ref[comp, x] for comp in range(3)]
        for comp, value in enumerate(plane_update(centre, minus_x, plus_x, rows_z, cols_y, pushed, shape)):
            out_ref[comp, x] = value

    def planes(ref, x):
        return [ref[comp, x] for comp in range(4)]

    plane(0, [low_ref[comp] for comp in range(4)], planes(q_ref, 1))

    def middle(x, carry):
        plane(x, planes(q_ref, x - 1), planes(q_ref, x + 1))
        return carry

    lax.fori_loop(1, count_x - 1, middle, 0)
    plane(count_x - 1, planes(q_ref, count_x - 2), [high_ref[comp] for comp in range(4)])
    if not last:
        write_faces(out_ref, face_refs, shape)


def face_shapes(shape):
    count_x, count_z, count_y = shape
    forms = [(4, count_z, count_y)] * 2 + [(4, count_x, count_y)] * 2 + [(4, count_z, 128)] * 2
    return [jax.ShapeDtypeStruct(form, jnp.float32) for form in forms]


def vmem_specs(count):
    return [pl.BlockSpec(memory_space=pltpu.VMEM)] * count


def exchange(faces):
    xa, xb, za, zb, ya, yb = faces
    return [
        swap(za, "gz", 0),
        swap(zb, "gz", 1),
        swap(ya, "gy", 0),
        swap(yb, "gy", 1),
        swap(xa, "gx", 0),
        swap(xb, "gx", 1),
    ]


def shards(flow, positions, loads, block_list):
    capacity = block_list.shape[-1]
    steps_count, _, _, part = positions.shape
    shape = flow.shape[1:]
    count_x, count_z, count_y = shape
    size_x, size_y, size_z = lax.axis_size("gx"), lax.axis_size("gy"), lax.axis_size("gz")
    points = part * size_z
    lanes = capacity * points
    params = pltpu.CompilerParams(vmem_limit_bytes=vmem_limit)
    q = flow
    turbines = block_list.reshape(capacity)

    own = jnp.concatenate([positions.reshape(steps_count, 3, part), loads.reshape(steps_count, 3, part)], axis=1)
    named = sorted_slots(turbines, capacity)
    lists = jnp.pad(jnp.stack(named).astype(jnp.float32), (0, part - capacity))
    own = jnp.concatenate([own, jnp.broadcast_to(lists, (steps_count, 2, part))], axis=1)
    table = own.reshape(1, 8 * steps_count, part)
    for axis in ("gz", "gy", "gx"):
        table = gather_relative(table, axis)

    faces = pl.pallas_call(
        functools.partial(faces_body, shape=shape),
        out_shape=face_shapes(shape),
        in_specs=vmem_specs(1),
        out_specs=vmem_specs(6),
        compiler_params=params,
        name="faces",
    )(q)
    sample_list = []
    for step in range(steps_count):
        last = step == steps_count - 1
        za, zb, ya, yb, xa, xb = exchange(faces)
        shapes = [
            jax.ShapeDtypeStruct(q.shape, jnp.float32),
            jax.ShapeDtypeStruct((3, lanes), jnp.float32),
        ] + ([] if last else face_shapes(shape))
        body = functools.partial(
            step_body, shape=shape, points=points, capacity=capacity, step=step, last=last
        )
        results = pl.pallas_call(
            body,
            out_shape=shapes,
            in_specs=[pl.BlockSpec(memory_space=pltpu.SMEM)] + vmem_specs(8),
            out_specs=vmem_specs(len(shapes)),
            scratch_shapes=[
                pltpu.VMEM((3,) + shape, jnp.float32),
                pltpu.VMEM((8, lanes), jnp.float32),
            ]
            + [pltpu.VMEM(form.shape, jnp.float32) for form in face_shapes(shape)],
            compiler_params=params,
            name="step",
        )(turbines, table, q, xa, xb, za, zb, ya, yb)
        q, samples, faces = results[0], results[1], results[2:]
        sample_list.append(samples)

    sums = jnp.stack(sample_list).reshape(3 * steps_count, capacity, points)
    sums = sums + from_distance(sums, "gz", 1)
    distance = 2
    while distance < size_z:
        sums = sums + from_distance(sums, "gz", distance)
        distance *= 2
    mine = lax.dynamic_slice_in_dim(sums, lax.axis_index("gz") * part, part, axis=2)[None]
    for axis in ("gy", "gx"):
        mine = gather_relative(mine, axis)
    holder = (lax.axis_index("gx") * size_y + lax.axis_index("gy")).astype(jnp.float32)
    named = table[:, 6, :capacity].reshape(-1, size_z, capacity).min(axis=1)
    match = (named == holder).astype(jnp.float32)
    returned = jnp.sum(mine * match[:, None, :, None], axis=(0, 2))
    return q, returned.reshape(positions.shape)


def solution(mesh):
    in_specs = (
        P(None, "gx", "gz", "gy"),
        P(None, None, ("gx", "gy"), "gz"),
        P(None, None, ("gx", "gy"), "gz"),
        P("gx", "gy", "gz", None),
    )
    out_specs = (P(None, "gx", "gz", "gy"), P(None, None, ("gx", "gy"), "gz"))
    return jax.shard_map(shards, mesh=mesh, in_specs=in_specs, out_specs=out_specs, check_vma=False)
```

```python
import functools
import math

import jax
import jax.numpy as jnp
from jax import lax
from jax.experimental import pallas as pl
from jax.experimental.pallas import tpu as pltpu
from jax.sharding import PartitionSpec as P

kernel_width = 2.0
kernel_norm = 1.0 / (math.pi**1.5 * kernel_width**3)
time_step = 0.1
smag_coef = 0.17
viscosity = 0.02
diffusivity = 0.02
prandtl = 0.4
vmem_limit = 48 << 20


def swap_pairs(count, first):
    pairs = []
    for low in range(first, count - 1, 2):
        pairs += [(low, low + 1), (low + 1, low)]
    return pairs


def swap(value, axis, first):
    pairs = swap_pairs(lax.axis_size(axis), first)
    if not pairs:
        return jnp.zeros_like(value)
    return lax.ppermute(value, axis, pairs)


def from_distance(value, axis, distance):
    count = lax.axis_size(axis)
    return lax.ppermute(value, axis, [(i, i ^ distance) for i in range(count)])


def gather_relative(value, axis):
    distance = 1
    while distance < lax.axis_size(axis):
        value = jnp.concatenate([value, from_distance(value, axis, distance)], axis=0)
        distance *= 2
    return value


def pick(flag, first, second):
    return jnp.where(flag, first, second)


def is_even(axis):
    return lax.rem(lax.axis_index(axis), 2) == 0


def write_faces(q_ref, face_refs, shape):
    count_x, count_z, count_y = shape
    za_ref, zb_ref, ya_ref, yb_ref, xa_ref, xb_ref = face_refs
    even_x, even_z, even_y = is_even("gx"), is_even("gz"), is_even("gy")
    low, high = q_ref[:, 0], q_ref[:, count_x - 1]
    xa_ref[...] = pick(even_x, high, low)
    xb_ref[...] = pick(even_x, low, high)
    for comp in range(4):
        low = q_ref[comp, :, 0, :]
        high = q_ref[comp, :, count_z - 1, :]
        za_ref[comp] = pick(even_z, high, low)
        zb_ref[comp] = pick(even_z, low, high)
    lane = lax.broadcasted_iota(jnp.int32, (count_z, 128), 1)
    for comp in range(4):
        low = jnp.zeros((count_z, 128), jnp.float32)
        high = jnp.zeros((count_z, 128), jnp.float32)
        for x in range(count_x):
            first = q_ref[comp, x, :, :128]
            last = q_ref[comp, x, :, count_y - 128 :]
            low = jnp.where(lane == x, pltpu.roll(first, x, 1), low)
            high = jnp.where(lane == x, pltpu.roll(last, (x + 1) % 128, 1), high)
        ya_ref[comp] = pick(even_y, high, low)
        yb_ref[comp] = pick(even_y, low, high)


def faces_body(q_ref, *face_refs, shape):
    write_faces(q_ref, face_refs, shape)


def sorted_slots(list_ref, capacity):
    slots = [list_ref[j] for j in range(capacity)]
    for first in range(capacity):
        for second in range(first + 1, capacity):
            a, b = slots[first], slots[second]
            slots[first], slots[second] = jnp.minimum(a, b), jnp.maximum(a, b)
    return slots


def masks_of(shape):
    count_z = shape[1]
    sub = lax.broadcasted_iota(jnp.int32, (count_z, 128), 0)
    lane = lax.broadcasted_iota(jnp.int32, (count_z, 128), 1)
    return sub == 0, sub == count_z - 1, lane == 0, lane == 127


def tile_update(shifts, pushed):
    diffs, laplace, centre = [], [], []
    for c, minus_x, plus_x, minus_y, plus_y, minus_z, plus_z in shifts:
        diffs.append((plus_x - minus_x, plus_y - minus_y, plus_z - minus_z))
        laplace.append((plus_x + minus_x) + (plus_y + minus_y) + (plus_z + minus_z) - 6.0 * c)
        centre.append(c)
    diagonal = diffs[0][0] * diffs[0][0] + diffs[1][1] * diffs[1][1] + diffs[2][2] * diffs[2][2]
    xy = diffs[0][1] + diffs[1][0]
    xz = diffs[0][2] + diffs[2][0]
    yz = diffs[1][2] + diffs[2][1]
    total = (diagonal + diagonal) + (xy * xy + xz * xz + yz * yz)
    root = total * lax.rsqrt(jnp.maximum(total, 1.1754944e-38))
    scale_u = time_step * viscosity + (0.5 * time_step * smag_coef**2) * root
    scale_t = time_step * diffusivity + (0.5 * time_step * smag_coef**2 / prandtl) * root
    half = [0.5 * time_step * centre[a] for a in range(3)]
    out = []
    for comp in range(4):
        d = diffs[comp]
        moved = half[0] * d[0] + half[1] * d[1] + half[2] * d[2]
        value = centre[comp] - moved + (scale_u if comp < 3 else scale_t) * laplace[comp]
        out.append(value + pushed[comp] if comp < 3 else value)
    return out


def split(value):
    high = value.astype(jnp.bfloat16)
    low = (value - high.astype(jnp.float32)).astype(jnp.bfloat16)
    return high, low


def turbine_rows(rows_ref, table_ref, slots, step, points):
    index_x, index_y, index_z = lax.axis_index("gx"), lax.axis_index("gy"), lax.axis_index("gz")
    size_x, size_y, size_z = lax.axis_size("gx"), lax.axis_size("gy"), lax.axis_size("gz")
    part = points // size_z
    for j, slot in enumerate(slots):
        t = jnp.minimum(slot, size_x * size_y - 1)
        place_x = lax.bitwise_xor(lax.div(t, size_y), index_x)
        place_y = lax.bitwise_xor(lax.rem(t, size_y), index_y)
        for c in range(size_z):
            entry = (place_x * size_y + place_y) * size_z + lax.bitwise_xor(index_z, c)
            offset = j * points + c * part
            rows_ref[:, offset : offset + part] = table_ref[entry, 8 * step : 8 * step + 8, :]
    return rows_ref[...]


def point_factors(rows, shape):
    lanes = rows.shape[1]

    def factor(row, axis, count):
        start = (lax.axis_index(axis) * count).astype(jnp.float32)
        cells = lax.broadcasted_iota(jnp.int32, (count, lanes), 0).astype(jnp.float32) + start
        gap = cells - row
        return jnp.exp(-(gap * gap) / kernel_width**2)

    count_x, count_z, count_y = shape
    factor_x = factor(rows[0:1], "gx", count_x)
    factor_y = factor(rows[1:2], "gy", count_y)
    factor_z = factor(rows[2:3], "gz", count_z) * kernel_norm
    weights = (factor_x[:, None, :] * factor_z[None, :, :]).reshape(count_x * count_z, lanes)
    return weights, split(factor_y)


def push(force_ref, rows, weights, factor_y, shape):
    high, low = factor_y
    right = jnp.concatenate([high, high, low], axis=1)
    for comp in range(3):
        first, second = split(weights * (rows[3 + comp : 4 + comp] * time_step))
        left = jnp.concatenate([first, second, first], axis=1)
        pushed = lax.dot_general(left, right, (((1,), (1,)), ((), ())), preferred_element_type=jnp.float32)
        force_ref[comp] = pushed.reshape(shape)


def sample(q_ref, weights, factor_y, shape):
    count_x, count_z, count_y = shape
    high, low = factor_y
    right = jnp.concatenate([high, high, low], axis=0)
    sums = []
    for comp in range(3):
        first, second = split(q_ref[comp].reshape(count_x * count_z, count_y))
        left = jnp.concatenate([first, second, first], axis=1)
        along = jnp.dot(left, right, preferred_element_type=jnp.float32)
        sums.append(jnp.sum(along * weights, axis=0, keepdims=True))
    return sums


def step_body(*refs, shape, points, capacity, step, steps):
    count_x, count_z, count_y = shape
    last, packs = step == steps - 1, step == steps - 2
    refs = list(refs)
    list_ref, table_ref, q_ref = refs[:3]
    za_ref, zb_ref, ya_ref, yb_ref, xa_ref, xb_ref = refs[3:9]
    refs = refs[9:]
    past_ref = None if step == 0 or last else refs.pop(0)
    out_ref = refs.pop(0)
    if not last:
        face_refs, refs = refs[:6], refs[6:]
        sample_ref = refs.pop(0)
    force_ref, rows_ref, low_z_ref, high_z_ref, low_y_ref, high_y_ref, low_x_ref, high_x_ref = refs
    slots = sorted_slots(list_ref, capacity)
    listed = slots[0] < lax.axis_size("gx") * lax.axis_size("gy")

    if not last:
        sample_ref[...] = jnp.zeros(sample_ref.shape, jnp.float32)
        if past_ref is not None:
            sample_ref[: 3 * step + 3] = past_ref[: 3 * step + 3]

    @pl.when(listed)
    def _():
        rows = turbine_rows(rows_ref, table_ref, slots, step, points)
        weights, factor_y = point_factors(rows, shape)
        push(force_ref, rows, weights, factor_y, shape)
        if step == 0:
            for comp, value in enumerate(sample(q_ref, weights, factor_y, shape)):
                sample_ref[comp : comp + 1] = value

    @pl.when(jnp.logical_not(listed))
    def _():
        force_ref[...] = jnp.zeros(force_ref.shape, jnp.float32)

    even_x, even_z, even_y = is_even("gx"), is_even("gz"), is_even("gy")
    index_y = lax.axis_index("gy")
    tiles = count_y // 128
    for tile in range(tiles):
        first, second = (ref[:4, :, tile * 128 : tile * 128 + 128] for ref in (za_ref, zb_ref))
        low_z_ref[:, tile] = pick(even_z, second, first)
        high_z_ref[:, tile] = pick(even_z, first, second)
    low_y_ref[...] = pick(index_y == 0, 0.0, pick(even_y, yb_ref[:4], ya_ref[:4]))
    high_y_ref[...] = pick(index_y == lax.axis_size("gy") - 1, 0.0, pick(even_y, ya_ref[:4], yb_ref[:4]))
    low_x_ref[...] = pick(even_x, xb_ref[...], xa_ref[...])
    high_x_ref[...] = pick(even_x, xa_ref[...], xb_ref[...])
    first_z, last_z, first_y, last_y = masks_of(shape)

    def plane(x, minus, plus):
        for tile in range(tiles):
            here = slice(tile * 128, tile * 128 + 128)
            shifts = []
            for comp in range(4):
                c = q_ref[comp, x, :, here]
                if tile:
                    before = pltpu.roll(q_ref[comp, x, :, tile * 128 - 128 : tile * 128], 1, 1)
                else:
                    turn = (128 - x) % 128 if isinstance(x, int) else 128 - x
                    before = pltpu.roll(low_y_ref[comp], turn, 1)
                if tile < tiles - 1:
                    after = pltpu.roll(q_ref[comp, x, :, tile * 128 + 128 : tile * 128 + 256], 127, 1)
                else:
                    after = pltpu.roll(high_y_ref[comp], 127 - x, 1)
                minus_y = jnp.where(first_y, before, pltpu.roll(c, 1, 1))
                plus_y = jnp.where(last_y, after, pltpu.roll(c, 127, 1))
                low_z = low_z_ref[comp, tile, pl.ds(x, 1), :]
                high_z = high_z_ref[comp, tile, pl.ds(x, 1), :]
                minus_z = jnp.where(first_z, low_z, pltpu.roll(c, 1, 0))
                plus_z = jnp.where(last_z, high_z, pltpu.roll(c, count_z - 1, 0))
                shifts.append((c, minus(comp, here), plus(comp, here), minus_y, plus_y, minus_z, plus_z))
            pushed = [force_ref[comp, x, :, here] for comp in range(3)]
            for comp, value in enumerate(tile_update(shifts, pushed)):
                out_ref[comp, x, :, here] = value

    def of_plane(x):
        return lambda comp, here: q_ref[comp, x, :, here]

    plane(0, lambda comp, here: low_x_ref[comp, :, here], of_plane(1))

    def middle(x, carry):
        plane(x, of_plane(x - 1), of_plane(x + 1))
        return carry

    lax.fori_loop(1, count_x - 1, middle, 0)
    plane(count_x - 1, of_plane(count_x - 2), lambda comp, here: high_x_ref[comp, :, here])

    if not last:
        za, rest = face_refs[0], face_refs[1:]
        write_faces(out_ref, [za.at[:4]] + list(rest), shape)

        @pl.when(listed)
        def _():
            rows = turbine_rows(rows_ref, table_ref, slots, step + 1, points)
            weights, factor_y = point_factors(rows, shape)
            for comp, value in enumerate(sample(out_ref, weights, factor_y, shape)):
                sample_ref[3 * step + 3 + comp : 3 * step + 4 + comp] = value

        if packs:
            count = 3 * steps
            za[4] = jnp.zeros((count_x, count_y), jnp.float32)
            for j in range(capacity):
                lane, row = (j % 2) * points, (j // 2) * count
                values = sample_ref[:count, j * points : (j + 1) * points]
                za[4, row : row + count, lane : lane + points] = values


def face_shapes(shape, extra=0):
    count_x, count_z, count_y = shape
    forms = [(4 + extra, count_x, count_y), (4, count_x, count_y)]
    forms += [(4, count_z, 128)] * 2 + [(4, count_z, count_y)] * 2
    return [jax.ShapeDtypeStruct(form, jnp.float32) for form in forms]


def vmem_specs(count):
    return [pl.BlockSpec(memory_space=pltpu.VMEM)] * count


def shards(flow, positions, loads, block_list):
    capacity = block_list.shape[-1]
    steps, _, _, part = positions.shape
    shape = flow.shape[1:]
    count_x, count_z, count_y = shape
    size_x, size_y, size_z = lax.axis_size("gx"), lax.axis_size("gy"), lax.axis_size("gz")
    points = part * size_z
    lanes = capacity * points
    params = pltpu.CompilerParams(vmem_limit_bytes=vmem_limit)
    q = flow
    turbines = block_list.reshape(capacity)
    barrier = lax.optimization_barrier

    faces = pl.pallas_call(
        functools.partial(faces_body, shape=shape),
        out_shape=face_shapes(shape),
        in_specs=vmem_specs(1),
        out_specs=vmem_specs(6),
        compiler_params=params,
        name="faces",
    )(q)

    named = block_list.reshape(1, 1, capacity).astype(jnp.float32)
    named = jnp.broadcast_to(jnp.pad(named, ((0, 0), (0, 0), (0, part - capacity))), (steps, 2, part))
    own = [positions.reshape(steps, 3, part), loads.reshape(steps, 3, part), named]
    table = jnp.concatenate(own, axis=1).reshape(1, 8 * steps, part)

    table = jnp.concatenate([table, from_distance(table, "gz", 1)], axis=0)
    waiting = list(faces)
    plan = [(0, "gz", 0), (1, "gz", 1), (2, "gy", 0), (3, "gy", 1), (4, "gx", 0), (5, "gx", 1)]
    hops = []
    for axis in ("gz", "gy", "gx"):
        distance = 2 if axis == "gz" else 1
        while distance < lax.axis_size(axis):
            hops.append((axis, distance))
            distance *= 2
    halos = [None] * 6
    for axis, distance in hops:
        table, waiting = barrier((table, waiting))
        received = from_distance(table, axis, distance)
        if plan:
            place, along, first = plan.pop(0)
            halos[place] = swap(waiting[place], along, first)
        table = jnp.concatenate([table, received], axis=0)
    for place, along, first in plan:
        halos[place] = swap(waiting[place], along, first)

    samples = None
    for step in range(steps):
        last, packs = step == steps - 1, step == steps - 2
        shapes = [jax.ShapeDtypeStruct(q.shape, jnp.float32)]
        if not last:
            shapes += face_shapes(shape, 1 if packs else 0)
            shapes += [jax.ShapeDtypeStruct((16, lanes), jnp.float32)]
        past = [] if step == 0 or last else [samples]
        results = pl.pallas_call(
            functools.partial(step_body, shape=shape, points=points, capacity=capacity, step=step, steps=steps),
            out_shape=shapes,
            in_specs=[pl.BlockSpec(memory_space=pltpu.SMEM)] + vmem_specs(8 + len(past)),
            out_specs=vmem_specs(len(shapes)),
            scratch_shapes=[pltpu.VMEM((3,) + shape, jnp.float32), pltpu.VMEM((8, lanes), jnp.float32)]
            + [pltpu.VMEM((4, count_y // 128, count_x, 128), jnp.float32)] * 2
            + [pltpu.VMEM(form.shape, jnp.float32) for form in face_shapes(shape)[2:]],
            compiler_params=params,
            name="step",
        )(turbines, table, q, *halos, *past)
        q = results[0]
        if last:
            break
        faces, samples = results[1:7], results[7]
        if not packs:
            halos = [swap(faces[place], along, first) for place, along, first in
                     [(0, "gz", 0), (1, "gz", 1), (2, "gy", 0), (3, "gy", 1), (4, "gx", 0), (5, "gx", 1)]]
            continue
        za, zb, ya, yb, xa, xb = faces
        za_in = swap(za, "gz", 0)
        zb_in = swap(zb, "gz", 1)
        sums = za[4] + za_in[4]
        row_blocks = pl.cdiv(3 * steps * pl.cdiv(capacity, 2), count_z)
        blocks = jnp.stack(
            [sums[b * count_z : (b + 1) * count_z, h * 128 : h * 128 + 128] for b in range(row_blocks) for h in range(2)]
        )
        count = blocks.shape[0]
        ya_in = swap(jnp.concatenate([ya, blocks], axis=0), "gy", 0)
        xa_in, xb_in = swap(xa, "gx", 0), swap(xb, "gx", 1)
        pieces = jnp.concatenate([blocks, ya_in[4:]], axis=0)
        yb_in = from_distance(jnp.concatenate([yb, pieces], axis=0), "gy", 3)
        pieces = jnp.concatenate([pieces, yb_in[4:]], axis=0).reshape(size_y, count, count_z, 128)
        halos = [za_in, zb_in, ya_in, yb_in, xa_in, xb_in]

    distance = 2
    while distance < size_z:
        pieces = pieces + from_distance(pieces, "gz", distance)
        distance *= 2
    mine = lax.dynamic_slice_in_dim(pieces, lax.axis_index("gz") * part, part, axis=3)[None]
    mine = gather_relative(mine, "gx")
    mine = mine.reshape(size_x * size_y, row_blocks, 2, count_z, part).transpose(0, 2, 1, 3, 4)
    mine = mine.reshape(size_x * size_y, 2, row_blocks * count_z, part)

    holder = (lax.axis_index("gx") * size_y + lax.axis_index("gy")).astype(jnp.float32)
    listed = table[:, 6, :capacity].reshape(size_x, size_y, size_z, capacity)
    slots = sorted_slots(jnp.moveaxis(listed, -1, 0), capacity)
    order = jnp.stack([jnp.min(slot, axis=2) for slot in slots])
    order = jnp.stack([order[:, :, k] for k in (0, 1, 3, 2)], axis=2).reshape(capacity, size_x * size_y)
    match = (order == holder).astype(jnp.float32)
    returned = 0.0
    for j in range(capacity):
        row = (j // 2) * 3 * steps
        values = mine[:, j % 2, row : row + 3 * steps]
        returned = returned + jnp.sum(values * match[j][:, None, None], axis=0)
    return q, returned.reshape(positions.shape)


def solution(mesh):
    in_specs = (
        P(None, "gx", "gz", "gy"),
        P(None, None, ("gx", "gy"), "gz"),
        P(None, None, ("gx", "gy"), "gz"),
        P("gx", "gy", "gz", None),
    )
    out_specs = (P(None, "gx", "gz", "gy"), P(None, None, ("gx", "gy"), "gz"))
    return jax.shard_map(shards, mesh=mesh, in_specs=in_specs, out_specs=out_specs, check_vma=False)
```

```python
import functools
import math

import jax
import jax.numpy as jnp
from jax import lax
from jax.experimental import pallas as pl
from jax.experimental.pallas import tpu as pltpu
from jax.sharding import PartitionSpec as P

kernel_width = 2.0
kernel_norm = 1.0 / (math.pi**1.5 * kernel_width**3)
time_step = 0.1
smag_coef = 0.17
viscosity = 0.02
diffusivity = 0.02
prandtl = 0.4
vmem_limit = 48 << 20


def swap_pairs(count, first):
    pairs = []
    for low in range(first, count - 1, 2):
        pairs += [(low, low + 1), (low + 1, low)]
    return pairs


def swap(value, axis, first):
    pairs = swap_pairs(lax.axis_size(axis), first)
    if not pairs:
        return jnp.zeros_like(value)
    return lax.ppermute(value, axis, pairs)


def from_distance(value, axis, distance):
    count = lax.axis_size(axis)
    return lax.ppermute(value, axis, [(i, i ^ distance) for i in range(count)])


def gather_relative(value, axis):
    distance = 1
    while distance < lax.axis_size(axis):
        value = jnp.concatenate([value, from_distance(value, axis, distance)], axis=0)
        distance *= 2
    return value


def pick(flag, first, second):
    return jnp.where(flag, first, second)


def is_even(axis):
    return lax.rem(lax.axis_index(axis), 2) == 0


def write_faces(q_ref, face_refs, shape):
    count_x, count_z, count_y = shape
    za_ref, zb_ref, ya_ref, yb_ref, xa_ref = face_refs[:5]
    even_x, even_z, even_y = is_even("gx"), is_even("gz"), is_even("gy")
    low, high = q_ref[:, 0], q_ref[:, count_x - 1]
    xa_ref[...] = pick(even_x, high, low)
    for xb_ref in face_refs[5:]:
        xb_ref[...] = pick(even_x, low, high)
    for comp in range(4):
        low = q_ref[comp, :, 0, :]
        high = q_ref[comp, :, count_z - 1, :]
        za_ref[comp] = pick(even_z, high, low)
        zb_ref[comp] = pick(even_z, low, high)
    lane = lax.broadcasted_iota(jnp.int32, (count_z, 128), 1)
    for comp in range(4):
        low = jnp.zeros((count_z, 128), jnp.float32)
        high = jnp.zeros((count_z, 128), jnp.float32)
        for x in range(count_x):
            first = q_ref[comp, x, :, :128]
            last = q_ref[comp, x, :, count_y - 128 :]
            low = jnp.where(lane == x, pltpu.roll(first, x, 1), low)
            high = jnp.where(lane == x, pltpu.roll(last, (x + 1) % 128, 1), high)
        ya_ref[comp] = pick(even_y, high, low)
        yb_ref[comp] = pick(even_y, low, high)


def faces_body(q_ref, *face_refs, shape):
    write_faces(q_ref, face_refs, shape)


def sorted_slots(list_ref, capacity):
    slots = [list_ref[j] for j in range(capacity)]
    for first in range(capacity):
        for second in range(first + 1, capacity):
            a, b = slots[first], slots[second]
            slots[first], slots[second] = jnp.minimum(a, b), jnp.maximum(a, b)
    return slots


def masks_of(shape):
    count_z = shape[1]
    sub = lax.broadcasted_iota(jnp.int32, (count_z, 128), 0)
    lane = lax.broadcasted_iota(jnp.int32, (count_z, 128), 1)
    return sub == 0, sub == count_z - 1, lane == 0, lane == 127


def tile_update(shifts, pushed):
    diffs, laplace, centre = [], [], []
    for c, minus_x, plus_x, minus_y, plus_y, minus_z, plus_z in shifts:
        diffs.append((plus_x - minus_x, plus_y - minus_y, plus_z - minus_z))
        laplace.append((plus_x + minus_x) + (plus_y + minus_y) + (plus_z + minus_z) - 6.0 * c)
        centre.append(c)
    diagonal = diffs[0][0] * diffs[0][0] + diffs[1][1] * diffs[1][1] + diffs[2][2] * diffs[2][2]
    xy = diffs[0][1] + diffs[1][0]
    xz = diffs[0][2] + diffs[2][0]
    yz = diffs[1][2] + diffs[2][1]
    total = (diagonal + diagonal) + (xy * xy + xz * xz + yz * yz)
    root = total * lax.rsqrt(jnp.maximum(total, 1.1754944e-38))
    scale_u = time_step * viscosity + (0.5 * time_step * smag_coef**2) * root
    scale_t = time_step * diffusivity + (0.5 * time_step * smag_coef**2 / prandtl) * root
    half = [0.5 * time_step * centre[a] for a in range(3)]
    out = []
    for comp in range(4):
        d = diffs[comp]
        moved = half[0] * d[0] + half[1] * d[1] + half[2] * d[2]
        value = centre[comp] - moved + (scale_u if comp < 3 else scale_t) * laplace[comp]
        out.append(value + pushed[comp] if comp < 3 else value)
    return out


def split(value):
    high = value.astype(jnp.bfloat16)
    low = (value - high.astype(jnp.float32)).astype(jnp.bfloat16)
    return high, low


def turbine_rows(rows_ref, table_ref, slots, step, points):
    size_x, size_y = lax.axis_size("gx"), lax.axis_size("gy")
    for j, slot in enumerate(slots):
        t = jnp.minimum(slot, size_x * size_y - 1)
        place_x = lax.bitwise_xor(lax.div(t, size_y), lax.axis_index("gx"))
        place_y = lax.bitwise_xor(lax.rem(t, size_y), lax.axis_index("gy"))
        entry = place_x * size_y + lax.bitwise_xor(place_y, lax.div(place_y, 2))
        rows_ref[:, j * points : (j + 1) * points] = table_ref[entry, 8 * step : 8 * step + 8, :]
    return rows_ref[...]


def point_factors(rows, shape):
    lanes = rows.shape[1]

    def factor(row, axis, count):
        start = (lax.axis_index(axis) * count).astype(jnp.float32)
        cells = lax.broadcasted_iota(jnp.int32, (count, lanes), 0).astype(jnp.float32) + start
        gap = cells - row
        return jnp.exp(-(gap * gap) / kernel_width**2)

    count_x, count_z, count_y = shape
    factor_x = factor(rows[0:1], "gx", count_x)
    factor_y = factor(rows[1:2], "gy", count_y)
    factor_z = factor(rows[2:3], "gz", count_z) * kernel_norm
    weights = (factor_x[:, None, :] * factor_z[None, :, :]).reshape(count_x * count_z, lanes)
    return weights, split(factor_y)


def push(force_ref, rows, weights, factor_y, shape):
    high, low = factor_y
    right = jnp.concatenate([high, high, low], axis=1)
    for comp in range(3):
        first, second = split(weights * (rows[3 + comp : 4 + comp] * time_step))
        left = jnp.concatenate([first, second, first], axis=1)
        pushed = lax.dot_general(left, right, (((1,), (1,)), ((), ())), preferred_element_type=jnp.float32)
        force_ref[comp] = pushed.reshape(shape)


def sample(q_ref, weights, factor_y, shape):
    count_x, count_z, count_y = shape
    high, low = factor_y
    right = jnp.concatenate([high, high, low], axis=0)
    sums = []
    for comp in range(3):
        first, second = split(q_ref[comp].reshape(count_x * count_z, count_y))
        left = jnp.concatenate([first, second, first], axis=1)
        along = jnp.dot(left, right, preferred_element_type=jnp.float32)
        sums.append(jnp.sum(along * weights, axis=0, keepdims=True))
    return sums


def step_body(*refs, shape, points, capacity, step, steps):
    count_x, count_z, count_y = shape
    last, packs = step == steps - 1, step == steps - 2
    faces = len(face_shapes(shape))
    refs = list(refs)
    list_ref, table_ref, q_ref = refs[:3]
    za_ref, zb_ref, ya_ref, yb_ref = refs[3:7]
    x_refs, refs = refs[7 : 3 + faces], refs[3 + faces :]
    past_ref = None if step == 0 or last else refs.pop(0)
    out_ref = refs.pop(0)
    sample_ref = None
    if not last:
        face_refs, refs = refs[:faces], refs[faces:]
        sample_ref = refs.pop(0)
    else:
        far_ref, out_ref, sems = out_ref, refs.pop(0), refs.pop(0)
    force_ref, rows_ref, low_z_ref, high_z_ref, low_y_ref, high_y_ref, low_x_ref, high_x_ref = refs
    slots = sorted_slots(list_ref, capacity)
    turbines = lax.axis_size("gx") * lax.axis_size("gy")
    listed = slots[0] < turbines

    if not last:
        sample_ref[...] = jnp.zeros(sample_ref.shape, jnp.float32)
        if past_ref is not None:
            sample_ref[: 3 * step + 3] = past_ref[: 3 * step + 3]

    @pl.when(listed)
    def _():
        rows = turbine_rows(rows_ref, table_ref, slots, step, points)
        weights, factor_y = point_factors(rows, shape)
        push(force_ref, rows, weights, factor_y, shape)
        if step == 0:
            for comp, value in enumerate(sample(q_ref, weights, factor_y, shape)):
                sample_ref[comp : comp + 1] = value

    @pl.when(jnp.logical_not(listed))
    def _():
        force_ref[...] = jnp.zeros(force_ref.shape, jnp.float32)

    even_x, even_z, even_y = is_even("gx"), is_even("gz"), is_even("gy")
    index_y = lax.axis_index("gy")
    tiles = count_y // 128
    for tile in range(tiles):
        first, second = (ref[:4, :, tile * 128 : tile * 128 + 128] for ref in (za_ref, zb_ref))
        low_z_ref[:, tile] = pick(even_z, second, first)
        high_z_ref[:, tile] = pick(even_z, first, second)
    low_y_ref[...] = pick(index_y == 0, 0.0, pick(even_y, yb_ref[:4], ya_ref[:4]))
    high_y_ref[...] = pick(index_y == lax.axis_size("gy") - 1, 0.0, pick(even_y, ya_ref[:4], yb_ref[:4]))
    first = x_refs[0][...]
    second = x_refs[1][...] if len(x_refs) > 1 else 0.0
    low_x_ref[...] = pick(even_x, second, first)
    high_x_ref[...] = pick(even_x, first, second)
    first_z, last_z, first_y, last_y = masks_of(shape)

    def plane(x, minus, plus):
        centre, up, down = [], [], []
        for comp in range(4):
            row = [q_ref[comp, x, :, tile * 128 : tile * 128 + 128] for tile in range(tiles)]
            turn = (128 - x) % 128 if isinstance(x, int) else 128 - x
            centre.append(row)
            up.append([pltpu.roll(low_y_ref[comp], turn, 1)] + [pltpu.roll(c, 1, 1) for c in row])
            down.append([pltpu.roll(c, 127, 1) for c in row] + [pltpu.roll(high_y_ref[comp], 127 - x, 1)])
        for tile in range(tiles):
            here = slice(tile * 128, tile * 128 + 128)
            shifts = []
            for comp in range(4):
                c = centre[comp][tile]
                minus_y = jnp.where(first_y, up[comp][tile], up[comp][tile + 1])
                plus_y = jnp.where(last_y, down[comp][tile + 1], down[comp][tile])
                low_z = low_z_ref[comp, tile, pl.ds(x, 1), :]
                high_z = high_z_ref[comp, tile, pl.ds(x, 1), :]
                minus_z = jnp.where(first_z, low_z, pltpu.roll(c, 1, 0))
                plus_z = jnp.where(last_z, high_z, pltpu.roll(c, count_z - 1, 0))
                shifts.append((c, minus(comp, here), plus(comp, here), minus_y, plus_y, minus_z, plus_z))
            pushed = [force_ref[comp, x, :, here] for comp in range(3)]
            for comp, value in enumerate(tile_update(shifts, pushed)):
                out_ref[comp, x, :, here] = value

    def of_plane(x):
        return lambda comp, here: q_ref[comp, x, :, here]

    def copy_out(number, start, count):
        here = pl.ds(start, count)
        return pltpu.make_async_copy(out_ref.at[:, here], far_ref.at[:, here], sems.at[number])

    inner = count_x - 2
    group = max(g for g in range(1, 11) if inner % g == 0)

    def middle(trip, carry):
        for k in range(group):
            x = 1 + trip * group + k
            plane(x, of_plane(x - 1), of_plane(x + 1))
        if last:
            copy_out(trip, 1 + trip * group, group).start()
        return carry

    lax.fori_loop(0, inner // group, middle, 0)
    plane(0, lambda comp, here: low_x_ref[comp, :, here], of_plane(1))
    plane(count_x - 1, of_plane(count_x - 2), lambda comp, here: high_x_ref[comp, :, here])

    if last:
        edges = [copy_out(inner // group, 0, 1), copy_out(inner // group + 1, count_x - 1, 1)]
        for edge in edges:
            edge.start()
        for trip in range(inner // group):
            copy_out(trip, 1 + trip * group, group).wait()
        for edge in edges:
            edge.wait()
        return

    za, others = face_refs[0], face_refs[1:]
    write_faces(out_ref, [za.at[:4]] + list(others), shape)

    @pl.when(listed)
    def _():
        rows = turbine_rows(rows_ref, table_ref, slots, step + 1, points)
        weights, factor_y = point_factors(rows, shape)
        for comp, value in enumerate(sample(out_ref, weights, factor_y, shape)):
            sample_ref[3 * step + 3 + comp : 3 * step + 4 + comp] = value

    if packs:
        count = 3 * steps + 1
        za[4] = jnp.zeros((count_x, count_y), jnp.float32)
        for j, slot in enumerate(slots):
            lane, row = (j % 2) * points, (j // 2) * count
            values = sample_ref[: count - 1, j * points : (j + 1) * points]
            za[4, row : row + count - 1, lane : lane + points] = values
            name = jnp.where(listed, 0.5 * (slot + 1).astype(jnp.float32), 0.0)
            za[4, row + count - 1 : row + count, lane : lane + points] = jnp.full((1, points), name)


def face_shapes(shape, extra=0):
    count_x, count_z, count_y = shape
    forms = [(4 + extra, count_x, count_y), (4, count_x, count_y)]
    forms += [(4, count_z, 128)] * 2 + [(4, count_z, count_y)] * (1 if lax.axis_size("gx") == 2 else 2)
    return [jax.ShapeDtypeStruct(form, jnp.float32) for form in forms]


def vmem_specs(count):
    return [pl.BlockSpec(memory_space=pltpu.VMEM)] * count


def swap_faces(faces):
    plan = [("gz", 0), ("gz", 1), ("gy", 0), ("gy", 1), ("gx", 0), ("gx", 1)]
    return [swap(face, axis, first) for face, (axis, first) in zip(faces, plan)]


def true_order(pieces, axis):
    distance = 1
    while distance < pieces.shape[0]:
        swapped = pieces.reshape((-1, 2, distance) + pieces.shape[1:])[:, ::-1].reshape(pieces.shape)
        odd = lax.rem(lax.div(lax.axis_index(axis), distance), 2) == 1
        pieces = jnp.where(odd, swapped, pieces)
        distance *= 2
    return pieces


def shards(flow, positions, loads, block_list):
    capacity = block_list.shape[-1]
    steps, _, _, part = positions.shape
    shape = flow.shape[1:]
    count_x, count_z, count_y = shape
    size_x, size_y, size_z = lax.axis_size("gx"), lax.axis_size("gy"), lax.axis_size("gz")
    points = part * size_z
    lanes = capacity * points
    params = pltpu.CompilerParams(vmem_limit_bytes=vmem_limit)
    q = flow
    turbines = block_list.reshape(capacity)
    barrier = lax.optimization_barrier
    forms = face_shapes(shape)

    own = jnp.concatenate([positions.reshape(steps, 3, part), loads.reshape(steps, 3, part)], axis=1)
    table = jnp.pad(own, ((0, 0), (0, 2), (0, 0))).reshape(1, 8 * steps, part)
    table = jnp.concatenate([table, from_distance(table, "gz", 1)], axis=0)
    faces = pl.pallas_call(
        functools.partial(faces_body, shape=shape),
        out_shape=forms,
        in_specs=vmem_specs(1),
        out_specs=vmem_specs(len(forms)),
        compiler_params=params,
        name="faces",
    )(q)
    table, faces = barrier((table, list(faces)))
    za, zb, ya, yb = faces[:4]
    distance = 2
    while distance < size_z:
        table = jnp.concatenate([table, from_distance(table, "gz", distance)], axis=0)
        distance *= 2
    za, zb = swap(za, "gz", 0), swap(zb, "gz", 1)
    table = true_order(table, "gz")
    table = jnp.concatenate([table[k] for k in range(size_z)], axis=1)
    rows = pl.cdiv(8 * steps, 2 * count_z) * 2 * count_z
    blocks = jnp.pad(table, ((0, rows - 8 * steps), (0, 0))).reshape(rows // count_z, count_z, points)
    blocks, ya, yb, za = barrier((blocks, ya, yb, za))
    ya = swap(jnp.concatenate([ya, blocks], axis=0), "gy", 0)
    blocks = jnp.concatenate([blocks, ya[4:]], axis=0)
    blocks, yb, zb, faces = barrier((blocks, yb, zb, list(faces)))
    yb = from_distance(jnp.concatenate([yb, blocks], axis=0), "gy", 3)
    x_faces = [swap(face, "gx", first) for first, face in enumerate(faces[4:])]
    blocks = jnp.concatenate([blocks, yb[4:]], axis=0)[None]
    table = gather_relative(blocks, "gx").reshape(size_x * size_y, rows, points)
    halos = [za, zb, ya, yb] + x_faces

    samples = None
    for step in range(steps):
        last, packs = step == steps - 1, step == steps - 2
        shapes = [jax.ShapeDtypeStruct(q.shape, jnp.float32)]
        out_specs = vmem_specs(1)
        scratch = []
        if last:
            out_specs = [pl.BlockSpec(memory_space=pl.ANY)]
            scratch = [pltpu.VMEM(q.shape, jnp.float32), pltpu.SemaphoreType.DMA((count_x,))]
        else:
            shapes += face_shapes(shape, 1 if packs else 0)
            if packs:
                scratch = [pltpu.VMEM((16, lanes), jnp.float32)]
            else:
                shapes += [jax.ShapeDtypeStruct((16, lanes), jnp.float32)]
            out_specs = vmem_specs(len(shapes))
        past = [] if step == 0 or last else [samples]
        results = pl.pallas_call(
            functools.partial(step_body, shape=shape, points=points, capacity=capacity, step=step, steps=steps),
            out_shape=shapes,
            in_specs=[pl.BlockSpec(memory_space=pltpu.SMEM)] + vmem_specs(2 + len(halos) + len(past)),
            out_specs=out_specs,
            scratch_shapes=scratch
            + [pltpu.VMEM((3,) + shape, jnp.float32), pltpu.VMEM((8, lanes), jnp.float32)]
            + [pltpu.VMEM((4, count_y // 128, count_x, 128), jnp.float32)] * 2
            + [pltpu.VMEM((4, count_z, 128), jnp.float32)] * 2
            + [pltpu.VMEM((4, count_z, count_y), jnp.float32)] * 2,
            compiler_params=params,
            name="step",
        )(turbines, table, q, *halos, *past)
        q = results[0]
        if last:
            break
        faces = results[1 : 1 + len(forms)]
        if not packs:
            samples = results[-1]
            halos = swap_faces(faces)
            continue
        za, zb, ya, yb = faces[:4]
        za_in, zb_in = swap(za, "gz", 0), swap(zb, "gz", 1)
        sums = za[4] + za_in[4]
        row_blocks = pl.cdiv((3 * steps + 1) * pl.cdiv(capacity, 2), count_z)
        blocks = jnp.stack(
            [sums[b * count_z : (b + 1) * count_z, h * 128 : h * 128 + 128] for b in range(row_blocks) for h in range(2)]
        )
        blocks, ya, zb_in = barrier((blocks, ya, zb_in))
        count = blocks.shape[0]
        ya_in = swap(jnp.concatenate([ya, blocks], axis=0), "gy", 0)
        x_faces = [swap(face, "gx", first) for first, face in enumerate(faces[4:])]
        pieces = jnp.concatenate([blocks, ya_in[4:]], axis=0)
        pieces, yb, x_faces = barrier((pieces, yb, x_faces))
        yb_in = from_distance(jnp.concatenate([yb, pieces], axis=0), "gy", 3)
        pieces = jnp.concatenate([pieces, yb_in[4:]], axis=0).reshape(size_y, count, count_z, 128)
        halos = [za_in, zb_in, ya_in, yb_in] + x_faces

    distance = 2
    while distance < size_z:
        pieces = pieces + from_distance(pieces, "gz", distance)
        distance *= 2
    pieces, q = barrier((pieces, q))
    mine = lax.dynamic_slice_in_dim(pieces, lax.axis_index("gz") * part, part, axis=3)[None]
    mine = gather_relative(mine, "gx")
    mine = mine.reshape(size_x * size_y, row_blocks, 2, count_z, part).transpose(0, 2, 1, 3, 4)
    mine = mine.reshape(size_x * size_y, 2, row_blocks * count_z, part)
    holder = (lax.axis_index("gx") * size_y + lax.axis_index("gy") + 1).astype(jnp.float32)
    returned = 0.0
    for j in range(capacity):
        row = (j // 2) * (3 * steps + 1)
        values = mine[:, j % 2, row : row + 3 * steps]
        match = mine[:, j % 2, row + 3 * steps :][:, :1] == holder
        returned = returned + jnp.sum(jnp.where(match, values, 0.0), axis=0)
    return q, returned.reshape(positions.shape)


def solution(mesh):
    in_specs = (
        P(None, "gx", "gz", "gy"),
        P(None, None, ("gx", "gy"), "gz"),
        P(None, None, ("gx", "gy"), "gz"),
        P("gx", "gy", "gz", None),
    )
    out_specs = (P(None, "gx", "gz", "gy"), P(None, None, ("gx", "gy"), "gz"))
    return jax.shard_map(shards, mesh=mesh, in_specs=in_specs, out_specs=out_specs, check_vma=False)
```

```python
import functools
import math

import jax
import jax.numpy as jnp
from jax import lax
from jax.experimental import pallas as pl
from jax.experimental.pallas import tpu as pltpu
from jax.sharding import PartitionSpec as P

kernel_width = 2.0
kernel_norm = 1.0 / (math.pi**1.5 * kernel_width**3)
time_step = 0.1
smag_coef = 0.17
viscosity = 0.02
diffusivity = 0.02
prandtl = 0.4
vmem_limit = 48 << 20


def swap_pairs(count, first):
    pairs = []
    for low in range(first, count - 1, 2):
        pairs += [(low, low + 1), (low + 1, low)]
    return pairs


def swap(value, axis, first):
    pairs = swap_pairs(lax.axis_size(axis), first)
    if not pairs:
        return jnp.zeros_like(value)
    return lax.ppermute(value, axis, pairs)


def from_distance(value, axis, distance):
    count = lax.axis_size(axis)
    return lax.ppermute(value, axis, [(i, i ^ distance) for i in range(count)])


def gather_relative(value, axis):
    distance = 1
    while distance < lax.axis_size(axis):
        value = jnp.concatenate([value, from_distance(value, axis, distance)], axis=0)
        distance *= 2
    return value


def pick(flag, first, second):
    return jnp.where(flag, first, second)


def is_even(axis):
    return lax.rem(lax.axis_index(axis), 2) == 0


def write_faces(q_ref, face_refs, shape):
    count_x, count_z, count_y = shape
    za_ref, zb_ref, ya_ref, yb_ref, xa_ref = face_refs[:5]
    even_x, even_z, even_y = is_even("gx"), is_even("gz"), is_even("gy")
    low, high = q_ref[:, 0], q_ref[:, count_x - 1]
    xa_ref[...] = pick(even_x, high, low)
    for xb_ref in face_refs[5:]:
        xb_ref[...] = pick(even_x, low, high)
    for comp in range(4):
        low = q_ref[comp, :, 0, :]
        high = q_ref[comp, :, count_z - 1, :]
        za_ref[comp] = pick(even_z, high, low)
        zb_ref[comp] = pick(even_z, low, high)
    lane = lax.broadcasted_iota(jnp.int32, (count_z, 128), 1)
    low = jnp.zeros((count_z, 128), jnp.float32)
    high = jnp.zeros((count_z, 128), jnp.float32)
    for comp in range(4):
        for x in range(count_x):
            place = comp * count_x + x
            first = q_ref[comp, x, :, :128]
            last = q_ref[comp, x, :, count_y - 128 :]
            low = jnp.where(lane == place, pltpu.roll(first, place, 1), low)
            high = jnp.where(lane == place, pltpu.roll(last, (place + 1) % 128, 1), high)
    ya_ref[0] = pick(even_y, high, low)
    yb_ref[0] = pick(even_y, low, high)


def faces_body(q_ref, *face_refs, shape):
    write_faces(q_ref, face_refs, shape)


def sorted_slots(list_ref, capacity):
    slots = [list_ref[j] for j in range(capacity)]
    for first in range(capacity):
        for second in range(first + 1, capacity):
            a, b = slots[first], slots[second]
            slots[first], slots[second] = jnp.minimum(a, b), jnp.maximum(a, b)
    return slots


def masks_of(shape):
    count_z = shape[1]
    sub = lax.broadcasted_iota(jnp.int32, (count_z, 128), 0)
    lane = lax.broadcasted_iota(jnp.int32, (count_z, 128), 1)
    return sub == 0, sub == count_z - 1, lane == 0, lane == 127


def tile_update(shifts, pushed):
    diffs, laplace, centre = [], [], []
    for c, minus_x, plus_x, minus_y, plus_y, minus_z, plus_z in shifts:
        diffs.append((plus_x - minus_x, plus_y - minus_y, plus_z - minus_z))
        laplace.append((plus_x + minus_x) + (plus_y + minus_y) + (plus_z + minus_z) - 6.0 * c)
        centre.append(c)
    diagonal = diffs[0][0] * diffs[0][0] + diffs[1][1] * diffs[1][1] + diffs[2][2] * diffs[2][2]
    xy = diffs[0][1] + diffs[1][0]
    xz = diffs[0][2] + diffs[2][0]
    yz = diffs[1][2] + diffs[2][1]
    total = (diagonal + diagonal) + (xy * xy + xz * xz + yz * yz)
    root = total * lax.rsqrt(jnp.maximum(total, 1.1754944e-38))
    scale_u = time_step * viscosity + (0.5 * time_step * smag_coef**2) * root
    scale_t = time_step * diffusivity + (0.5 * time_step * smag_coef**2 / prandtl) * root
    half = [0.5 * time_step * centre[a] for a in range(3)]
    out = []
    for comp in range(4):
        d = diffs[comp]
        moved = half[0] * d[0] + half[1] * d[1] + half[2] * d[2]
        value = centre[comp] - moved + (scale_u if comp < 3 else scale_t) * laplace[comp]
        out.append(value + pushed[comp] if comp < 3 else value)
    return out


def split(value):
    high = value.astype(jnp.bfloat16)
    low = (value - high.astype(jnp.float32)).astype(jnp.bfloat16)
    return high, low


def turbine_rows(rows_ref, table_ref, slots, step, points):
    size_x, size_y = lax.axis_size("gx"), lax.axis_size("gy")
    for j, slot in enumerate(slots):
        t = jnp.minimum(slot, size_x * size_y - 1)
        place_x = lax.bitwise_xor(lax.div(t, size_y), lax.axis_index("gx"))
        place_y = lax.bitwise_xor(lax.rem(t, size_y), lax.axis_index("gy"))
        entry = place_x * size_y + lax.bitwise_xor(place_y, lax.div(place_y, 2))
        rows_ref[:, j * points : (j + 1) * points] = table_ref[entry, 8 * step : 8 * step + 8, :]
    return rows_ref[...]


def point_factors(rows, shape):
    lanes = rows.shape[1]

    def factor(row, axis, count):
        start = (lax.axis_index(axis) * count).astype(jnp.float32)
        cells = lax.broadcasted_iota(jnp.int32, (count, lanes), 0).astype(jnp.float32) + start
        gap = cells - row
        return jnp.exp(-(gap * gap) / kernel_width**2)

    count_x, count_z, count_y = shape
    factor_x = factor(rows[0:1], "gx", count_x)
    factor_y = factor(rows[1:2], "gy", count_y)
    factor_z = factor(rows[2:3], "gz", count_z) * kernel_norm
    weights = (factor_x[:, None, :] * factor_z[None, :, :]).reshape(count_x * count_z, lanes)
    return weights, split(factor_y)


def push(force_ref, rows, weights, factor_y, shape):
    high, low = factor_y
    right = jnp.concatenate([high, high, low], axis=1)
    for comp in range(3):
        first, second = split(weights * (rows[3 + comp : 4 + comp] * time_step))
        left = jnp.concatenate([first, second, first], axis=1)
        pushed = lax.dot_general(left, right, (((1,), (1,)), ((), ())), preferred_element_type=jnp.float32)
        force_ref[comp] = pushed.reshape(shape)


def sample(q_ref, weights, factor_y, shape):
    count_x, count_z, count_y = shape
    high, low = factor_y
    right = jnp.concatenate([high, high, low], axis=0)
    sums = []
    for comp in range(3):
        first, second = split(q_ref[comp].reshape(count_x * count_z, count_y))
        left = jnp.concatenate([first, second, first], axis=1)
        along = jnp.dot(left, right, preferred_element_type=jnp.float32)
        sums.append(jnp.sum(along * weights, axis=0, keepdims=True))
    return sums


def step_body(*refs, shape, points, capacity, step, steps):
    count_x, count_z, count_y = shape
    last, packs = step == steps - 1, step == steps - 2
    faces = len(face_shapes(shape))
    refs = list(refs)
    list_ref, table_ref, q_ref = refs[:3]
    za_ref, zb_ref, ya_ref, yb_ref = refs[3:7]
    x_refs, refs = refs[7 : 3 + faces], refs[3 + faces :]
    past_ref = None if step == 0 or last else refs.pop(0)
    out_ref = refs.pop(0)
    sample_ref = None
    if not last:
        face_refs, refs = refs[:faces], refs[faces:]
        sample_ref = refs.pop(0)
    else:
        far_ref, out_ref, sems = out_ref, refs.pop(0), refs.pop(0)
    force_ref, rows_ref, low_z_ref, high_z_ref, low_y_ref, high_y_ref, low_x_ref, high_x_ref = refs
    slots = sorted_slots(list_ref, capacity)
    turbines = lax.axis_size("gx") * lax.axis_size("gy")
    listed = slots[0] < turbines

    if not last:
        sample_ref[...] = jnp.zeros(sample_ref.shape, jnp.float32)
        if past_ref is not None:
            sample_ref[: 3 * step + 3] = past_ref[: 3 * step + 3]

    @pl.when(listed)
    def _():
        rows = turbine_rows(rows_ref, table_ref, slots, step, points)
        weights, factor_y = point_factors(rows, shape)
        push(force_ref, rows, weights, factor_y, shape)
        if step == 0:
            for comp, value in enumerate(sample(q_ref, weights, factor_y, shape)):
                sample_ref[comp : comp + 1] = value

    @pl.when(jnp.logical_not(listed))
    def _():
        force_ref[...] = jnp.zeros(force_ref.shape, jnp.float32)

    even_x, even_z, even_y = is_even("gx"), is_even("gz"), is_even("gy")
    index_y = lax.axis_index("gy")
    tiles = count_y // 128
    for tile in range(tiles):
        first, second = (ref[:4, :, tile * 128 : tile * 128 + 128] for ref in (za_ref, zb_ref))
        low_z_ref[:, tile] = pick(even_z, second, first)
        high_z_ref[:, tile] = pick(even_z, first, second)
    low_y_ref[...] = pick(index_y == 0, 0.0, pick(even_y, yb_ref[0], ya_ref[0]))
    high_y_ref[...] = pick(index_y == lax.axis_size("gy") - 1, 0.0, pick(even_y, ya_ref[0], yb_ref[0]))
    first = x_refs[0][...]
    second = x_refs[1][...] if len(x_refs) > 1 else 0.0
    low_x_ref[...] = pick(even_x, second, first)
    high_x_ref[...] = pick(even_x, first, second)
    first_z, last_z, first_y, last_y = masks_of(shape)

    def plane(x, minus, plus):
        centre, up, down = [], [], []
        for comp in range(4):
            row = [q_ref[comp, x, :, tile * 128 : tile * 128 + 128] for tile in range(tiles)]
            place = comp * count_x + x
            turn = (128 - place) % 128 if isinstance(place, int) else 128 - place
            centre.append(row)
            up.append([pltpu.roll(low_y_ref[...], turn, 1)] + [pltpu.roll(c, 1, 1) for c in row])
            down.append([pltpu.roll(c, 127, 1) for c in row] + [pltpu.roll(high_y_ref[...], 127 - place, 1)])
        for tile in range(tiles):
            here = slice(tile * 128, tile * 128 + 128)
            shifts = []
            for comp in range(4):
                c = centre[comp][tile]
                minus_y = jnp.where(first_y, up[comp][tile], up[comp][tile + 1])
                plus_y = jnp.where(last_y, down[comp][tile + 1], down[comp][tile])
                low_z = low_z_ref[comp, tile, pl.ds(x, 1), :]
                high_z = high_z_ref[comp, tile, pl.ds(x, 1), :]
                minus_z = jnp.where(first_z, low_z, pltpu.roll(c, 1, 0))
                plus_z = jnp.where(last_z, high_z, pltpu.roll(c, count_z - 1, 0))
                shifts.append((c, minus(comp, here), plus(comp, here), minus_y, plus_y, minus_z, plus_z))
            pushed = [force_ref[comp, x, :, here] for comp in range(3)]
            for comp, value in enumerate(tile_update(shifts, pushed)):
                out_ref[comp, x, :, here] = value

    def of_plane(x):
        return lambda comp, here: q_ref[comp, x, :, here]

    def copy_out(number, start, count):
        here = pl.ds(start, count)
        return pltpu.make_async_copy(out_ref.at[:, here], far_ref.at[:, here], sems.at[number])

    inner = count_x - 2
    group = max(g for g in range(1, 11) if inner % g == 0)

    def middle(trip, carry):
        for k in range(group):
            x = 1 + trip * group + k
            plane(x, of_plane(x - 1), of_plane(x + 1))
        if last:
            copy_out(trip, 1 + trip * group, group).start()
        return carry

    lax.fori_loop(0, inner // group, middle, 0)
    plane(0, lambda comp, here: low_x_ref[comp, :, here], of_plane(1))
    plane(count_x - 1, of_plane(count_x - 2), lambda comp, here: high_x_ref[comp, :, here])

    if last:
        edges = [copy_out(inner // group, 0, 1), copy_out(inner // group + 1, count_x - 1, 1)]
        for edge in edges:
            edge.start()
        for trip in range(inner // group):
            copy_out(trip, 1 + trip * group, group).wait()
        for edge in edges:
            edge.wait()
        return

    za, others = face_refs[0], face_refs[1:]
    write_faces(out_ref, [za.at[:4]] + list(others), shape)

    @pl.when(listed)
    def _():
        rows = turbine_rows(rows_ref, table_ref, slots, step + 1, points)
        weights, factor_y = point_factors(rows, shape)
        for comp, value in enumerate(sample(out_ref, weights, factor_y, shape)):
            sample_ref[3 * step + 3 + comp : 3 * step + 4 + comp] = value

    if packs:
        count = 3 * steps + 1
        za[4] = jnp.zeros((count_x, count_y), jnp.float32)
        for j, slot in enumerate(slots):
            lane, row = (j % 2) * points, (j // 2) * count
            values = sample_ref[: count - 1, j * points : (j + 1) * points]
            za[4, row : row + count - 1, lane : lane + points] = values
            name = jnp.where(listed, 0.5 * (slot + 1).astype(jnp.float32), 0.0)
            za[4, row + count - 1 : row + count, lane : lane + points] = jnp.full((1, points), name)


def face_shapes(shape, extra=0):
    count_x, count_z, count_y = shape
    forms = [(4 + extra, count_x, count_y), (4, count_x, count_y)]
    forms += [(1, count_z, 128)] * 2 + [(4, count_z, count_y)] * (1 if lax.axis_size("gx") == 2 else 2)
    return [jax.ShapeDtypeStruct(form, jnp.float32) for form in forms]


def vmem_specs(count):
    return [pl.BlockSpec(memory_space=pltpu.VMEM)] * count


def swap_faces(faces):
    plan = [("gz", 0), ("gz", 1), ("gy", 0), ("gy", 1), ("gx", 0), ("gx", 1)]
    return [swap(face, axis, first) for face, (axis, first) in zip(faces, plan)]


def true_order(pieces, axis):
    distance = 1
    while distance < pieces.shape[0]:
        swapped = pieces.reshape((-1, 2, distance) + pieces.shape[1:])[:, ::-1].reshape(pieces.shape)
        odd = lax.rem(lax.div(lax.axis_index(axis), distance), 2) == 1
        pieces = jnp.where(odd, swapped, pieces)
        distance *= 2
    return pieces


def shards(flow, positions, loads, block_list):
    capacity = block_list.shape[-1]
    steps, _, _, part = positions.shape
    shape = flow.shape[1:]
    count_x, count_z, count_y = shape
    size_x, size_y, size_z = lax.axis_size("gx"), lax.axis_size("gy"), lax.axis_size("gz")
    points = part * size_z
    lanes = capacity * points
    params = pltpu.CompilerParams(vmem_limit_bytes=vmem_limit)
    q = flow
    turbines = block_list.reshape(capacity)
    barrier = lax.optimization_barrier
    forms = face_shapes(shape)

    own = jnp.concatenate([positions.reshape(steps, 3, part), loads.reshape(steps, 3, part)], axis=1)
    table = jnp.pad(own, ((0, 0), (0, 2), (0, 0))).reshape(1, 8 * steps, part)
    table = jnp.concatenate([table, from_distance(table, "gz", 1)], axis=0)
    faces = pl.pallas_call(
        functools.partial(faces_body, shape=shape),
        out_shape=forms,
        in_specs=vmem_specs(1),
        out_specs=vmem_specs(len(forms)),
        compiler_params=params,
        name="faces",
    )(q)
    table, faces = barrier((table, list(faces)))
    za, zb, ya, yb = faces[:4]
    distance = 2
    while distance < size_z:
        table = jnp.concatenate([table, from_distance(table, "gz", distance)], axis=0)
        distance *= 2
    za, zb = swap(za, "gz", 0), swap(zb, "gz", 1)
    table = true_order(table, "gz")
    table = jnp.concatenate([table[k] for k in range(size_z)], axis=1)
    rows = pl.cdiv(8 * steps, 2 * count_z) * 2 * count_z
    blocks = jnp.pad(table, ((0, rows - 8 * steps), (0, 0))).reshape(rows // count_z, count_z, points)
    blocks, ya = barrier((blocks, ya))
    ya = swap(jnp.concatenate([ya, blocks], axis=0), "gy", 0)
    blocks = jnp.concatenate([blocks, ya[1:]], axis=0)
    blocks, yb, za = barrier((blocks, yb, za))
    yb = from_distance(jnp.concatenate([yb, blocks], axis=0), "gy", 3)
    x_faces = [swap(face, "gx", first) for first, face in enumerate(faces[4:])]
    blocks = jnp.concatenate([blocks, yb[1:]], axis=0)[None]
    blocks, zb = barrier((blocks, zb))
    table = gather_relative(blocks, "gx").reshape(size_x * size_y, rows, points)
    halos = [za, zb, ya, yb] + x_faces

    samples = None
    for step in range(steps):
        last, packs = step == steps - 1, step == steps - 2
        shapes = [jax.ShapeDtypeStruct(q.shape, jnp.float32)]
        out_specs = vmem_specs(1)
        scratch = []
        if last:
            out_specs = [pl.BlockSpec(memory_space=pl.ANY)]
            scratch = [pltpu.VMEM(q.shape, jnp.float32), pltpu.SemaphoreType.DMA((count_x,))]
        else:
            shapes += face_shapes(shape, 1 if packs else 0)
            if packs:
                scratch = [pltpu.VMEM((16, lanes), jnp.float32)]
            else:
                shapes += [jax.ShapeDtypeStruct((16, lanes), jnp.float32)]
            out_specs = vmem_specs(len(shapes))
        past = [] if step == 0 or last else [samples]
        results = pl.pallas_call(
            functools.partial(step_body, shape=shape, points=points, capacity=capacity, step=step, steps=steps),
            out_shape=shapes,
            in_specs=[pl.BlockSpec(memory_space=pltpu.SMEM)] + vmem_specs(2 + len(halos) + len(past)),
            out_specs=out_specs,
            scratch_shapes=scratch
            + [pltpu.VMEM((3,) + shape, jnp.float32), pltpu.VMEM((8, lanes), jnp.float32)]
            + [pltpu.VMEM((4, count_y // 128, count_x, 128), jnp.float32)] * 2
            + [pltpu.VMEM((count_z, 128), jnp.float32)] * 2
            + [pltpu.VMEM((4, count_z, count_y), jnp.float32)] * 2,
            compiler_params=params,
            name="step",
        )(turbines, table, q, *halos, *past)
        q = results[0]
        if last:
            break
        faces = results[1 : 1 + len(forms)]
        if not packs:
            samples = results[-1]
            halos = swap_faces(faces)
            continue
        za, zb, ya, yb = faces[:4]
        za_in, zb_in = swap(za, "gz", 0), swap(zb, "gz", 1)
        sums = za[4] + za_in[4]
        row_blocks = pl.cdiv((3 * steps + 1) * pl.cdiv(capacity, 2), count_z)
        blocks = jnp.stack(
            [sums[b * count_z : (b + 1) * count_z, h * 128 : h * 128 + 128] for b in range(row_blocks) for h in range(2)]
        )
        blocks, ya, zb_in = barrier((blocks, ya, zb_in))
        count = blocks.shape[0]
        ya_in = swap(jnp.concatenate([ya, blocks], axis=0), "gy", 0)
        x_faces = [swap(face, "gx", first) for first, face in enumerate(faces[4:])]
        pieces = jnp.concatenate([blocks, ya_in[1:]], axis=0)
        pieces, yb, x_faces = barrier((pieces, yb, x_faces))
        yb_in = from_distance(jnp.concatenate([yb, pieces], axis=0), "gy", 3)
        pieces = jnp.concatenate([pieces, yb_in[1:]], axis=0).reshape(size_y, count, count_z, 128)
        halos = [za_in, zb_in, ya_in, yb_in] + x_faces

    distance = 2
    while distance < size_z:
        pieces = pieces + from_distance(pieces, "gz", distance)
        distance *= 2
    pieces, q = barrier((pieces, q))
    mine = lax.dynamic_slice_in_dim(pieces, lax.axis_index("gz") * part, part, axis=3)[None]
    mine = gather_relative(mine, "gx")
    mine = mine.reshape(size_x * size_y, row_blocks, 2, count_z, part).transpose(0, 2, 1, 3, 4)
    mine = mine.reshape(size_x * size_y, 2, row_blocks * count_z, part)
    holder = (lax.axis_index("gx") * size_y + lax.axis_index("gy") + 1).astype(jnp.float32)
    returned = 0.0
    for j in range(capacity):
        row = (j // 2) * (3 * steps + 1)
        values = mine[:, j % 2, row : row + 3 * steps]
        match = mine[:, j % 2, row + 3 * steps :][:, :1] == holder
        returned = returned + jnp.sum(jnp.where(match, values, 0.0), axis=0)
    return q, returned.reshape(positions.shape)


def solution(mesh):
    in_specs = (
        P(None, "gx", "gz", "gy"),
        P(None, None, ("gx", "gy"), "gz"),
        P(None, None, ("gx", "gy"), "gz"),
        P("gx", "gy", "gz", None),
    )
    out_specs = (P(None, "gx", "gz", "gy"), P(None, None, ("gx", "gy"), "gz"))
    return jax.shard_map(shards, mesh=mesh, in_specs=in_specs, out_specs=out_specs, check_vma=False)
```

```python
import functools
import math

import jax
import jax.numpy as jnp
from jax import lax
from jax.experimental import pallas as pl
from jax.experimental.pallas import tpu as pltpu
from jax.sharding import PartitionSpec as P

kernel_width = 2.0
kernel_norm = 1.0 / (math.pi**1.5 * kernel_width**3)
time_step = 0.1
smag_coef = 0.17
viscosity = 0.02
diffusivity = 0.02
prandtl = 0.4
vmem_limit = 48 << 20


def swap_pairs(count, first):
    pairs = []
    for low in range(first, count - 1, 2):
        pairs += [(low, low + 1), (low + 1, low)]
    return pairs


def swap(value, axis, first):
    pairs = swap_pairs(lax.axis_size(axis), first)
    if not pairs:
        return jnp.zeros_like(value)
    return lax.ppermute(value, axis, pairs)


def from_distance(value, axis, distance):
    count = lax.axis_size(axis)
    return lax.ppermute(value, axis, [(i, i ^ distance) for i in range(count)])


def gather_relative(value, axis):
    distance = 1
    while distance < lax.axis_size(axis):
        value = jnp.concatenate([value, from_distance(value, axis, distance)], axis=0)
        distance *= 2
    return value


def pick(flag, first, second):
    return jnp.where(flag, first, second)


def is_even(axis):
    return lax.rem(lax.axis_index(axis), 2) == 0


def write_faces(q_ref, face_refs, shape):
    count_x, count_z, count_y = shape
    za_ref, zb_ref, ya_ref, yb_ref, xa_ref = face_refs[:5]
    even_x, even_z, even_y = is_even("gx"), is_even("gz"), is_even("gy")
    low, high = q_ref[:, 0], q_ref[:, count_x - 1]
    xa_ref[...] = pick(even_x, high, low)
    for xb_ref in face_refs[5:]:
        xb_ref[...] = pick(even_x, low, high)
    for comp in range(4):
        low = q_ref[comp, :, 0, :]
        high = q_ref[comp, :, count_z - 1, :]
        za_ref[comp] = pick(even_z, high, low)
        zb_ref[comp] = pick(even_z, low, high)
    lane = lax.broadcasted_iota(jnp.int32, (count_z, 128), 1)
    low = jnp.zeros((count_z, 128), jnp.float32)
    high = jnp.zeros((count_z, 128), jnp.float32)
    for comp in range(4):
        for x in range(count_x):
            place = comp * count_x + x
            first = q_ref[comp, x, :, :128]
            last = q_ref[comp, x, :, count_y - 128 :]
            low = jnp.where(lane == place, pltpu.roll(first, place, 1), low)
            high = jnp.where(lane == place, pltpu.roll(last, (place + 1) % 128, 1), high)
    ya_ref[...] = pick(even_y, high, low)
    yb_ref[...] = pick(even_y, low, high)


def faces_body(q_ref, *face_refs, shape):
    write_faces(q_ref, face_refs, shape)


def sorted_slots(list_ref, capacity):
    slots = [list_ref[j] for j in range(capacity)]
    for first in range(capacity):
        for second in range(first + 1, capacity):
            a, b = slots[first], slots[second]
            slots[first], slots[second] = jnp.minimum(a, b), jnp.maximum(a, b)
    return slots


def masks_of(shape):
    count_z = shape[1]
    sub = lax.broadcasted_iota(jnp.int32, (count_z, 128), 0)
    lane = lax.broadcasted_iota(jnp.int32, (count_z, 128), 1)
    return sub == 0, sub == count_z - 1, lane == 0, lane == 127


def tile_update(shifts, pushed):
    diffs, laplace, centre = [], [], []
    for c, minus_x, plus_x, minus_y, plus_y, minus_z, plus_z in shifts:
        diffs.append((plus_x - minus_x, plus_y - minus_y, plus_z - minus_z))
        laplace.append((plus_x + minus_x) + (plus_y + minus_y) + (plus_z + minus_z) - 6.0 * c)
        centre.append(c)
    diagonal = diffs[0][0] * diffs[0][0] + diffs[1][1] * diffs[1][1] + diffs[2][2] * diffs[2][2]
    xy = diffs[0][1] + diffs[1][0]
    xz = diffs[0][2] + diffs[2][0]
    yz = diffs[1][2] + diffs[2][1]
    total = (diagonal + diagonal) + (xy * xy + xz * xz + yz * yz)
    root = total * lax.rsqrt(jnp.maximum(total, 1.1754944e-38))
    scale_u = time_step * viscosity + (0.5 * time_step * smag_coef**2) * root
    scale_t = time_step * diffusivity + (0.5 * time_step * smag_coef**2 / prandtl) * root
    half = [0.5 * time_step * centre[a] for a in range(3)]
    out = []
    for comp in range(4):
        d = diffs[comp]
        moved = half[0] * d[0] + half[1] * d[1] + half[2] * d[2]
        value = centre[comp] - moved + (scale_u if comp < 3 else scale_t) * laplace[comp]
        out.append(value + pushed[comp] if comp < 3 else value)
    return out


def split(value):
    high = value.astype(jnp.bfloat16)
    low = (value - high.astype(jnp.float32)).astype(jnp.bfloat16)
    return high, low


def turbine_rows(rows_ref, table_ref, slots, step, points):
    size_x, size_y = lax.axis_size("gx"), lax.axis_size("gy")
    for j, slot in enumerate(slots):
        t = jnp.minimum(slot, size_x * size_y - 1)
        place_x = lax.bitwise_xor(lax.div(t, size_y), lax.axis_index("gx"))
        place_y = lax.bitwise_xor(lax.rem(t, size_y), lax.axis_index("gy"))
        entry = place_x * size_y + lax.bitwise_xor(place_y, lax.div(place_y, 2))
        rows_ref[:, j * points : (j + 1) * points] = table_ref[entry, 8 * step : 8 * step + 8, :]
    return rows_ref[...]


def point_factors(rows, shape):
    lanes = rows.shape[1]

    def factor(row, axis, count):
        start = (lax.axis_index(axis) * count).astype(jnp.float32)
        cells = lax.broadcasted_iota(jnp.int32, (count, lanes), 0).astype(jnp.float32) + start
        gap = cells - row
        return jnp.exp(-(gap * gap) / kernel_width**2)

    count_x, count_z, count_y = shape
    factor_x = factor(rows[0:1], "gx", count_x)
    factor_y = factor(rows[1:2], "gy", count_y)
    factor_z = factor(rows[2:3], "gz", count_z) * kernel_norm
    weights = (factor_x[:, None, :] * factor_z[None, :, :]).reshape(count_x * count_z, lanes)
    return weights, split(factor_y)


def push(force_ref, rows, weights, factor_y, shape):
    high, low = factor_y
    right = jnp.concatenate([high, high, low], axis=1)
    for comp in range(3):
        first, second = split(weights * (rows[3 + comp : 4 + comp] * time_step))
        left = jnp.concatenate([first, second, first], axis=1)
        pushed = lax.dot_general(left, right, (((1,), (1,)), ((), ())), preferred_element_type=jnp.float32)
        force_ref[comp] = pushed.reshape(shape)


def sample(q_ref, weights, factor_y, shape):
    count_x, count_z, count_y = shape
    high, low = factor_y
    right = jnp.concatenate([high, high, low], axis=0)
    sums = []
    for comp in range(3):
        first, second = split(q_ref[comp].reshape(count_x * count_z, count_y))
        left = jnp.concatenate([first, second, first], axis=1)
        along = jnp.dot(left, right, preferred_element_type=jnp.float32)
        sums.append(jnp.sum(along * weights, axis=0, keepdims=True))
    return sums


def push_body(list_ref, table_ref, force_ref, rows_ref, *, shape, points, capacity, step):
    slots = sorted_slots(list_ref, capacity)
    listed = slots[0] < lax.axis_size("gx") * lax.axis_size("gy")

    @pl.when(listed)
    def _():
        rows = turbine_rows(rows_ref, table_ref, slots, step, points)
        push(force_ref, rows, *point_factors(rows, shape), shape)

    @pl.when(jnp.logical_not(listed))
    def _():
        force_ref[...] = jnp.zeros(force_ref.shape, jnp.float32)


def sample_body(list_ref, table_ref, q_ref, sample_ref, rows_ref, *, shape, points, capacity, step):
    slots = sorted_slots(list_ref, capacity)
    listed = slots[0] < lax.axis_size("gx") * lax.axis_size("gy")
    sample_ref[...] = jnp.zeros(sample_ref.shape, jnp.float32)

    @pl.when(listed)
    def _():
        rows = turbine_rows(rows_ref, table_ref, slots, step, points)
        for comp, value in enumerate(sample(q_ref, *point_factors(rows, shape), shape)):
            sample_ref[comp : comp + 1] = value


def step_body(*refs, shape, points, capacity, step, steps):
    count_x, count_z, count_y = shape
    last, packs = step == steps - 1, step == steps - 2
    faces = len(face_shapes(shape))
    refs = list(refs)
    list_ref, table_ref, force_ref, q_ref = refs[:4]
    za_ref, zb_ref, ya_ref, yb_ref = refs[4:8]
    x_refs, refs = refs[8 : 4 + faces], refs[4 + faces :]
    if packs:
        past_refs, refs = refs[: steps - 1], refs[steps - 1 :]
    out_ref = refs.pop(0)
    if last:
        far_ref, out_ref, sems = out_ref, refs.pop(0), refs.pop(0)
    else:
        face_refs, refs = refs[:faces], refs[faces:]
    if packs:
        pack_ref, rows_ref, sample_ref = refs.pop(0), refs.pop(0), refs.pop(0)
    low_z_ref, high_z_ref, low_y_ref, high_y_ref, low_x_ref, high_x_ref = refs

    even_x, even_z, even_y = is_even("gx"), is_even("gz"), is_even("gy")
    index_y = lax.axis_index("gy")
    tiles = count_y // 128
    for tile in range(tiles):
        first, second = (ref[:, :, tile * 128 : tile * 128 + 128] for ref in (za_ref, zb_ref))
        low_z_ref[:, tile] = pick(even_z, second, first)
        high_z_ref[:, tile] = pick(even_z, first, second)
    low_y_ref[...] = pick(index_y == 0, 0.0, pick(even_y, yb_ref[:count_z], ya_ref[:count_z]))
    high_y_ref[...] = pick(index_y == lax.axis_size("gy") - 1, 0.0, pick(even_y, ya_ref[:count_z], yb_ref[:count_z]))
    first = x_refs[0][...]
    second = x_refs[1][...] if len(x_refs) > 1 else 0.0
    low_x_ref[...] = pick(even_x, second, first)
    high_x_ref[...] = pick(even_x, first, second)
    first_z, last_z, first_y, last_y = masks_of(shape)

    def plane(x, minus, plus):
        centre, up, down = [], [], []
        for comp in range(4):
            row = [q_ref[comp, x, :, tile * 128 : tile * 128 + 128] for tile in range(tiles)]
            place = comp * count_x + x
            turn = (128 - place) % 128 if isinstance(place, int) else 128 - place
            centre.append(row)
            up.append([pltpu.roll(low_y_ref[...], turn, 1)] + [pltpu.roll(c, 1, 1) for c in row])
            down.append([pltpu.roll(c, 127, 1) for c in row] + [pltpu.roll(high_y_ref[...], 127 - place, 1)])
        for tile in range(tiles):
            here = slice(tile * 128, tile * 128 + 128)
            shifts = []
            for comp in range(4):
                c = centre[comp][tile]
                minus_y = jnp.where(first_y, up[comp][tile], up[comp][tile + 1])
                plus_y = jnp.where(last_y, down[comp][tile + 1], down[comp][tile])
                low_z = low_z_ref[comp, tile, pl.ds(x, 1), :]
                high_z = high_z_ref[comp, tile, pl.ds(x, 1), :]
                minus_z = jnp.where(first_z, low_z, pltpu.roll(c, 1, 0))
                plus_z = jnp.where(last_z, high_z, pltpu.roll(c, count_z - 1, 0))
                shifts.append((c, minus(comp, here), plus(comp, here), minus_y, plus_y, minus_z, plus_z))
            pushed = [force_ref[comp, x, :, here] for comp in range(3)]
            for comp, value in enumerate(tile_update(shifts, pushed)):
                out_ref[comp, x, :, here] = value

    def of_plane(x):
        return lambda comp, here: q_ref[comp, x, :, here]

    def copy_out(number, start, count):
        here = pl.ds(start, count)
        return pltpu.make_async_copy(out_ref.at[:, here], far_ref.at[:, here], sems.at[number])

    inner = count_x - 2
    group = max(g for g in range(1, 11) if inner % g == 0)

    def middle(trip, carry):
        for k in range(group):
            x = 1 + trip * group + k
            plane(x, of_plane(x - 1), of_plane(x + 1))
        if last:
            copy_out(trip, 1 + trip * group, group).start()
        return carry

    lax.fori_loop(0, inner // group, middle, 0)
    plane(0, lambda comp, here: low_x_ref[comp, :, here], of_plane(1))
    plane(count_x - 1, of_plane(count_x - 2), lambda comp, here: high_x_ref[comp, :, here])

    if last:
        edges = [copy_out(inner // group, 0, 1), copy_out(inner // group + 1, count_x - 1, 1)]
        for edge in edges:
            edge.start()
        for trip in range(inner // group):
            copy_out(trip, 1 + trip * group, group).wait()
        for edge in edges:
            edge.wait()
        return

    write_faces(out_ref, face_refs, shape)
    if not packs:
        return

    slots = sorted_slots(list_ref, capacity)
    listed = slots[0] < lax.axis_size("gx") * lax.axis_size("gy")
    sample_body(
        list_ref, table_ref, out_ref, sample_ref, rows_ref, shape=shape, points=points, capacity=capacity, step=step + 1
    )
    pack_ref[...] = jnp.zeros(pack_ref.shape, jnp.float32)
    for j, slot in enumerate(slots):
        here, row = slice(j * points, (j + 1) * points), j * (3 * steps + 1)
        for number, ref in enumerate(list(past_refs) + [sample_ref]):
            pack_ref[row + 3 * number : row + 3 * number + 3] = ref[:3, here]
        name = jnp.where(listed, 0.5 * (slot + 1).astype(jnp.float32), 0.0)
        pack_ref[row + 3 * steps : row + 3 * steps + 1] = jnp.full((1, points), name)


def face_shapes(shape):
    count_x, count_z, count_y = shape
    forms = [(4, count_x, count_y)] * 2
    forms += [(count_z, 128)] * 2 + [(4, count_z, count_y)] * (1 if lax.axis_size("gx") == 2 else 2)
    return [jax.ShapeDtypeStruct(form, jnp.float32) for form in forms]


def vmem_specs(count):
    return [pl.BlockSpec(memory_space=pltpu.VMEM)] * count


def swap_faces(faces):
    plan = [("gz", 0), ("gz", 1), ("gy", 0), ("gy", 1), ("gx", 0), ("gx", 1)]
    return [swap(face, axis, first) for face, (axis, first) in zip(faces, plan)]


def true_order(pieces, axis):
    distance = 1
    while distance < pieces.shape[0]:
        swapped = pieces.reshape((-1, 2, distance) + pieces.shape[1:])[:, ::-1].reshape(pieces.shape)
        odd = lax.rem(lax.div(lax.axis_index(axis), distance), 2) == 1
        pieces = jnp.where(odd, swapped, pieces)
        distance *= 2
    return pieces


def shards(flow, positions, loads, block_list):
    capacity = block_list.shape[-1]
    steps, _, _, part = positions.shape
    shape = flow.shape[1:]
    count_x, count_z, count_y = shape
    size_x, size_y, size_z = lax.axis_size("gx"), lax.axis_size("gy"), lax.axis_size("gz")
    points = part * size_z
    lanes = capacity * points
    params = pltpu.CompilerParams(vmem_limit_bytes=vmem_limit)
    q = flow
    turbines = block_list.reshape(capacity)
    barrier = lax.optimization_barrier
    forms = face_shapes(shape)

    own = jnp.concatenate([positions.reshape(steps, 3, part), loads.reshape(steps, 3, part)], axis=1)
    rows = 8 * steps
    table = jnp.pad(own, ((0, 0), (0, 2), (0, 0))).reshape(1, rows, part)
    table = jnp.concatenate([table, from_distance(table, "gz", 1)], axis=0)
    faces = pl.pallas_call(
        functools.partial(faces_body, shape=shape),
        out_shape=forms,
        in_specs=vmem_specs(1),
        out_specs=vmem_specs(len(forms)),
        compiler_params=params,
        name="faces",
    )(q)
    table, faces = barrier((table, list(faces)))
    za, zb, ya, yb = faces[:4]
    za, zb = swap(za, "gz", 0), swap(zb, "gz", 1)
    distance = 2
    while distance < size_z:
        table = jnp.concatenate([table, from_distance(table, "gz", distance)], axis=0)
        distance *= 2
    table = true_order(table, "gz")
    table = jnp.concatenate([table[k] for k in range(size_z)], axis=1)
    table, ya, za, zb = barrier((table, ya, za, zb))
    ya = swap(jnp.concatenate([ya, table], axis=0), "gy", 0)
    x_faces = [swap(face, "gx", first) for first, face in enumerate(faces[4:])]
    table = jnp.concatenate([table, ya[count_z:]], axis=0)
    table, yb, x_faces = barrier((table, yb, x_faces))
    yb = from_distance(jnp.concatenate([yb, table], axis=0), "gy", 3)
    table = jnp.concatenate([table, yb[count_z:]], axis=0)
    table = gather_relative(table[None], "gx").reshape(size_x * size_y, rows, points)
    halos = [za, zb, ya, yb] + x_faces

    smem = pl.BlockSpec(memory_space=pltpu.SMEM)
    row_scratch = pltpu.VMEM((8, lanes), jnp.float32)
    count = 3 * steps + 1
    pack_rows = pl.cdiv(capacity * count, 8) * 8
    forces = [
        pl.pallas_call(
            functools.partial(push_body, shape=shape, points=points, capacity=capacity, step=step),
            out_shape=jax.ShapeDtypeStruct((3,) + shape, jnp.float32),
            in_specs=[smem] + vmem_specs(1),
            out_specs=vmem_specs(1)[0],
            scratch_shapes=[row_scratch],
            compiler_params=params,
            name="push",
        )(turbines, table)
        for step in range(steps)
    ]
    past = []
    for step in range(steps):
        last, packs = step == steps - 1, step == steps - 2
        fixed = dict(shape=shape, points=points, capacity=capacity, step=step)
        if not last:
            past.append(
                pl.pallas_call(
                    functools.partial(sample_body, **fixed),
                    out_shape=jax.ShapeDtypeStruct((8, lanes), jnp.float32),
                    in_specs=[smem] + vmem_specs(2),
                    out_specs=vmem_specs(1)[0],
                    scratch_shapes=[row_scratch],
                    compiler_params=params,
                    name="sample",
                )(turbines, table, q)
            )
        shapes = [jax.ShapeDtypeStruct(q.shape, jnp.float32)]
        scratch = []
        if last:
            out_specs = [pl.BlockSpec(memory_space=pl.ANY)]
            scratch = [pltpu.VMEM(q.shape, jnp.float32), pltpu.SemaphoreType.DMA((count_x,))]
        else:
            shapes += forms
            if packs:
                shapes += [jax.ShapeDtypeStruct((pack_rows, points), jnp.float32)]
                scratch = [row_scratch, row_scratch]
            out_specs = vmem_specs(len(shapes))
        inputs = [turbines, table, forces[step], q] + halos + (past if packs else [])
        results = pl.pallas_call(
            functools.partial(step_body, steps=steps, **fixed),
            out_shape=shapes,
            in_specs=[smem] + vmem_specs(len(inputs) - 1),
            out_specs=out_specs,
            scratch_shapes=scratch
            + [pltpu.VMEM((4, count_y // 128, count_x, 128), jnp.float32)] * 2
            + [pltpu.VMEM((count_z, 128), jnp.float32)] * 2
            + [pltpu.VMEM((4, count_z, count_y), jnp.float32)] * 2,
            compiler_params=params,
            name="step",
        )(*inputs)
        q = results[0]
        if last:
            break
        faces = results[1 : 1 + len(forms)]
        if not packs:
            halos = swap_faces(faces)
            continue
        za, zb, ya, yb = faces[:4]
        pieces = results[-1]
        za, zb = swap(za, "gz", 0), swap(zb, "gz", 1)
        ya = swap(jnp.concatenate([ya, pieces], axis=0), "gy", 0)
        x_faces = [swap(face, "gx", first) for first, face in enumerate(faces[4:])]
        pieces = jnp.concatenate([pieces, ya[count_z:]], axis=0)
        pieces, yb, za, zb, x_faces = barrier((pieces, yb, za, zb, x_faces))
        yb = from_distance(jnp.concatenate([yb, pieces], axis=0), "gy", 3)
        pieces = jnp.concatenate([pieces, yb[count_z:]], axis=0)
        halos = [za, zb, ya, yb] + x_faces
        pieces, forces[-1] = barrier((pieces, forces[-1]))
        distance = 1
        while distance < size_z:
            pieces = pieces + from_distance(pieces, "gz", distance)
            distance *= 2

    pieces, q = barrier((pieces, q))
    mine = lax.dynamic_slice_in_dim(pieces, lax.axis_index("gz") * part, part, axis=1)[None]
    mine = gather_relative(mine, "gx").reshape(size_x * size_y, pack_rows, part)
    holder = (lax.axis_index("gx") * size_y + lax.axis_index("gy") + 1).astype(jnp.float32)
    returned = 0.0
    for j in range(capacity):
        values = mine[:, j * count : j * count + 3 * steps]
        match = mine[:, (j + 1) * count - 1 : (j + 1) * count, :1] == holder
        returned = returned + jnp.sum(jnp.where(match, values, 0.0), axis=0)
    return q, returned.reshape(positions.shape)


def solution(mesh):
    in_specs = (
        P(None, "gx", "gz", "gy"),
        P(None, None, ("gx", "gy"), "gz"),
        P(None, None, ("gx", "gy"), "gz"),
        P("gx", "gy", "gz", None),
    )
    out_specs = (P(None, "gx", "gz", "gy"), P(None, None, ("gx", "gy"), "gz"))
    return jax.shard_map(shards, mesh=mesh, in_specs=in_specs, out_specs=out_specs, check_vma=False)
```

```python
import functools
import math

import jax
import jax.numpy as jnp
from jax import lax
from jax.experimental import pallas as pl
from jax.experimental.pallas import tpu as pltpu
from jax.sharding import PartitionSpec as P

kernel_width = 2.0
kernel_norm = 1.0 / (math.pi**1.5 * kernel_width**3)
time_step = 0.1
smag_coef = 0.17
viscosity = 0.02
diffusivity = 0.02
prandtl = 0.4
vmem_limit = 24 << 20


def swap_pairs(count, first):
    pairs = []
    for low in range(first, count - 1, 2):
        pairs += [(low, low + 1), (low + 1, low)]
    return pairs


def swap(value, axis, first):
    pairs = swap_pairs(lax.axis_size(axis), first)
    if not pairs:
        return jnp.zeros_like(value)
    return lax.ppermute(value, axis, pairs)


def from_distance(value, axis, distance):
    count = lax.axis_size(axis)
    return lax.ppermute(value, axis, [(i, i ^ distance) for i in range(count)])


def gather_relative(value, axis):
    distance = 1
    while distance < lax.axis_size(axis):
        value = jnp.concatenate([value, from_distance(value, axis, distance)], axis=0)
        distance *= 2
    return value


def pick(flag, first, second):
    return jnp.where(flag, first, second)


def is_even(axis):
    return lax.rem(lax.axis_index(axis), 2) == 0


def write_faces(q_ref, face_refs, shape):
    count_x, count_z, count_y = shape
    za_ref, zb_ref, ya_ref, yb_ref, xa_ref = face_refs[:5]
    even_x, even_z, even_y = is_even("gx"), is_even("gz"), is_even("gy")
    low, high = q_ref[:, 0], q_ref[:, count_x - 1]
    xa_ref[...] = pick(even_x, high, low)
    for xb_ref in face_refs[5:]:
        xb_ref[...] = pick(even_x, low, high)
    for comp in range(4):
        low = q_ref[comp, :, 0, :]
        high = q_ref[comp, :, count_z - 1, :]
        za_ref[comp * count_x : (comp + 1) * count_x] = pick(even_z, high, low)
        zb_ref[comp * count_x : (comp + 1) * count_x] = pick(even_z, low, high)
    lane = lax.broadcasted_iota(jnp.int32, (count_z, 128), 1)
    low = jnp.zeros((count_z, 128), jnp.float32)
    high = jnp.zeros((count_z, 128), jnp.float32)
    for comp in range(4):
        for x in range(count_x):
            place = comp * count_x + x
            first = q_ref[comp, x, :, :128]
            last = q_ref[comp, x, :, count_y - 128 :]
            low = jnp.where(lane == place, pltpu.roll(first, place, 1), low)
            high = jnp.where(lane == place, pltpu.roll(last, (place + 1) % 128, 1), high)
    ya_ref[...] = pick(even_y, high, low)
    yb_ref[...] = pick(even_y, low, high)


def faces_body(q_ref, *face_refs, shape):
    write_faces(q_ref, face_refs, shape)


def sorted_slots(list_ref, capacity):
    slots = [list_ref[j] for j in range(capacity)]
    for first in range(capacity):
        for second in range(first + 1, capacity):
            a, b = slots[first], slots[second]
            slots[first], slots[second] = jnp.minimum(a, b), jnp.maximum(a, b)
    return slots


def masks_of(shape):
    count_z = shape[1]
    sub = lax.broadcasted_iota(jnp.int32, (count_z, 128), 0)
    lane = lax.broadcasted_iota(jnp.int32, (count_z, 128), 1)
    return sub == 0, sub == count_z - 1, lane == 0, lane == 127


def tile_update(shifts, pushed):
    diffs, laplace, centre = [], [], []
    for c, minus_x, plus_x, minus_y, plus_y, minus_z, plus_z in shifts:
        diffs.append((plus_x - minus_x, plus_y - minus_y, plus_z - minus_z))
        laplace.append((plus_x + minus_x) + (plus_y + minus_y) + (plus_z + minus_z) - 6.0 * c)
        centre.append(c)
    diagonal = diffs[0][0] * diffs[0][0] + diffs[1][1] * diffs[1][1] + diffs[2][2] * diffs[2][2]
    xy = diffs[0][1] + diffs[1][0]
    xz = diffs[0][2] + diffs[2][0]
    yz = diffs[1][2] + diffs[2][1]
    total = (diagonal + diagonal) + (xy * xy + xz * xz + yz * yz)
    root = total * lax.rsqrt(jnp.maximum(total, 1.1754944e-38))
    scale_u = time_step * viscosity + (0.5 * time_step * smag_coef**2) * root
    scale_t = time_step * diffusivity + (0.5 * time_step * smag_coef**2 / prandtl) * root
    half = [0.5 * time_step * centre[a] for a in range(3)]
    out = []
    for comp in range(4):
        d = diffs[comp]
        moved = half[0] * d[0] + half[1] * d[1] + half[2] * d[2]
        value = centre[comp] - moved + (scale_u if comp < 3 else scale_t) * laplace[comp]
        out.append(value + pushed[comp] if comp < 3 else value)
    return out


def split(value):
    high = value.astype(jnp.bfloat16)
    low = (value - high.astype(jnp.float32)).astype(jnp.bfloat16)
    return high, low


def turbine_rows(rows_ref, table_ref, slots, step, points):
    size_x, size_y = lax.axis_size("gx"), lax.axis_size("gy")
    for j, slot in enumerate(slots):
        t = jnp.minimum(slot, size_x * size_y - 1)
        place_x = lax.bitwise_xor(lax.div(t, size_y), lax.axis_index("gx"))
        place_y = lax.bitwise_xor(lax.rem(t, size_y), lax.axis_index("gy"))
        entry = place_x * size_y + lax.bitwise_xor(place_y, lax.div(place_y, 2))
        rows_ref[:, j * points : (j + 1) * points] = table_ref[entry, 8 * step : 8 * step + 8, :]
    return rows_ref[...]


def point_factors(rows, shape):
    lanes = rows.shape[1]

    def factor(row, axis, count):
        start = (lax.axis_index(axis) * count).astype(jnp.float32)
        cells = lax.broadcasted_iota(jnp.int32, (count, lanes), 0).astype(jnp.float32) + start
        gap = cells - row
        return jnp.exp(-(gap * gap) / kernel_width**2)

    count_x, count_z, count_y = shape
    factor_x = factor(rows[0:1], "gx", count_x)
    factor_y = factor(rows[1:2], "gy", count_y)
    factor_z = factor(rows[2:3], "gz", count_z) * kernel_norm
    weights = (factor_x[:, None, :] * factor_z[None, :, :]).reshape(count_x * count_z, lanes)
    return weights, split(factor_y)


def push(force_ref, rows, weights, factor_y, shape):
    high, low = factor_y
    right = jnp.concatenate([high, high, low], axis=1)
    for comp in range(3):
        first, second = split(weights * (rows[3 + comp : 4 + comp] * time_step))
        left = jnp.concatenate([first, second, first], axis=1)
        pushed = lax.dot_general(left, right, (((1,), (1,)), ((), ())), preferred_element_type=jnp.float32)
        force_ref[comp] = pushed.reshape(shape)


def sample(q_ref, weights, factor_y, shape):
    count_x, count_z, count_y = shape
    high, low = factor_y
    right = jnp.concatenate([high, high, low], axis=0)
    sums = []
    for comp in range(3):
        first, second = split(q_ref[comp].reshape(count_x * count_z, count_y))
        left = jnp.concatenate([first, second, first], axis=1)
        along = jnp.dot(left, right, preferred_element_type=jnp.float32)
        sums.append(jnp.sum(along * weights, axis=0, keepdims=True))
    return sums


def step_body(*refs, shape, points, capacity, step, steps):
    count_x, count_z, count_y = shape
    last, packs = step == steps - 1, step == steps - 2
    faces = len(face_shapes(shape))
    refs = list(refs)
    list_ref, table_ref, q_ref = refs[:3]
    za_ref, zb_ref, ya_ref, yb_ref = refs[3:7]
    x_refs, refs = refs[7 : 3 + faces], refs[3 + faces :]
    past_ref = None if step == 0 or last else refs.pop(0)
    out_ref = refs.pop(0)
    sample_ref = None
    if not last:
        face_refs, refs = refs[:faces], refs[faces:]
        sample_ref = refs.pop(0)
    else:
        far_ref, out_ref, sems = out_ref, refs.pop(0), refs.pop(0)
    force_ref, rows_ref, low_z_ref, high_z_ref, low_y_ref, high_y_ref, low_x_ref, high_x_ref = refs
    slots = sorted_slots(list_ref, capacity)
    turbines = lax.axis_size("gx") * lax.axis_size("gy")
    listed = slots[0] < turbines

    if not last:
        sample_ref[...] = jnp.zeros(sample_ref.shape, jnp.float32)
        if past_ref is not None:
            sample_ref[: 3 * step + 3] = past_ref[: 3 * step + 3]

    @pl.when(listed)
    def _():
        rows = turbine_rows(rows_ref, table_ref, slots, step, points)
        weights, factor_y = point_factors(rows, shape)
        push(force_ref, rows, weights, factor_y, shape)
        if step == 0:
            for comp, value in enumerate(sample(q_ref, weights, factor_y, shape)):
                sample_ref[comp : comp + 1] = value

    @pl.when(jnp.logical_not(listed))
    def _():
        force_ref[...] = jnp.zeros(force_ref.shape, jnp.float32)

    even_x, even_z, even_y = is_even("gx"), is_even("gz"), is_even("gy")
    index_y = lax.axis_index("gy")
    tiles = count_y // 128
    for comp in range(4):
        for tile in range(tiles):
            there = slice(comp * count_x, (comp + 1) * count_x), slice(tile * 128, tile * 128 + 128)
            first, second = za_ref[there], zb_ref[there]
            low_z_ref[comp, tile] = pick(even_z, second, first)
            high_z_ref[comp, tile] = pick(even_z, first, second)
    low_y_ref[...] = pick(index_y == 0, 0.0, pick(even_y, yb_ref[:count_z], ya_ref[:count_z]))
    high_y_ref[...] = pick(index_y == lax.axis_size("gy") - 1, 0.0, pick(even_y, ya_ref[:count_z], yb_ref[:count_z]))
    first = x_refs[0][...]
    second = x_refs[1][...] if len(x_refs) > 1 else 0.0
    low_x_ref[...] = pick(even_x, second, first)
    high_x_ref[...] = pick(even_x, first, second)
    first_z, last_z, first_y, last_y = masks_of(shape)

    def plane(x, minus, plus):
        centre, up, down = [], [], []
        for comp in range(4):
            row = [q_ref[comp, x, :, tile * 128 : tile * 128 + 128] for tile in range(tiles)]
            place = comp * count_x + x
            turn = (128 - place) % 128 if isinstance(place, int) else 128 - place
            centre.append(row)
            up.append([pltpu.roll(low_y_ref[...], turn, 1)] + [pltpu.roll(c, 1, 1) for c in row])
            down.append([pltpu.roll(c, 127, 1) for c in row] + [pltpu.roll(high_y_ref[...], 127 - place, 1)])
        for tile in range(tiles):
            here = slice(tile * 128, tile * 128 + 128)
            shifts = []
            for comp in range(4):
                c = centre[comp][tile]
                minus_y = jnp.where(first_y, up[comp][tile], up[comp][tile + 1])
                plus_y = jnp.where(last_y, down[comp][tile + 1], down[comp][tile])
                low_z = low_z_ref[comp, tile, pl.ds(x, 1), :]
                high_z = high_z_ref[comp, tile, pl.ds(x, 1), :]
                minus_z = jnp.where(first_z, low_z, pltpu.roll(c, 1, 0))
                plus_z = jnp.where(last_z, high_z, pltpu.roll(c, count_z - 1, 0))
                shifts.append((c, minus(comp, here), plus(comp, here), minus_y, plus_y, minus_z, plus_z))
            pushed = [force_ref[comp, x, :, here] for comp in range(3)]
            for comp, value in enumerate(tile_update(shifts, pushed)):
                out_ref[comp, x, :, here] = value

    def of_plane(x):
        return lambda comp, here: q_ref[comp, x, :, here]

    def copy_out(number, start, count):
        here = pl.ds(start, count)
        return pltpu.make_async_copy(out_ref.at[:, here], far_ref.at[:, here], sems.at[number])

    inner = count_x - 2
    group = max(g for g in range(1, 11) if inner % g == 0)

    def middle(trip, carry):
        for k in range(group):
            x = 1 + trip * group + k
            plane(x, of_plane(x - 1), of_plane(x + 1))
        if last:
            copy_out(trip, 1 + trip * group, group).start()
        return carry

    lax.fori_loop(0, inner // group, middle, 0)
    plane(0, lambda comp, here: low_x_ref[comp, :, here], of_plane(1))
    plane(count_x - 1, of_plane(count_x - 2), lambda comp, here: high_x_ref[comp, :, here])

    if last:
        edges = [copy_out(inner // group, 0, 1), copy_out(inner // group + 1, count_x - 1, 1)]
        for edge in edges:
            edge.start()
        for trip in range(inner // group):
            copy_out(trip, 1 + trip * group, group).wait()
        for edge in edges:
            edge.wait()
        return

    write_faces(out_ref, face_refs, shape)

    @pl.when(listed)
    def _():
        rows = turbine_rows(rows_ref, table_ref, slots, step + 1, points)
        weights, factor_y = point_factors(rows, shape)
        for comp, value in enumerate(sample(out_ref, weights, factor_y, shape)):
            sample_ref[3 * step + 3 + comp : 3 * step + 4 + comp] = value

    if packs:
        count = 3 * steps + 1
        za_ref = face_refs[0]
        start = 4 * count_x
        za_ref[start:] = jnp.zeros((za_ref.shape[0] - start, count_y), jnp.float32)
        for j, slot in enumerate(slots):
            lane, row = (j % 2) * points, start + (j // 2) * count
            values = sample_ref[: count - 1, j * points : (j + 1) * points]
            za_ref[row : row + count - 1, lane : lane + points] = values
            name = jnp.where(listed, 0.5 * (slot + 1).astype(jnp.float32), 0.0)
            za_ref[row + count - 1 : row + count, lane : lane + points] = jnp.full((1, points), name)


def face_shapes(shape, extra=0):
    count_x, count_z, count_y = shape
    forms = [(4 * count_x + extra, count_y), (4 * count_x, count_y)]
    forms += [(count_z, 128)] * 2 + [(4, count_z, count_y)] * (1 if lax.axis_size("gx") == 2 else 2)
    return [jax.ShapeDtypeStruct(form, jnp.float32) for form in forms]


def vmem_specs(count):
    return [pl.BlockSpec(memory_space=pltpu.VMEM)] * count


def swap_faces(faces):
    plan = [("gz", 0), ("gz", 1), ("gy", 0), ("gy", 1), ("gx", 0), ("gx", 1)]
    return [swap(face, axis, first) for face, (axis, first) in zip(faces, plan)]


def masked(halo, axis, first):
    index = lax.axis_index(axis)
    partner = index + 1 - 2 * lax.rem(index + first, 2)
    inside = jnp.logical_and(partner >= 0, partner < lax.axis_size(axis))
    return jnp.where(inside, halo, 0.0)


def true_order(pieces, axis):
    distance = 1
    while distance < pieces.shape[0]:
        swapped = pieces.reshape((-1, 2, distance) + pieces.shape[1:])[:, ::-1].reshape(pieces.shape)
        odd = lax.rem(lax.div(lax.axis_index(axis), distance), 2) == 1
        pieces = jnp.where(odd, swapped, pieces)
        distance *= 2
    return pieces


def shards(flow, positions, loads, block_list):
    capacity = block_list.shape[-1]
    steps, _, _, part = positions.shape
    shape = flow.shape[1:]
    count_x, count_z, count_y = shape
    size_x, size_y, size_z = lax.axis_size("gx"), lax.axis_size("gy"), lax.axis_size("gz")
    points = part * size_z
    lanes = capacity * points
    params = pltpu.CompilerParams(vmem_limit_bytes=vmem_limit)
    q = flow
    turbines = block_list.reshape(capacity)
    barrier = lax.optimization_barrier
    forms = face_shapes(shape)

    extra = pl.cdiv((3 * steps + 1) * pl.cdiv(capacity, 2), 8) * 8

    own = jnp.concatenate([positions.reshape(steps, 3, part), loads.reshape(steps, 3, part)], axis=1)
    table = jnp.pad(own, ((0, 0), (0, 2), (0, 0))).reshape(1, 8 * steps, part)
    table = jnp.concatenate([table, from_distance(table, "gz", 1)], axis=0)
    faces = pl.pallas_call(
        functools.partial(faces_body, shape=shape),
        out_shape=forms,
        in_specs=vmem_specs(1),
        out_specs=vmem_specs(len(forms)),
        compiler_params=params,
        name="faces",
    )(q)
    table, faces = barrier((table, list(faces)))
    za, zb, ya, yb = faces[:4]
    za = masked(swap(za, "gz", 0), "gz", 0)
    distance = 2
    while distance < size_z:
        received = from_distance(table, "gz", distance)
        received, za = barrier((received, za))
        table = jnp.concatenate([table, received], axis=0)
        distance *= 2
    table = true_order(table, "gz")
    table = jnp.concatenate([table[k] for k in range(size_z)], axis=1)
    rows = 8 * steps
    zb, ya, table = barrier((zb, ya, table))
    zb = masked(swap(zb, "gz", 1), "gz", 1)
    ya = swap(jnp.concatenate([ya, table], axis=0), "gy", 0)
    ya, zb = barrier((ya, zb))
    table = jnp.concatenate([table, ya[count_z:]], axis=0)
    yb = from_distance(jnp.concatenate([yb, table], axis=0), "gy", 3)
    x_faces = [swap(face, "gx", first) for first, face in enumerate(faces[4:])]
    table = jnp.concatenate([table, yb[count_z:]], axis=0)
    table = gather_relative(table[None], "gx").reshape(size_x * size_y, rows, points)
    halos = [za, zb, ya, yb] + x_faces

    samples = None
    for step in range(steps):
        last, packs = step == steps - 1, step == steps - 2
        shapes = [jax.ShapeDtypeStruct(q.shape, jnp.float32)]
        out_specs = vmem_specs(1)
        scratch = []
        if last:
            out_specs = [pl.BlockSpec(memory_space=pl.ANY)]
            scratch = [pltpu.VMEM(q.shape, jnp.float32), pltpu.SemaphoreType.DMA((count_x,))]
        else:
            shapes += face_shapes(shape, extra if packs else 0)
            if packs:
                scratch = [pltpu.VMEM((16, lanes), jnp.float32)]
            else:
                shapes += [jax.ShapeDtypeStruct((16, lanes), jnp.float32)]
            out_specs = vmem_specs(len(shapes))
        past = [] if step == 0 or last else [samples]
        results = pl.pallas_call(
            functools.partial(step_body, shape=shape, points=points, capacity=capacity, step=step, steps=steps),
            out_shape=shapes,
            in_specs=[pl.BlockSpec(memory_space=pltpu.SMEM)] + vmem_specs(2 + len(halos) + len(past)),
            out_specs=out_specs,
            scratch_shapes=scratch
            + [pltpu.VMEM((3,) + shape, jnp.float32), pltpu.VMEM((8, lanes), jnp.float32)]
            + [pltpu.VMEM((4, count_y // 128, count_x, 128), jnp.float32)] * 2
            + [pltpu.VMEM((count_z, 128), jnp.float32)] * 2
            + [pltpu.VMEM((4, count_z, count_y), jnp.float32)] * 2,
            compiler_params=params,
            name="step",
        )(turbines, table, q, *halos, *past)
        q = results[0]
        if last:
            break
        faces = results[1 : 1 + len(forms)]
        if not packs:
            samples = results[-1]
            halos = swap_faces(faces)
            continue
        za, zb, ya, yb = faces[:4]
        za_in = swap(za, "gz", 0)
        sums = za[4 * count_x :] + za_in[4 * count_x :]
        pieces = jnp.concatenate([sums[:, h * 128 : h * 128 + 128] for h in range(2)], axis=0)
        pieces, ya, zb = barrier((pieces, ya, zb))
        zb_in = masked(swap(zb, "gz", 1), "gz", 1)
        ya_in = swap(jnp.concatenate([ya, pieces], axis=0), "gy", 0)
        ya_in, zb_in, x_faces = barrier((ya_in, zb_in, faces[4:]))
        x_faces = [swap(face, "gx", first) for first, face in enumerate(x_faces)]
        pieces = jnp.concatenate([pieces, ya_in[count_z:]], axis=0)
        yb_in = from_distance(jnp.concatenate([yb, pieces], axis=0), "gy", 3)
        pieces = jnp.concatenate([pieces, yb_in[count_z:]], axis=0)
        pieces, x_faces = barrier((pieces, x_faces))
        halos = [za_in, zb_in, ya_in, yb_in] + x_faces

    distance = 2
    while distance < size_z:
        pieces = pieces + from_distance(pieces, "gz", distance)
        distance *= 2
    pieces, q = barrier((pieces, q))
    mine = lax.dynamic_slice_in_dim(pieces, lax.axis_index("gz") * part, part, axis=1)[None]
    mine = gather_relative(mine, "gx").reshape(size_x * size_y, 2, extra, part)
    holder = (lax.axis_index("gx") * size_y + lax.axis_index("gy") + 1).astype(jnp.float32)
    returned = 0.0
    for j in range(capacity):
        row = (j // 2) * (3 * steps + 1)
        values = mine[:, j % 2, row : row + 3 * steps]
        match = mine[:, j % 2, row + 3 * steps :][:, :1] == holder
        returned = returned + jnp.sum(jnp.where(match, values, 0.0), axis=0)
    return q, returned.reshape(positions.shape)


def solution(mesh):
    in_specs = (
        P(None, "gx", "gz", "gy"),
        P(None, None, ("gx", "gy"), "gz"),
        P(None, None, ("gx", "gy"), "gz"),
        P("gx", "gy", "gz", None),
    )
    out_specs = (P(None, "gx", "gz", "gy"), P(None, None, ("gx", "gy"), "gz"))
    return jax.shard_map(shards, mesh=mesh, in_specs=in_specs, out_specs=out_specs, check_vma=False)
```

```python
import functools
import math

import jax
import jax.numpy as jnp
from jax import lax
from jax.experimental import pallas as pl
from jax.experimental.pallas import tpu as pltpu
from jax.sharding import PartitionSpec as P

kernel_width = 2.0
kernel_norm = 1.0 / (math.pi**1.5 * kernel_width**3)
time_step = 0.1
smag_coef = 0.17
viscosity = 0.02
diffusivity = 0.02
prandtl = 0.4
vmem_limit = 24 << 20


def swap_pairs(count, first):
    pairs = []
    for low in range(first, count - 1, 2):
        pairs += [(low, low + 1), (low + 1, low)]
    return pairs


def swap(value, axis, first):
    pairs = swap_pairs(lax.axis_size(axis), first)
    if not pairs:
        return jnp.zeros_like(value)
    return lax.ppermute(value, axis, pairs)


def from_distance(value, axis, distance):
    count = lax.axis_size(axis)
    return lax.ppermute(value, axis, [(i, i ^ distance) for i in range(count)])


def gather_relative(value, axis):
    distance = 1
    while distance < lax.axis_size(axis):
        value = jnp.concatenate([value, from_distance(value, axis, distance)], axis=0)
        distance *= 2
    return value


def pick(flag, first, second):
    return jnp.where(flag, first, second)


def is_even(axis):
    return lax.rem(lax.axis_index(axis), 2) == 0


def write_faces(q_ref, face_refs, shape):
    count_x, count_z, count_y = shape
    za_ref, zb_ref, ya_ref, yb_ref, xa_ref = face_refs[:5]
    even_x, even_z, even_y = is_even("gx"), is_even("gz"), is_even("gy")
    low, high = q_ref[:, 0], q_ref[:, count_x - 1]
    xa_ref[...] = pick(even_x, high, low)
    for xb_ref in face_refs[5:]:
        xb_ref[...] = pick(even_x, low, high)
    for comp in range(4):
        low = q_ref[comp, :, 0, :]
        high = q_ref[comp, :, count_z - 1, :]
        za_ref[comp * count_x : (comp + 1) * count_x] = pick(even_z, high, low)
        zb_ref[comp * count_x : (comp + 1) * count_x] = pick(even_z, low, high)
    lane = lax.broadcasted_iota(jnp.int32, (count_z, 128), 1)
    low = jnp.zeros((count_z, 128), jnp.float32)
    high = jnp.zeros((count_z, 128), jnp.float32)
    for comp in range(4):
        for x in range(count_x):
            place = comp * count_x + x
            first = q_ref[comp, x, :, :128]
            last = q_ref[comp, x, :, count_y - 128 :]
            low = jnp.where(lane == place, pltpu.roll(first, place, 1), low)
            high = jnp.where(lane == place, pltpu.roll(last, (place + 1) % 128, 1), high)
    ya_ref[...] = pick(even_y, high, low)
    yb_ref[...] = pick(even_y, low, high)


def faces_body(q_ref, *face_refs, shape):
    write_faces(q_ref, face_refs, shape)


def sorted_slots(list_ref, capacity):
    slots = [list_ref[j] for j in range(capacity)]
    for first in range(capacity):
        for second in range(first + 1, capacity):
            a, b = slots[first], slots[second]
            slots[first], slots[second] = jnp.minimum(a, b), jnp.maximum(a, b)
    return slots


def masks_of(shape):
    count_z = shape[1]
    sub = lax.broadcasted_iota(jnp.int32, (count_z, 128), 0)
    lane = lax.broadcasted_iota(jnp.int32, (count_z, 128), 1)
    return sub == 0, sub == count_z - 1, lane == 0, lane == 127


def tile_update(shifts, pushed):
    diffs, laplace, centre = [], [], []
    for c, minus_x, plus_x, minus_y, plus_y, minus_z, plus_z in shifts:
        diffs.append((plus_x - minus_x, plus_y - minus_y, plus_z - minus_z))
        laplace.append((plus_x + minus_x) + (plus_y + minus_y) + (plus_z + minus_z) - 6.0 * c)
        centre.append(c)
    diagonal = diffs[0][0] * diffs[0][0] + diffs[1][1] * diffs[1][1] + diffs[2][2] * diffs[2][2]
    xy = diffs[0][1] + diffs[1][0]
    xz = diffs[0][2] + diffs[2][0]
    yz = diffs[1][2] + diffs[2][1]
    total = (diagonal + diagonal) + (xy * xy + xz * xz + yz * yz)
    root = total * lax.rsqrt(jnp.maximum(total, 1.1754944e-38))
    scale_u = time_step * viscosity + (0.5 * time_step * smag_coef**2) * root
    scale_t = time_step * diffusivity + (0.5 * time_step * smag_coef**2 / prandtl) * root
    half = [0.5 * time_step * centre[a] for a in range(3)]
    out = []
    for comp in range(4):
        d = diffs[comp]
        moved = half[0] * d[0] + half[1] * d[1] + half[2] * d[2]
        value = centre[comp] - moved + (scale_u if comp < 3 else scale_t) * laplace[comp]
        out.append(value + pushed[comp] if comp < 3 else value)
    return out


def split(value):
    high = value.astype(jnp.bfloat16)
    low = (value - high.astype(jnp.float32)).astype(jnp.bfloat16)
    return high, low


def turbine_rows(rows_ref, table_ref, slots, step, points):
    size_x, size_y = lax.axis_size("gx"), lax.axis_size("gy")
    for j, slot in enumerate(slots):
        t = jnp.minimum(slot, size_x * size_y - 1)
        place_x = lax.bitwise_xor(lax.div(t, size_y), lax.axis_index("gx"))
        place_y = lax.bitwise_xor(lax.rem(t, size_y), lax.axis_index("gy"))
        entry = place_x * size_y + lax.bitwise_xor(place_y, lax.div(place_y, 2))
        rows_ref[:, j * points : (j + 1) * points] = table_ref[entry, 8 * step : 8 * step + 8, :]
    return rows_ref[...]


def point_factors(rows, shape):
    lanes = rows.shape[1]

    def factor(row, axis, count):
        start = (lax.axis_index(axis) * count).astype(jnp.float32)
        cells = lax.broadcasted_iota(jnp.int32, (count, lanes), 0).astype(jnp.float32) + start
        gap = cells - row
        return jnp.exp(-(gap * gap) / kernel_width**2)

    count_x, count_z, count_y = shape
    factor_x = factor(rows[0:1], "gx", count_x)
    factor_y = factor(rows[1:2], "gy", count_y)
    factor_z = factor(rows[2:3], "gz", count_z) * kernel_norm
    weights = (factor_x[:, None, :] * factor_z[None, :, :]).reshape(count_x * count_z, lanes)
    return weights, split(factor_y)


def push(force_ref, rows, weights, factor_y, shape):
    high, low = factor_y
    right = jnp.concatenate([high, high, low], axis=1)
    for comp in range(3):
        first, second = split(weights * (rows[3 + comp : 4 + comp] * time_step))
        left = jnp.concatenate([first, second, first], axis=1)
        pushed = lax.dot_general(left, right, (((1,), (1,)), ((), ())), preferred_element_type=jnp.float32)
        force_ref[comp] = pushed.reshape(shape)


def sample(q_ref, weights, factor_y, shape):
    count_x, count_z, count_y = shape
    high, low = factor_y
    right = jnp.concatenate([high, high, low], axis=0)
    sums = []
    for comp in range(3):
        first, second = split(q_ref[comp].reshape(count_x * count_z, count_y))
        left = jnp.concatenate([first, second, first], axis=1)
        along = jnp.dot(left, right, preferred_element_type=jnp.float32)
        sums.append(jnp.sum(along * weights, axis=0, keepdims=True))
    return sums


def step_body(*refs, shape, points, capacity, step, steps):
    count_x, count_z, count_y = shape
    last, packs = step == steps - 1, step == steps - 2
    faces = len(face_shapes(shape))
    refs = list(refs)
    list_ref, table_ref, q_ref = refs[:3]
    za_ref, zb_ref, ya_ref, yb_ref = refs[3:7]
    x_refs, refs = refs[7 : 3 + faces], refs[3 + faces :]
    past_ref = None if step == 0 or last else refs.pop(0)
    out_ref = refs.pop(0)
    sample_ref = None
    if not last:
        face_refs, refs = refs[:faces], refs[faces:]
        sample_ref = refs.pop(0)
    else:
        far_ref, out_ref, sems = out_ref, refs.pop(0), refs.pop(0)
    force_ref, rows_ref, low_z_ref, high_z_ref, low_y_ref, high_y_ref, low_x_ref, high_x_ref = refs
    slots = sorted_slots(list_ref, capacity)
    turbines = lax.axis_size("gx") * lax.axis_size("gy")
    listed = slots[0] < turbines

    if not last:
        sample_ref[...] = jnp.zeros(sample_ref.shape, jnp.float32)
        if past_ref is not None:
            sample_ref[: 3 * step + 3] = past_ref[: 3 * step + 3]

    @pl.when(listed)
    def _():
        rows = turbine_rows(rows_ref, table_ref, slots, step, points)
        weights, factor_y = point_factors(rows, shape)
        push(force_ref, rows, weights, factor_y, shape)
        if step == 0:
            for comp, value in enumerate(sample(q_ref, weights, factor_y, shape)):
                sample_ref[comp : comp + 1] = value

    @pl.when(jnp.logical_not(listed))
    def _():
        force_ref[...] = jnp.zeros(force_ref.shape, jnp.float32)

    even_x, even_z, even_y = is_even("gx"), is_even("gz"), is_even("gy")
    index_y = lax.axis_index("gy")
    tiles = count_y // 128
    for comp in range(4):
        for tile in range(tiles):
            there = slice(comp * count_x, (comp + 1) * count_x), slice(tile * 128, tile * 128 + 128)
            first, second = za_ref[there], zb_ref[there]
            low_z_ref[comp, tile] = pick(even_z, second, first)
            high_z_ref[comp, tile] = pick(even_z, first, second)
    low_y_ref[...] = pick(index_y == 0, 0.0, pick(even_y, yb_ref[:count_z], ya_ref[:count_z]))
    high_y_ref[...] = pick(index_y == lax.axis_size("gy") - 1, 0.0, pick(even_y, ya_ref[:count_z], yb_ref[:count_z]))
    first = x_refs[0][...]
    second = x_refs[1][...] if len(x_refs) > 1 else 0.0
    low_x_ref[...] = pick(even_x, second, first)
    high_x_ref[...] = pick(even_x, first, second)
    first_z, last_z, first_y, last_y = masks_of(shape)

    def plane(x, minus, plus):
        centre, up, down = [], [], []
        for comp in range(4):
            row = [q_ref[comp, x, :, tile * 128 : tile * 128 + 128] for tile in range(tiles)]
            place = comp * count_x + x
            turn = (128 - place) % 128 if isinstance(place, int) else 128 - place
            centre.append(row)
            up.append([pltpu.roll(low_y_ref[...], turn, 1)] + [pltpu.roll(c, 1, 1) for c in row])
            down.append([pltpu.roll(c, 127, 1) for c in row] + [pltpu.roll(high_y_ref[...], 127 - place, 1)])
        for tile in range(tiles):
            here = slice(tile * 128, tile * 128 + 128)
            shifts = []
            for comp in range(4):
                c = centre[comp][tile]
                minus_y = jnp.where(first_y, up[comp][tile], up[comp][tile + 1])
                plus_y = jnp.where(last_y, down[comp][tile + 1], down[comp][tile])
                low_z = low_z_ref[comp, tile, pl.ds(x, 1), :]
                high_z = high_z_ref[comp, tile, pl.ds(x, 1), :]
                minus_z = jnp.where(first_z, low_z, pltpu.roll(c, 1, 0))
                plus_z = jnp.where(last_z, high_z, pltpu.roll(c, count_z - 1, 0))
                shifts.append((c, minus(comp, here), plus(comp, here), minus_y, plus_y, minus_z, plus_z))
            pushed = [force_ref[comp, x, :, here] for comp in range(3)]
            for comp, value in enumerate(tile_update(shifts, pushed)):
                out_ref[comp, x, :, here] = value

    def of_plane(x):
        return lambda comp, here: q_ref[comp, x, :, here]

    def copy_out(number, start, count):
        here = pl.ds(start, count)
        return pltpu.make_async_copy(out_ref.at[:, here], far_ref.at[:, here], sems.at[number])

    inner = count_x - 2
    group = max(g for g in range(1, 11) if inner % g == 0)

    def middle(trip, carry):
        for k in range(group):
            x = 1 + trip * group + k
            plane(x, of_plane(x - 1), of_plane(x + 1))
        if last:
            copy_out(trip, 1 + trip * group, group).start()
        return carry

    lax.fori_loop(0, inner // group, middle, 0)
    plane(0, lambda comp, here: low_x_ref[comp, :, here], of_plane(1))
    plane(count_x - 1, of_plane(count_x - 2), lambda comp, here: high_x_ref[comp, :, here])

    if last:
        edges = [copy_out(inner // group, 0, 1), copy_out(inner // group + 1, count_x - 1, 1)]
        for edge in edges:
            edge.start()
        for trip in range(inner // group):
            copy_out(trip, 1 + trip * group, group).wait()
        for edge in edges:
            edge.wait()
        return

    write_faces(out_ref, face_refs, shape)

    @pl.when(listed)
    def _():
        rows = turbine_rows(rows_ref, table_ref, slots, step + 1, points)
        weights, factor_y = point_factors(rows, shape)
        for comp, value in enumerate(sample(out_ref, weights, factor_y, shape)):
            sample_ref[3 * step + 3 + comp : 3 * step + 4 + comp] = value

    if packs:
        count = 3 * steps + 1
        za_ref = face_refs[0]
        start = 4 * count_x
        za_ref[start:] = jnp.zeros((za_ref.shape[0] - start, count_y), jnp.float32)
        for j, slot in enumerate(slots):
            lane, row = (j % 2) * points, start + (j // 2) * count
            values = sample_ref[: count - 1, j * points : (j + 1) * points]
            za_ref[row : row + count - 1, lane : lane + points] = values
            name = jnp.where(listed, 0.5 * (slot + 1).astype(jnp.float32), 0.0)
            za_ref[row + count - 1 : row + count, lane : lane + points] = jnp.full((1, points), name)


def face_shapes(shape, extra=0):
    count_x, count_z, count_y = shape
    forms = [(4 * count_x + extra, count_y), (4 * count_x, count_y)]
    forms += [(count_z, 128)] * 2 + [(4, count_z, count_y)] * (1 if lax.axis_size("gx") == 2 else 2)
    return [jax.ShapeDtypeStruct(form, jnp.float32) for form in forms]


def vmem_specs(count):
    return [pl.BlockSpec(memory_space=pltpu.VMEM)] * count


def swap_faces(faces):
    za, zb, ya, yb = faces[:4]
    halos = [swap(za, "gz", 0), swap(zb, "gz", 1), swap(ya, "gy", 0), from_distance(yb, "gy", 3)]
    return halos + [swap(face, "gx", first) for first, face in enumerate(faces[4:])]


def masked(halo, axis, first):
    index = lax.axis_index(axis)
    partner = index + 1 - 2 * lax.rem(index + first, 2)
    inside = jnp.logical_and(partner >= 0, partner < lax.axis_size(axis))
    return jnp.where(inside, halo, 0.0)


def true_order(pieces, axis):
    distance = 1
    while distance < pieces.shape[0]:
        swapped = pieces.reshape((-1, 2, distance) + pieces.shape[1:])[:, ::-1].reshape(pieces.shape)
        odd = lax.rem(lax.div(lax.axis_index(axis), distance), 2) == 1
        pieces = jnp.where(odd, swapped, pieces)
        distance *= 2
    return pieces


def shards(flow, positions, loads, block_list):
    capacity = block_list.shape[-1]
    steps, _, _, part = positions.shape
    shape = flow.shape[1:]
    count_x, count_z, count_y = shape
    size_x, size_y, size_z = lax.axis_size("gx"), lax.axis_size("gy"), lax.axis_size("gz")
    points = part * size_z
    lanes = capacity * points
    params = pltpu.CompilerParams(vmem_limit_bytes=vmem_limit)
    q = flow
    turbines = block_list.reshape(capacity)
    barrier = lax.optimization_barrier
    forms = face_shapes(shape)

    extra = pl.cdiv((3 * steps + 1) * pl.cdiv(capacity, 2), 8) * 8

    own = jnp.concatenate([positions.reshape(steps, 3, part), loads.reshape(steps, 3, part)], axis=1)
    table = jnp.pad(own, ((0, 0), (0, 2), (0, 0))).reshape(1, 8 * steps, part)
    table = jnp.concatenate([table, from_distance(table, "gz", 1)], axis=0)
    faces = pl.pallas_call(
        functools.partial(faces_body, shape=shape),
        out_shape=forms,
        in_specs=vmem_specs(1),
        out_specs=vmem_specs(len(forms)),
        compiler_params=params,
        name="faces",
    )(q)
    table, faces = barrier((table, list(faces)))
    za, zb, ya, yb = faces[:4]
    za = masked(swap(za, "gz", 0), "gz", 0)
    distance = 2
    while distance < size_z:
        received = from_distance(table, "gz", distance)
        received, za = barrier((received, za))
        table = jnp.concatenate([table, received], axis=0)
        distance *= 2
    table = true_order(table, "gz")
    table = jnp.concatenate([table[k] for k in range(size_z)], axis=1)
    rows = 8 * steps
    zb, ya, table = barrier((zb, ya, table))
    zb = masked(swap(zb, "gz", 1), "gz", 1)
    ya = swap(jnp.concatenate([ya, table], axis=0), "gy", 0)
    ya, zb = barrier((ya, zb))
    table = jnp.concatenate([table, ya[count_z:]], axis=0)
    yb = from_distance(jnp.concatenate([yb, table], axis=0), "gy", 3)
    x_faces = [swap(face, "gx", first) for first, face in enumerate(faces[4:])]
    table = jnp.concatenate([table, yb[count_z:]], axis=0)
    table = gather_relative(table[None], "gx").reshape(size_x * size_y, rows, points)
    halos = [za, zb, ya, yb] + x_faces

    samples = None
    for step in range(steps):
        last, packs = step == steps - 1, step == steps - 2
        shapes = [jax.ShapeDtypeStruct(q.shape, jnp.float32)]
        out_specs = vmem_specs(1)
        scratch = []
        if last:
            out_specs = [pl.BlockSpec(memory_space=pl.ANY)]
            scratch = [pltpu.VMEM(q.shape, jnp.float32), pltpu.SemaphoreType.DMA((count_x,))]
        else:
            shapes += face_shapes(shape, extra if packs else 0)
            if packs:
                scratch = [pltpu.VMEM((16, lanes), jnp.float32)]
            else:
                shapes += [jax.ShapeDtypeStruct((16, lanes), jnp.float32)]
            out_specs = vmem_specs(len(shapes))
        past = [] if step == 0 or last else [samples]
        results = pl.pallas_call(
            functools.partial(step_body, shape=shape, points=points, capacity=capacity, step=step, steps=steps),
            out_shape=shapes,
            in_specs=[pl.BlockSpec(memory_space=pltpu.SMEM)] + vmem_specs(2 + len(halos) + len(past)),
            out_specs=out_specs,
            scratch_shapes=scratch
            + [pltpu.VMEM((3,) + shape, jnp.float32), pltpu.VMEM((8, lanes), jnp.float32)]
            + [pltpu.VMEM((4, count_y // 128, count_x, 128), jnp.float32)] * 2
            + [pltpu.VMEM((count_z, 128), jnp.float32)] * 2
            + [pltpu.VMEM((4, count_z, count_y), jnp.float32)] * 2,
            compiler_params=params,
            name="step",
        )(turbines, table, q, *halos, *past)
        q = results[0]
        if last:
            break
        faces = results[1 : 1 + len(forms)]
        if not packs:
            samples = results[-1]
            halos = swap_faces(faces)
            continue
        za, zb, ya, yb = faces[:4]
        za_in, zb_in = swap(za, "gz", 0), swap(zb, "gz", 1)
        sums = za[4 * count_x :] + za_in[4 * count_x :]
        pieces = jnp.concatenate([sums[:, h * 128 : h * 128 + 128] for h in range(2)], axis=0)
        pieces, ya, zb_in = barrier((pieces, ya, zb_in))
        ya_in = swap(jnp.concatenate([ya, pieces], axis=0), "gy", 0)
        x_faces = [swap(face, "gx", first) for first, face in enumerate(faces[4:])]
        pieces = jnp.concatenate([pieces, ya_in[count_z:]], axis=0)
        pieces, yb, x_faces = barrier((pieces, yb, x_faces))
        yb_in = from_distance(jnp.concatenate([yb, pieces], axis=0), "gy", 3)
        pieces = jnp.concatenate([pieces, yb_in[count_z:]], axis=0)
        halos = [za_in, zb_in, ya_in, yb_in] + x_faces

    distance = 2
    while distance < size_z:
        pieces = pieces + from_distance(pieces, "gz", distance)
        distance *= 2
    pieces, q = barrier((pieces, q))
    mine = lax.dynamic_slice_in_dim(pieces, lax.axis_index("gz") * part, part, axis=1)[None]
    mine = gather_relative(mine, "gx").reshape(size_x * size_y, 2, extra, part)
    holder = (lax.axis_index("gx") * size_y + lax.axis_index("gy") + 1).astype(jnp.float32)
    returned = 0.0
    for j in range(capacity):
        row = (j // 2) * (3 * steps + 1)
        values = mine[:, j % 2, row : row + 3 * steps]
        match = mine[:, j % 2, row + 3 * steps :][:, :1] == holder
        returned = returned + jnp.sum(jnp.where(match, values, 0.0), axis=0)
    return q, returned.reshape(positions.shape)


def solution(mesh):
    in_specs = (
        P(None, "gx", "gz", "gy"),
        P(None, None, ("gx", "gy"), "gz"),
        P(None, None, ("gx", "gy"), "gz"),
        P("gx", "gy", "gz", None),
    )
    out_specs = (P(None, "gx", "gz", "gy"), P(None, None, ("gx", "gy"), "gz"))
    return jax.shard_map(shards, mesh=mesh, in_specs=in_specs, out_specs=out_specs, check_vma=False)
```

```python
import functools
import math

import jax
import jax.numpy as jnp
from jax import lax
from jax.experimental import pallas as pl
from jax.experimental.pallas import tpu as pltpu
from jax.sharding import PartitionSpec as P

kernel_width = 2.0
kernel_norm = 1.0 / (math.pi**1.5 * kernel_width**3)
time_step = 0.1
smag_coef = 0.17
viscosity = 0.02
diffusivity = 0.02
prandtl = 0.4
vmem_limit = 24 << 20


def swap_pairs(count, first):
    pairs = []
    for low in range(first, count - 1, 2):
        pairs += [(low, low + 1), (low + 1, low)]
    return pairs


def swap(value, axis, first):
    pairs = swap_pairs(lax.axis_size(axis), first)
    if not pairs:
        return jnp.zeros_like(value)
    return lax.ppermute(value, axis, pairs)


def from_distance(value, axis, distance):
    count = lax.axis_size(axis)
    return lax.ppermute(value, axis, [(i, i ^ distance) for i in range(count)])


def gather_relative(value, axis):
    distance = 1
    while distance < lax.axis_size(axis):
        value = jnp.concatenate([value, from_distance(value, axis, distance)], axis=0)
        distance *= 2
    return value


def pick(flag, first, second):
    return jnp.where(flag, first, second)


def is_even(axis):
    return lax.rem(lax.axis_index(axis), 2) == 0


def write_faces(q_ref, face_refs, shape):
    count_x, count_z, count_y = shape
    za_ref, zb_ref, ya_ref, yb_ref, xa_ref = face_refs[:5]
    even_x, even_z, even_y = is_even("gx"), is_even("gz"), is_even("gy")
    low, high = q_ref[:, 0], q_ref[:, count_x - 1]
    xa_ref[...] = pick(even_x, high, low)
    for xb_ref in face_refs[5:]:
        xb_ref[...] = pick(even_x, low, high)
    for comp in range(4):
        low = q_ref[comp, :, 0, :]
        high = q_ref[comp, :, count_z - 1, :]
        za_ref[comp * count_x : (comp + 1) * count_x] = pick(even_z, high, low)
        zb_ref[comp * count_x : (comp + 1) * count_x] = pick(even_z, low, high)
    lane = lax.broadcasted_iota(jnp.int32, (count_z, 128), 1)
    low = jnp.zeros((count_z, 128), jnp.float32)
    high = jnp.zeros((count_z, 128), jnp.float32)
    for comp in range(4):
        for x in range(count_x):
            place = comp * count_x + x
            first = q_ref[comp, x, :, :128]
            last = q_ref[comp, x, :, count_y - 128 :]
            low = jnp.where(lane == place, pltpu.roll(first, place, 1), low)
            high = jnp.where(lane == place, pltpu.roll(last, (place + 1) % 128, 1), high)
    ya_ref[...] = pick(even_y, high, low)
    yb_ref[...] = pick(even_y, low, high)


def faces_body(q_ref, *face_refs, shape):
    write_faces(q_ref, face_refs, shape)


def sorted_slots(list_ref, capacity):
    slots = [list_ref[j] for j in range(capacity)]
    for first in range(capacity):
        for second in range(first + 1, capacity):
            a, b = slots[first], slots[second]
            slots[first], slots[second] = jnp.minimum(a, b), jnp.maximum(a, b)
    return slots


def masks_of(shape):
    count_z = shape[1]
    sub = lax.broadcasted_iota(jnp.int32, (count_z, 128), 0)
    lane = lax.broadcasted_iota(jnp.int32, (count_z, 128), 1)
    return sub == 0, sub == count_z - 1, lane == 0, lane == 127


def tile_update(shifts, pushed):
    diffs, laplace, centre = [], [], []
    for c, minus_x, plus_x, minus_y, plus_y, minus_z, plus_z in shifts:
        diffs.append((plus_x - minus_x, plus_y - minus_y, plus_z - minus_z))
        laplace.append((plus_x + minus_x) + (plus_y + minus_y) + (plus_z + minus_z) - 6.0 * c)
        centre.append(c)
    diagonal = diffs[0][0] * diffs[0][0] + diffs[1][1] * diffs[1][1] + diffs[2][2] * diffs[2][2]
    xy = diffs[0][1] + diffs[1][0]
    xz = diffs[0][2] + diffs[2][0]
    yz = diffs[1][2] + diffs[2][1]
    total = (diagonal + diagonal) + (xy * xy + xz * xz + yz * yz)
    root = total * lax.rsqrt(jnp.maximum(total, 1.1754944e-38))
    scale_u = time_step * viscosity + (0.5 * time_step * smag_coef**2) * root
    scale_t = time_step * diffusivity + (0.5 * time_step * smag_coef**2 / prandtl) * root
    half = [0.5 * time_step * centre[a] for a in range(3)]
    out = []
    for comp in range(4):
        d = diffs[comp]
        moved = half[0] * d[0] + half[1] * d[1] + half[2] * d[2]
        value = centre[comp] - moved + (scale_u if comp < 3 else scale_t) * laplace[comp]
        out.append(value + pushed[comp] if comp < 3 else value)
    return out


def split(value):
    high = value.astype(jnp.bfloat16)
    low = (value - high.astype(jnp.float32)).astype(jnp.bfloat16)
    return high, low


def turbine_rows(rows_ref, table_ref, slots, step, points):
    size_x, size_y = lax.axis_size("gx"), lax.axis_size("gy")
    for j, slot in enumerate(slots):
        t = jnp.minimum(slot, size_x * size_y - 1)
        place_x = lax.bitwise_xor(lax.div(t, size_y), lax.axis_index("gx"))
        place_y = lax.bitwise_xor(lax.rem(t, size_y), lax.axis_index("gy"))
        entry = place_x * size_y + lax.bitwise_xor(place_y, lax.div(place_y, 2))
        rows_ref[:, j * points : (j + 1) * points] = table_ref[entry, 8 * step : 8 * step + 8, :]
    return rows_ref[...]


def point_factors(rows, listed, shape):
    lanes = rows.shape[1]

    def factor(row, axis, count):
        start = (lax.axis_index(axis) * count).astype(jnp.float32)
        cells = lax.broadcasted_iota(jnp.int32, (count, lanes), 0).astype(jnp.float32) + start
        gap = cells - row
        return jnp.exp(-(gap * gap) / kernel_width**2)

    count_x, count_z, count_y = shape
    factor_x = factor(rows[0:1], "gx", count_x)
    factor_y = factor(rows[1:2], "gy", count_y)
    factor_z = factor(rows[2:3], "gz", count_z) * jnp.where(listed, kernel_norm, 0.0)
    weights = (factor_x[:, None, :] * factor_z[None, :, :]).reshape(count_x * count_z, lanes)
    return weights, split(factor_y)


def store_factors(rows, listed, weight_ref, right_ref, shape, along_points):
    weights, (high, low) = point_factors(rows, listed, shape)
    weight_ref[...] = weights.reshape(weight_ref.shape)
    right_ref[...] = jnp.concatenate([high, high, low], axis=1 if along_points else 0)


def push(force_ref, rows, weight_ref, right_ref, start, planes, shape):
    count_z = shape[1]
    weights = weight_ref[start : start + planes].reshape(planes * count_z, -1)
    left = []
    for comp in range(3):
        first, second = split(weights * (rows[3 + comp : 4 + comp] * time_step))
        left.append(jnp.concatenate([first, second, first], axis=1))
    left = jnp.concatenate(left, axis=0)
    pushed = lax.dot_general(left, right_ref[...], (((1,), (1,)), ((), ())), preferred_element_type=jnp.float32)
    force_ref[:, start : start + planes] = pushed.reshape((3, planes) + shape[1:])


def sample(q_ref, weight_ref, right_ref, start, planes, shape):
    count_z = shape[1]
    left = []
    for comp in range(3):
        first, second = split(q_ref[comp, start : start + planes].reshape(planes * count_z, -1))
        left.append(jnp.concatenate([first, second, first], axis=1))
    along = jnp.dot(jnp.concatenate(left, axis=0), right_ref[...], preferred_element_type=jnp.float32)
    weights = weight_ref[start : start + planes].reshape(planes * count_z, -1)
    rows = planes * count_z
    return [jnp.sum(along[k * rows : (k + 1) * rows] * weights, axis=0, keepdims=True) for k in range(3)]


def step_body(*refs, shape, points, capacity, step, steps):
    count_x, count_z, count_y = shape
    last, packs = step == steps - 1, step == steps - 2
    faces = len(face_shapes(shape))
    refs = list(refs)
    list_ref, table_ref, q_ref = refs[:3]
    za_ref, zb_ref, ya_ref, yb_ref = refs[3:7]
    x_refs, refs = refs[7 : 3 + faces], refs[3 + faces :]
    past_ref = None if step == 0 or last else refs.pop(0)
    out_ref = refs.pop(0)
    sample_ref = None
    if not last:
        face_refs, refs = refs[:faces], refs[faces:]
        sample_ref = refs.pop(0)
    else:
        far_ref, out_ref, sems = out_ref, refs.pop(0), refs.pop(0)
    force_ref, rows_ref, low_z_ref, high_z_ref, low_y_ref, high_y_ref, low_x_ref, high_x_ref = refs[:8]
    weight_ref, push_right_ref = refs[8:10]
    if not last:
        next_weight_ref, sample_right_ref = refs[10:12]
    if step == 0:
        first_right_ref = refs[12]
    slots = sorted_slots(list_ref, capacity)
    turbines = lax.axis_size("gx") * lax.axis_size("gy")
    listed = slots[0] < turbines

    if not last:
        sample_ref[...] = jnp.zeros(sample_ref.shape, jnp.float32)
        if past_ref is not None:
            sample_ref[: 3 * step + 3] = past_ref[: 3 * step + 3]

    if not last:
        rows = turbine_rows(rows_ref, table_ref, slots, step + 1, points)
        store_factors(rows, listed, next_weight_ref, sample_right_ref, shape, False)
    rows = turbine_rows(rows_ref, table_ref, slots, step, points)
    store_factors(rows, listed, weight_ref, push_right_ref, shape, True)
    if step == 0:
        first_right_ref[...] = jnp.concatenate(
            [part for part in (lambda high, low: (high, high, low))(*point_factors(rows, listed, shape)[1])], axis=0
        )

    even_x, even_z, even_y = is_even("gx"), is_even("gz"), is_even("gy")
    index_y = lax.axis_index("gy")
    tiles = count_y // 128
    for comp in range(4):
        for tile in range(tiles):
            there = slice(comp * count_x, (comp + 1) * count_x), slice(tile * 128, tile * 128 + 128)
            first, second = za_ref[there], zb_ref[there]
            low_z_ref[comp, tile] = pick(even_z, second, first)
            high_z_ref[comp, tile] = pick(even_z, first, second)
    low_y_ref[...] = pick(index_y == 0, 0.0, pick(even_y, yb_ref[:count_z], ya_ref[:count_z]))
    high_y_ref[...] = pick(index_y == lax.axis_size("gy") - 1, 0.0, pick(even_y, ya_ref[:count_z], yb_ref[:count_z]))
    first = x_refs[0][...]
    second = x_refs[1][...] if len(x_refs) > 1 else 0.0
    low_x_ref[...] = pick(even_x, second, first)
    high_x_ref[...] = pick(even_x, first, second)
    first_z, last_z, first_y, last_y = masks_of(shape)

    def plane(x, minus, plus):
        centre, up, down = [], [], []
        for comp in range(4):
            row = [q_ref[comp, x, :, tile * 128 : tile * 128 + 128] for tile in range(tiles)]
            place = comp * count_x + x
            turn = (128 - place) % 128 if isinstance(place, int) else 128 - place
            centre.append(row)
            up.append([pltpu.roll(low_y_ref[...], turn, 1)] + [pltpu.roll(c, 1, 1) for c in row])
            down.append([pltpu.roll(c, 127, 1) for c in row] + [pltpu.roll(high_y_ref[...], 127 - place, 1)])
        for tile in range(tiles):
            here = slice(tile * 128, tile * 128 + 128)
            shifts = []
            for comp in range(4):
                c = centre[comp][tile]
                minus_y = jnp.where(first_y, up[comp][tile], up[comp][tile + 1])
                plus_y = jnp.where(last_y, down[comp][tile + 1], down[comp][tile])
                low_z = low_z_ref[comp, tile, pl.ds(x, 1), :]
                high_z = high_z_ref[comp, tile, pl.ds(x, 1), :]
                minus_z = jnp.where(first_z, low_z, pltpu.roll(c, 1, 0))
                plus_z = jnp.where(last_z, high_z, pltpu.roll(c, count_z - 1, 0))
                shifts.append((c, minus(comp, here), plus(comp, here), minus_y, plus_y, minus_z, plus_z))
            pushed = [force_ref[comp, x, :, here] for comp in range(3)]
            for comp, value in enumerate(tile_update(shifts, pushed)):
                out_ref[comp, x, :, here] = value

    def of_plane(x):
        return lambda comp, here: q_ref[comp, x, :, here]

    def copy_out(number, start, count):
        here = pl.ds(start, count)
        return pltpu.make_async_copy(out_ref.at[:, here], far_ref.at[:, here], sems.at[number])

    group = max(g for g in range(1, 9) if count_x % g == 0)
    groups = count_x // group
    sums = [0.0] * 3
    first_sums = [0.0] * 3
    push(force_ref, rows, weight_ref, push_right_ref, 0, group, shape)
    for number in range(groups):
        start = number * group
        if number + 1 < groups:
            push(force_ref, rows, weight_ref, push_right_ref, start + group, group, shape)
        if step == 0:
            more = sample(q_ref, weight_ref, first_right_ref, start, group, shape)
            first_sums = [a + b for a, b in zip(first_sums, more)]
        for x in range(start, start + group):
            minus = of_plane(x - 1) if x else lambda comp, here: low_x_ref[comp, :, here]
            plus = of_plane(x + 1) if x < count_x - 1 else lambda comp, here: high_x_ref[comp, :, here]
            plane(x, minus, plus)
        if last:
            copy_out(number, start, group).start()
        elif number:
            more = sample(out_ref, next_weight_ref, sample_right_ref, start - group, group, shape)
            sums = [a + b for a, b in zip(sums, more)]
    if last:
        for number in range(groups):
            copy_out(number, number * group, group).wait()
        return
    more = sample(out_ref, next_weight_ref, sample_right_ref, count_x - group, group, shape)
    for comp in range(3):
        sample_ref[3 * step + 3 + comp : 3 * step + 4 + comp] = sums[comp] + more[comp]
        if step == 0:
            sample_ref[comp : comp + 1] = first_sums[comp]
    write_faces(out_ref, face_refs, shape)

    if packs:
        count = 3 * steps + 1
        za_ref = face_refs[0]
        start = 4 * count_x
        za_ref[start:] = jnp.zeros((za_ref.shape[0] - start, count_y), jnp.float32)
        for j, slot in enumerate(slots):
            lane, row = (j % 2) * points, start + (j // 2) * count
            values = sample_ref[: count - 1, j * points : (j + 1) * points]
            za_ref[row : row + count - 1, lane : lane + points] = values
            name = jnp.where(listed, 0.5 * (slot + 1).astype(jnp.float32), 0.0)
            za_ref[row + count - 1 : row + count, lane : lane + points] = jnp.full((1, points), name)


def face_shapes(shape, extra=0):
    count_x, count_z, count_y = shape
    forms = [(4 * count_x + extra, count_y), (4 * count_x, count_y)]
    forms += [(count_z, 128)] * 2 + [(4, count_z, count_y)] * (1 if lax.axis_size("gx") == 2 else 2)
    return [jax.ShapeDtypeStruct(form, jnp.float32) for form in forms]


def vmem_specs(count):
    return [pl.BlockSpec(memory_space=pltpu.VMEM)] * count


def swap_faces(faces):
    za, zb, ya, yb = faces[:4]
    halos = [swap(za, "gz", 0), swap(zb, "gz", 1), swap(ya, "gy", 0), from_distance(yb, "gy", 3)]
    return halos + [swap(face, "gx", first) for first, face in enumerate(faces[4:])]


def masked(halo, axis, first):
    index = lax.axis_index(axis)
    partner = index + 1 - 2 * lax.rem(index + first, 2)
    inside = jnp.logical_and(partner >= 0, partner < lax.axis_size(axis))
    return jnp.where(inside, halo, 0.0)


def true_order(pieces, axis):
    distance = 1
    while distance < pieces.shape[0]:
        swapped = pieces.reshape((-1, 2, distance) + pieces.shape[1:])[:, ::-1].reshape(pieces.shape)
        odd = lax.rem(lax.div(lax.axis_index(axis), distance), 2) == 1
        pieces = jnp.where(odd, swapped, pieces)
        distance *= 2
    return pieces


def shards(flow, positions, loads, block_list):
    capacity = block_list.shape[-1]
    steps, _, _, part = positions.shape
    shape = flow.shape[1:]
    count_x, count_z, count_y = shape
    size_x, size_y, size_z = lax.axis_size("gx"), lax.axis_size("gy"), lax.axis_size("gz")
    points = part * size_z
    lanes = capacity * points
    params = pltpu.CompilerParams(vmem_limit_bytes=vmem_limit)
    q = flow
    turbines = block_list.reshape(capacity)
    barrier = lax.optimization_barrier
    forms = face_shapes(shape)

    extra = pl.cdiv((3 * steps + 1) * pl.cdiv(capacity, 2), 8) * 8

    own = jnp.concatenate([positions.reshape(steps, 3, part), loads.reshape(steps, 3, part)], axis=1)
    table = jnp.pad(own, ((0, 0), (0, 2), (0, 0))).reshape(1, 8 * steps, part)
    table = jnp.concatenate([table, from_distance(table, "gz", 1)], axis=0)
    faces = pl.pallas_call(
        functools.partial(faces_body, shape=shape),
        out_shape=forms,
        in_specs=vmem_specs(1),
        out_specs=vmem_specs(len(forms)),
        compiler_params=params,
        name="faces",
    )(q)
    table, faces = barrier((table, list(faces)))
    za, zb, ya, yb = faces[:4]
    za = masked(swap(za, "gz", 0), "gz", 0)
    distance = 2
    while distance < size_z:
        received = from_distance(table, "gz", distance)
        received, za = barrier((received, za))
        table = jnp.concatenate([table, received], axis=0)
        distance *= 2
    table = true_order(table, "gz")
    table = jnp.concatenate([table[k] for k in range(size_z)], axis=1)
    rows = 8 * steps
    zb, ya, table = barrier((zb, ya, table))
    zb = masked(swap(zb, "gz", 1), "gz", 1)
    ya = swap(jnp.concatenate([ya, table], axis=0), "gy", 0)
    ya, zb = barrier((ya, zb))
    table = jnp.concatenate([table, ya[count_z:]], axis=0)
    yb = from_distance(jnp.concatenate([yb, table], axis=0), "gy", 3)
    x_faces = [swap(face, "gx", first) for first, face in enumerate(faces[4:])]
    table = jnp.concatenate([table, yb[count_z:]], axis=0)
    table = gather_relative(table[None], "gx").reshape(size_x * size_y, rows, points)
    halos = [za, zb, ya, yb] + x_faces

    samples = None
    for step in range(steps):
        last, packs = step == steps - 1, step == steps - 2
        shapes = [jax.ShapeDtypeStruct(q.shape, jnp.float32)]
        out_specs = vmem_specs(1)
        scratch = []
        if last:
            out_specs = [pl.BlockSpec(memory_space=pl.ANY)]
            scratch = [pltpu.VMEM(q.shape, jnp.float32), pltpu.SemaphoreType.DMA((count_x,))]
        else:
            shapes += face_shapes(shape, extra if packs else 0)
            if packs:
                scratch = [pltpu.VMEM((16, lanes), jnp.float32)]
            else:
                shapes += [jax.ShapeDtypeStruct((16, lanes), jnp.float32)]
            out_specs = vmem_specs(len(shapes))
        past = [] if step == 0 or last else [samples]
        results = pl.pallas_call(
            functools.partial(step_body, shape=shape, points=points, capacity=capacity, step=step, steps=steps),
            out_shape=shapes,
            in_specs=[pl.BlockSpec(memory_space=pltpu.SMEM)] + vmem_specs(2 + len(halos) + len(past)),
            out_specs=out_specs,
            scratch_shapes=scratch
            + [pltpu.VMEM((3,) + shape, jnp.float32), pltpu.VMEM((8, lanes), jnp.float32)]
            + [pltpu.VMEM((4, count_y // 128, count_x, 128), jnp.float32)] * 2
            + [pltpu.VMEM((count_z, 128), jnp.float32)] * 2
            + [pltpu.VMEM((4, count_z, count_y), jnp.float32)] * 2
            + [pltpu.VMEM((count_x, count_z, lanes), jnp.float32), pltpu.VMEM((count_y, 3 * lanes), jnp.bfloat16)]
            + ([] if last else [pltpu.VMEM((count_x, count_z, lanes), jnp.float32)])
            + ([] if last else [pltpu.VMEM((3 * count_y, lanes), jnp.bfloat16)])
            + ([pltpu.VMEM((3 * count_y, lanes), jnp.bfloat16)] if step == 0 else []),
            compiler_params=params,
            name="step",
        )(turbines, table, q, *halos, *past)
        q = results[0]
        if last:
            break
        faces = results[1 : 1 + len(forms)]
        if not packs:
            samples = results[-1]
            halos = swap_faces(faces)
            continue
        za, zb, ya, yb = faces[:4]
        za_in, zb_in = swap(za, "gz", 0), swap(zb, "gz", 1)
        sums = za[4 * count_x :] + za_in[4 * count_x :]
        pieces = jnp.concatenate([sums[:, h * 128 : h * 128 + 128] for h in range(2)], axis=0)
        pieces, ya, zb_in = barrier((pieces, ya, zb_in))
        ya_in = swap(jnp.concatenate([ya, pieces], axis=0), "gy", 0)
        x_faces = [swap(face, "gx", first) for first, face in enumerate(faces[4:])]
        pieces = jnp.concatenate([pieces, ya_in[count_z:]], axis=0)
        pieces, yb, x_faces = barrier((pieces, yb, x_faces))
        yb_in = from_distance(jnp.concatenate([yb, pieces], axis=0), "gy", 3)
        pieces = jnp.concatenate([pieces, yb_in[count_z:]], axis=0)
        halos = [za_in, zb_in, ya_in, yb_in] + x_faces

    distance = 2
    while distance < size_z:
        pieces = pieces + from_distance(pieces, "gz", distance)
        distance *= 2
    pieces, q = barrier((pieces, q))
    mine = lax.dynamic_slice_in_dim(pieces, lax.axis_index("gz") * part, part, axis=1)[None]
    mine = gather_relative(mine, "gx").reshape(size_x * size_y, 2, extra, part)
    holder = (lax.axis_index("gx") * size_y + lax.axis_index("gy") + 1).astype(jnp.float32)
    returned = 0.0
    for j in range(capacity):
        row = (j // 2) * (3 * steps + 1)
        values = mine[:, j % 2, row : row + 3 * steps]
        match = mine[:, j % 2, row + 3 * steps :][:, :1] == holder
        returned = returned + jnp.sum(jnp.where(match, values, 0.0), axis=0)
    return q, returned.reshape(positions.shape)


def solution(mesh):
    in_specs = (
        P(None, "gx", "gz", "gy"),
        P(None, None, ("gx", "gy"), "gz"),
        P(None, None, ("gx", "gy"), "gz"),
        P("gx", "gy", "gz", None),
    )
    out_specs = (P(None, "gx", "gz", "gy"), P(None, None, ("gx", "gy"), "gz"))
    return jax.shard_map(shards, mesh=mesh, in_specs=in_specs, out_specs=out_specs, check_vma=False)
```

```python
import functools
import math

import jax
import jax.numpy as jnp
from jax import lax
from jax.experimental import pallas as pl
from jax.experimental.pallas import tpu as pltpu
from jax.sharding import PartitionSpec as P

kernel_width = 2.0
kernel_norm = 1.0 / (math.pi**1.5 * kernel_width**3)
time_step = 0.1
smag_coef = 0.17
viscosity = 0.02
diffusivity = 0.02
prandtl = 0.4
vmem_limit = 24 << 20


def swap_pairs(count, first):
    pairs = []
    for low in range(first, count - 1, 2):
        pairs += [(low, low + 1), (low + 1, low)]
    return pairs


def swap(value, axis, first):
    pairs = swap_pairs(lax.axis_size(axis), first)
    if not pairs:
        return jnp.zeros_like(value)
    return lax.ppermute(value, axis, pairs)


def swap_inner(value, axis):
    size, chips = lax.axis_size(axis), lax.axis_size("gx")
    target = {low: high for low, high in swap_pairs(size, 1)}
    pairs = []
    for x in range(chips):
        for k in range(size):
            pairs.append((x * size + k, x * size + target[k] if k in target else (x ^ 1) * size + k))
    return lax.ppermute(value, ("gx", axis), pairs)


def from_distance(value, axis, distance):
    count = lax.axis_size(axis)
    return lax.ppermute(value, axis, [(i, i ^ distance) for i in range(count)])


def gather_relative(value, axis):
    distance = 1
    while distance < lax.axis_size(axis):
        value = jnp.concatenate([value, from_distance(value, axis, distance)], axis=0)
        distance *= 2
    return value


def pick(flag, first, second):
    return jnp.where(flag, first, second)


def is_even(axis):
    return lax.rem(lax.axis_index(axis), 2) == 0


def write_faces(q_ref, face_refs, shape):
    count_x, count_z, count_y = shape
    za_ref, zb_ref, ya_ref, yb_ref, xa_ref = face_refs[:5]
    even_x, even_z, even_y = is_even("gx"), is_even("gz"), is_even("gy")
    low, high = q_ref[:, 0], q_ref[:, count_x - 1]
    xa_ref[...] = pick(even_x, high, low)
    for xb_ref in face_refs[5:]:
        xb_ref[...] = pick(even_x, low, high)
    for comp in range(4):
        low = q_ref[comp, :, 0, :]
        high = q_ref[comp, :, count_z - 1, :]
        za_ref[comp * count_x : (comp + 1) * count_x] = pick(even_z, high, low)
        zb_ref[comp * count_x : (comp + 1) * count_x] = pick(even_z, low, high)
    lane = lax.broadcasted_iota(jnp.int32, (count_z, 128), 1)
    low = jnp.zeros((count_z, 128), jnp.float32)
    high = jnp.zeros((count_z, 128), jnp.float32)
    for comp in range(4):
        for x in range(count_x):
            place = comp * count_x + x
            first = q_ref[comp, x, :, :128]
            last = q_ref[comp, x, :, count_y - 128 :]
            low = jnp.where(lane == place, pltpu.roll(first, place, 1), low)
            high = jnp.where(lane == place, pltpu.roll(last, (place + 1) % 128, 1), high)
    ya_ref[...] = pick(even_y, high, low)
    yb_ref[...] = pick(even_y, low, high)


def faces_body(q_ref, *face_refs, shape):
    write_faces(q_ref, face_refs, shape)


def sorted_slots(list_ref, capacity):
    slots = [list_ref[j] for j in range(capacity)]
    for first in range(capacity):
        for second in range(first + 1, capacity):
            a, b = slots[first], slots[second]
            slots[first], slots[second] = jnp.minimum(a, b), jnp.maximum(a, b)
    return slots


def masks_of(shape):
    count_z = shape[1]
    sub = lax.broadcasted_iota(jnp.int32, (count_z, 128), 0)
    lane = lax.broadcasted_iota(jnp.int32, (count_z, 128), 1)
    return sub == 0, sub == count_z - 1, lane == 0, lane == 127


def tile_update(shifts, pushed):
    diffs, laplace, centre = [], [], []
    for c, minus_x, plus_x, minus_y, plus_y, minus_z, plus_z in shifts:
        diffs.append((plus_x - minus_x, plus_y - minus_y, plus_z - minus_z))
        laplace.append((plus_x + minus_x) + (plus_y + minus_y) + (plus_z + minus_z) - 6.0 * c)
        centre.append(c)
    diagonal = diffs[0][0] * diffs[0][0] + diffs[1][1] * diffs[1][1] + diffs[2][2] * diffs[2][2]
    xy = diffs[0][1] + diffs[1][0]
    xz = diffs[0][2] + diffs[2][0]
    yz = diffs[1][2] + diffs[2][1]
    total = (diagonal + diagonal) + (xy * xy + xz * xz + yz * yz)
    root = total * lax.rsqrt(jnp.maximum(total, 1.1754944e-38))
    scale_u = time_step * viscosity + (0.5 * time_step * smag_coef**2) * root
    scale_t = time_step * diffusivity + (0.5 * time_step * smag_coef**2 / prandtl) * root
    half = [0.5 * time_step * centre[a] for a in range(3)]
    out = []
    for comp in range(4):
        d = diffs[comp]
        moved = half[0] * d[0] + half[1] * d[1] + half[2] * d[2]
        value = centre[comp] - moved + (scale_u if comp < 3 else scale_t) * laplace[comp]
        out.append(value + pushed[comp] if comp < 3 else value)
    return out


def split(value):
    high = value.astype(jnp.bfloat16)
    low = (value - high.astype(jnp.float32)).astype(jnp.bfloat16)
    return high, low


def turbine_rows(rows_ref, table_ref, slots, step, points):
    size_x, size_y = lax.axis_size("gx"), lax.axis_size("gy")
    for j, slot in enumerate(slots):
        t = jnp.minimum(slot, size_x * size_y - 1)
        place_x = lax.bitwise_xor(lax.div(t, size_y), lax.axis_index("gx"))
        place_y = lax.bitwise_xor(lax.rem(t, size_y), lax.axis_index("gy"))
        entry = place_x * size_y + lax.bitwise_xor(place_y, lax.div(place_y, 2))
        rows_ref[:, j * points : (j + 1) * points] = table_ref[entry, 8 * step : 8 * step + 8, :]
    return rows_ref[...]


def point_factors(rows, listed, shape):
    lanes = rows.shape[1]

    def factor(row, axis, count):
        start = (lax.axis_index(axis) * count).astype(jnp.float32)
        cells = lax.broadcasted_iota(jnp.int32, (count, lanes), 0).astype(jnp.float32) + start
        gap = cells - row
        return jnp.exp(-(gap * gap) / kernel_width**2)

    count_x, count_z, count_y = shape
    factor_x = factor(rows[0:1], "gx", count_x)
    factor_y = factor(rows[1:2], "gy", count_y)
    factor_z = factor(rows[2:3], "gz", count_z) * jnp.where(listed, kernel_norm, 0.0)
    weights = (factor_x[:, None, :] * factor_z[None, :, :]).reshape(count_x * count_z, lanes)
    return weights, split(factor_y)


def store_factors(rows, listed, weight_ref, right_ref, shape, along_points):
    weights, (high, low) = point_factors(rows, listed, shape)
    weight_ref[...] = weights.reshape(weight_ref.shape)
    right_ref[...] = jnp.concatenate([high, high, low], axis=1 if along_points else 0)


def push(force_ref, rows, weight_ref, right_ref, start, planes, shape):
    count_z = shape[1]
    weights = weight_ref[start : start + planes].reshape(planes * count_z, -1)
    left = []
    for comp in range(3):
        first, second = split(weights * (rows[3 + comp : 4 + comp] * time_step))
        left.append(jnp.concatenate([first, second, first], axis=1))
    left = jnp.concatenate(left, axis=0)
    pushed = lax.dot_general(left, right_ref[...], (((1,), (1,)), ((), ())), preferred_element_type=jnp.float32)
    force_ref[:, start : start + planes] = pushed.reshape((3, planes) + shape[1:])


def sample(q_ref, weight_ref, right_ref, start, planes, shape):
    count_z = shape[1]
    left = []
    for comp in range(3):
        first, second = split(q_ref[comp, start : start + planes].reshape(planes * count_z, -1))
        left.append(jnp.concatenate([first, second, first], axis=1))
    along = jnp.dot(jnp.concatenate(left, axis=0), right_ref[...], preferred_element_type=jnp.float32)
    weights = weight_ref[start : start + planes].reshape(planes * count_z, -1)
    rows = planes * count_z
    return [jnp.sum(along[k * rows : (k + 1) * rows] * weights, axis=0, keepdims=True) for k in range(3)]


def step_body(*refs, shape, points, capacity, step, steps):
    count_x, count_z, count_y = shape
    last, packs = step == steps - 1, step == steps - 2
    faces = len(face_shapes(shape))
    refs = list(refs)
    list_ref, table_ref, q_ref = refs[:3]
    za_ref, zb_ref, ya_ref, yb_ref = refs[3:7]
    x_refs, refs = refs[7 : 3 + faces], refs[3 + faces :]
    past_ref = None if step == 0 or last else refs.pop(0)
    out_ref = refs.pop(0)
    sample_ref = None
    if not last:
        face_refs, refs = refs[:faces], refs[faces:]
        sample_ref = refs.pop(0)
    else:
        far_ref, out_ref, sems = out_ref, refs.pop(0), refs.pop(0)
    force_ref, rows_ref, low_z_ref, high_z_ref, low_y_ref, high_y_ref, low_x_ref, high_x_ref = refs[:8]
    weight_ref, push_right_ref = refs[8:10]
    if not last:
        next_weight_ref, sample_right_ref = refs[10:12]
    if step == 0:
        first_right_ref = refs[12]
    slots = sorted_slots(list_ref, capacity)
    turbines = lax.axis_size("gx") * lax.axis_size("gy")
    listed = slots[0] < turbines

    if not last:
        sample_ref[...] = jnp.zeros(sample_ref.shape, jnp.float32)
        if past_ref is not None:
            sample_ref[: 3 * step + 3] = past_ref[: 3 * step + 3]

    if not last:
        rows = turbine_rows(rows_ref, table_ref, slots, step + 1, points)
        store_factors(rows, listed, next_weight_ref, sample_right_ref, shape, False)
    rows = turbine_rows(rows_ref, table_ref, slots, step, points)
    store_factors(rows, listed, weight_ref, push_right_ref, shape, True)
    if step == 0:
        high, low = point_factors(rows, listed, shape)[1]
        first_right_ref[...] = jnp.concatenate([high, high, low], axis=0)

    even_x, even_z, even_y = is_even("gx"), is_even("gz"), is_even("gy")
    index_y, index_z = lax.axis_index("gy"), lax.axis_index("gz")
    tiles = count_y // 128
    for comp in range(4):
        for tile in range(tiles):
            there = slice(comp * count_x, (comp + 1) * count_x), slice(tile * 128, tile * 128 + 128)
            first, second = za_ref[there], zb_ref[there]
            low_z_ref[comp, tile] = pick(index_z == 0, 0.0, pick(even_z, second, first))
            high_z_ref[comp, tile] = pick(index_z == lax.axis_size("gz") - 1, 0.0, pick(even_z, first, second))
    low_y_ref[...] = pick(index_y == 0, 0.0, pick(even_y, yb_ref[:count_z], ya_ref[:count_z]))
    high_y_ref[...] = pick(index_y == lax.axis_size("gy") - 1, 0.0, pick(even_y, ya_ref[:count_z], yb_ref[:count_z]))
    first = x_refs[0][...]
    second = x_refs[1][...] if len(x_refs) > 1 else 0.0
    low_x_ref[...] = pick(even_x, second, first)
    high_x_ref[...] = pick(even_x, first, second)
    first_z, last_z, first_y, last_y = masks_of(shape)

    def plane(x, minus, plus):
        centre, up, down = [], [], []
        for comp in range(4):
            row = [q_ref[comp, x, :, tile * 128 : tile * 128 + 128] for tile in range(tiles)]
            place = comp * count_x + x
            turn = (128 - place) % 128 if isinstance(place, int) else 128 - place
            centre.append(row)
            up.append([pltpu.roll(low_y_ref[...], turn, 1)] + [pltpu.roll(c, 1, 1) for c in row])
            down.append([pltpu.roll(c, 127, 1) for c in row] + [pltpu.roll(high_y_ref[...], 127 - place, 1)])
        for tile in range(tiles):
            here = slice(tile * 128, tile * 128 + 128)
            shifts = []
            for comp in range(4):
                c = centre[comp][tile]
                minus_y = jnp.where(first_y, up[comp][tile], up[comp][tile + 1])
                plus_y = jnp.where(last_y, down[comp][tile + 1], down[comp][tile])
                low_z = low_z_ref[comp, tile, pl.ds(x, 1), :]
                high_z = high_z_ref[comp, tile, pl.ds(x, 1), :]
                minus_z = jnp.where(first_z, low_z, pltpu.roll(c, 1, 0))
                plus_z = jnp.where(last_z, high_z, pltpu.roll(c, count_z - 1, 0))
                shifts.append((c, minus(comp, here), plus(comp, here), minus_y, plus_y, minus_z, plus_z))
            pushed = [force_ref[comp, x, :, here] for comp in range(3)]
            for comp, value in enumerate(tile_update(shifts, pushed)):
                out_ref[comp, x, :, here] = value

    def of_plane(x):
        return lambda comp, here: q_ref[comp, x, :, here]

    def copy_out(number, start, count):
        here = pl.ds(start, count)
        return pltpu.make_async_copy(out_ref.at[:, here], far_ref.at[:, here], sems.at[number])

    group = max(g for g in range(1, 9) if count_x % g == 0)
    groups = count_x // group
    sums = [0.0] * 3
    first_sums = [0.0] * 3
    push(force_ref, rows, weight_ref, push_right_ref, 0, group, shape)
    for number in range(groups):
        start = number * group
        if number + 1 < groups:
            push(force_ref, rows, weight_ref, push_right_ref, start + group, group, shape)
        if step == 0:
            more = sample(q_ref, weight_ref, first_right_ref, start, group, shape)
            first_sums = [a + b for a, b in zip(first_sums, more)]
        for x in range(start, start + group):
            minus = of_plane(x - 1) if x else lambda comp, here: low_x_ref[comp, :, here]
            plus = of_plane(x + 1) if x < count_x - 1 else lambda comp, here: high_x_ref[comp, :, here]
            plane(x, minus, plus)
        if last:
            copy_out(number, start, group).start()
        elif number:
            more = sample(out_ref, next_weight_ref, sample_right_ref, start - group, group, shape)
            sums = [a + b for a, b in zip(sums, more)]
    if last:
        for number in range(groups):
            copy_out(number, number * group, group).wait()
        return
    more = sample(out_ref, next_weight_ref, sample_right_ref, count_x - group, group, shape)
    for comp in range(3):
        sample_ref[3 * step + 3 + comp : 3 * step + 4 + comp] = sums[comp] + more[comp]
        if step == 0:
            sample_ref[comp : comp + 1] = first_sums[comp]
    write_faces(out_ref, face_refs, shape)

    if packs:
        count = 3 * steps + 1
        za_ref = face_refs[0]
        start = 4 * count_x
        za_ref[start:] = jnp.zeros((za_ref.shape[0] - start, count_y), jnp.float32)
        for j, slot in enumerate(slots):
            lane, row = (j % 2) * points, start + (j // 2) * count
            values = sample_ref[: count - 1, j * points : (j + 1) * points]
            za_ref[row : row + count - 1, lane : lane + points] = values
            name = jnp.where(listed, 0.5 * (slot + 1).astype(jnp.float32), 0.0)
            za_ref[row + count - 1 : row + count, lane : lane + points] = jnp.full((1, points), name)


def face_shapes(shape, extra=0):
    count_x, count_z, count_y = shape
    forms = [(4 * count_x + extra, count_y), (4 * count_x, count_y)]
    forms += [(count_z, 128)] * 2 + [(4, count_z, count_y)] * (1 if lax.axis_size("gx") == 2 else 2)
    return [jax.ShapeDtypeStruct(form, jnp.float32) for form in forms]


def vmem_specs(count):
    return [pl.BlockSpec(memory_space=pltpu.VMEM)] * count


def swap_faces(faces):
    za, zb, ya, yb = faces[:4]
    zb, za = swap_inner(zb, "gz"), swap(za, "gz", 0)
    yb, ya = swap_inner(yb, "gy"), swap(ya, "gy", 0)
    halos = [za, zb, ya, yb]
    return halos + [swap(face, "gx", first) for first, face in enumerate(faces[4:])]


def masked(halo, axis, first):
    index = lax.axis_index(axis)
    partner = index + 1 - 2 * lax.rem(index + first, 2)
    inside = jnp.logical_and(partner >= 0, partner < lax.axis_size(axis))
    return jnp.where(inside, halo, 0.0)


def true_order(pieces, axis):
    distance = 1
    while distance < pieces.shape[0]:
        swapped = pieces.reshape((-1, 2, distance) + pieces.shape[1:])[:, ::-1].reshape(pieces.shape)
        odd = lax.rem(lax.div(lax.axis_index(axis), distance), 2) == 1
        pieces = jnp.where(odd, swapped, pieces)
        distance *= 2
    return pieces


def shards(flow, positions, loads, block_list):
    capacity = block_list.shape[-1]
    steps, _, _, part = positions.shape
    shape = flow.shape[1:]
    count_x, count_z, count_y = shape
    size_x, size_y, size_z = lax.axis_size("gx"), lax.axis_size("gy"), lax.axis_size("gz")
    points = part * size_z
    lanes = capacity * points
    params = pltpu.CompilerParams(vmem_limit_bytes=vmem_limit)
    q = flow
    turbines = block_list.reshape(capacity)
    barrier = lax.optimization_barrier
    forms = face_shapes(shape)

    extra = pl.cdiv((3 * steps + 1) * pl.cdiv(capacity, 2), 8) * 8

    own = jnp.concatenate([positions.reshape(steps, 3, part), loads.reshape(steps, 3, part)], axis=1)
    table = jnp.pad(own, ((0, 0), (0, 2), (0, 0))).reshape(1, 8 * steps, part)
    table = jnp.concatenate([table, from_distance(table, "gz", 1)], axis=0)
    faces = pl.pallas_call(
        functools.partial(faces_body, shape=shape),
        out_shape=forms,
        in_specs=vmem_specs(1),
        out_specs=vmem_specs(len(forms)),
        compiler_params=params,
        name="faces",
    )(q)
    table, faces = barrier((table, list(faces)))
    za, zb, ya, yb = faces[:4]
    za = masked(swap(za, "gz", 0), "gz", 0)
    distance = 2
    while distance < size_z:
        received = from_distance(table, "gz", distance)
        received, za = barrier((received, za))
        table = jnp.concatenate([table, received], axis=0)
        distance *= 2
    table = true_order(table, "gz")
    table = jnp.concatenate([table[k] for k in range(size_z)], axis=1)
    rows = 8 * steps
    zb, ya, table = barrier((zb, ya, table))
    zb = masked(swap_inner(zb, "gz"), "gz", 1)
    ya = swap(jnp.concatenate([ya, table], axis=0), "gy", 0)
    ya, zb = barrier((ya, zb))
    table = jnp.concatenate([table, ya[count_z:]], axis=0)
    yb = from_distance(jnp.concatenate([yb, table], axis=0), "gy", 3)
    x_faces = [swap(face, "gx", first) for first, face in enumerate(faces[4:])]
    table = jnp.concatenate([table, yb[count_z:]], axis=0)
    table = gather_relative(table[None], "gx").reshape(size_x * size_y, rows, points)
    halos = [za, zb, ya, yb] + x_faces

    samples = None
    for step in range(steps):
        last, packs = step == steps - 1, step == steps - 2
        shapes = [jax.ShapeDtypeStruct(q.shape, jnp.float32)]
        out_specs = vmem_specs(1)
        scratch = []
        if last:
            out_specs = [pl.BlockSpec(memory_space=pl.ANY)]
            scratch = [pltpu.VMEM(q.shape, jnp.float32), pltpu.SemaphoreType.DMA((count_x,))]
        else:
            shapes += face_shapes(shape, extra if packs else 0)
            if packs:
                scratch = [pltpu.VMEM((16, lanes), jnp.float32)]
            else:
                shapes += [jax.ShapeDtypeStruct((16, lanes), jnp.float32)]
            out_specs = vmem_specs(len(shapes))
        past = [] if step == 0 or last else [samples]
        results = pl.pallas_call(
            functools.partial(step_body, shape=shape, points=points, capacity=capacity, step=step, steps=steps),
            out_shape=shapes,
            in_specs=[pl.BlockSpec(memory_space=pltpu.SMEM)] + vmem_specs(2 + len(halos) + len(past)),
            out_specs=out_specs,
            scratch_shapes=scratch
            + [pltpu.VMEM((3,) + shape, jnp.float32), pltpu.VMEM((8, lanes), jnp.float32)]
            + [pltpu.VMEM((4, count_y // 128, count_x, 128), jnp.float32)] * 2
            + [pltpu.VMEM((count_z, 128), jnp.float32)] * 2
            + [pltpu.VMEM((4, count_z, count_y), jnp.float32)] * 2
            + [pltpu.VMEM((count_x, count_z, lanes), jnp.float32), pltpu.VMEM((count_y, 3 * lanes), jnp.bfloat16)]
            + ([] if last else [pltpu.VMEM((count_x, count_z, lanes), jnp.float32)])
            + ([] if last else [pltpu.VMEM((3 * count_y, lanes), jnp.bfloat16)])
            + ([pltpu.VMEM((3 * count_y, lanes), jnp.bfloat16)] if step == 0 else []),
            compiler_params=params,
            name="step",
        )(turbines, table, q, *halos, *past)
        q = results[0]
        if last:
            break
        faces = results[1 : 1 + len(forms)]
        if not packs:
            samples = results[-1]
            halos = swap_faces(faces)
            continue
        za, zb, ya, yb = faces[:4]
        za_in, zb_in = swap(za, "gz", 0), swap_inner(zb, "gz")
        sums = za[4 * count_x :] + za_in[4 * count_x :]
        pieces = jnp.concatenate([sums[:, h * 128 : h * 128 + 128] for h in range(2)], axis=0)
        pieces, ya, zb_in = barrier((pieces, ya, zb_in))
        ya_in = swap(jnp.concatenate([ya, pieces], axis=0), "gy", 0)
        x_faces = [swap(face, "gx", first) for first, face in enumerate(faces[4:])]
        pieces = jnp.concatenate([pieces, ya_in[count_z:]], axis=0)
        pieces, yb, x_faces = barrier((pieces, yb, x_faces))
        yb_in = from_distance(jnp.concatenate([yb, pieces], axis=0), "gy", 3)
        pieces = jnp.concatenate([pieces, yb_in[count_z:]], axis=0)
        halos = [za_in, zb_in, ya_in, yb_in] + x_faces

    distance = 2
    while distance < size_z:
        pieces = pieces + from_distance(pieces, "gz", distance)
        distance *= 2
    pieces, q = barrier((pieces, q))
    mine = lax.dynamic_slice_in_dim(pieces, lax.axis_index("gz") * part, part, axis=1)[None]
    mine = gather_relative(mine, "gx").reshape(size_x * size_y, 2, extra, part)
    holder = (lax.axis_index("gx") * size_y + lax.axis_index("gy") + 1).astype(jnp.float32)
    returned = 0.0
    for j in range(capacity):
        row = (j // 2) * (3 * steps + 1)
        values = mine[:, j % 2, row : row + 3 * steps]
        match = mine[:, j % 2, row + 3 * steps :][:, :1] == holder
        returned = returned + jnp.sum(jnp.where(match, values, 0.0), axis=0)
    return q, returned.reshape(positions.shape)


def solution(mesh):
    in_specs = (
        P(None, "gx", "gz", "gy"),
        P(None, None, ("gx", "gy"), "gz"),
        P(None, None, ("gx", "gy"), "gz"),
        P("gx", "gy", "gz", None),
    )
    out_specs = (P(None, "gx", "gz", "gy"), P(None, None, ("gx", "gy"), "gz"))
    return jax.shard_map(shards, mesh=mesh, in_specs=in_specs, out_specs=out_specs, check_vma=False)
```

```python
import functools
import math

import jax
import jax.numpy as jnp
from jax import lax
from jax.experimental import pallas as pl
from jax.experimental.pallas import tpu as pltpu
from jax.sharding import PartitionSpec as P

kernel_width = 2.0
kernel_norm = 1.0 / (math.pi**1.5 * kernel_width**3)
time_step = 0.1
smag_coef = 0.17
viscosity = 0.02
diffusivity = 0.02
prandtl = 0.4
vmem_limit = 24 << 20


def swap_pairs(count, first):
    pairs = []
    for low in range(first, count - 1, 2):
        pairs += [(low, low + 1), (low + 1, low)]
    return pairs


def swap(value, axis, first):
    pairs = swap_pairs(lax.axis_size(axis), first)
    if not pairs:
        return jnp.zeros_like(value)
    return lax.ppermute(value, axis, pairs)


def swap_inner(value, axis):
    size, chips = lax.axis_size(axis), lax.axis_size("gx")
    target = {low: high for low, high in swap_pairs(size, 1)}
    pairs = []
    for x in range(chips):
        for k in range(size):
            pairs.append((x * size + k, x * size + target[k] if k in target else (x ^ 1) * size + k))
    return lax.ppermute(value, ("gx", axis), pairs)


def from_distance(value, axis, distance):
    count = lax.axis_size(axis)
    return lax.ppermute(value, axis, [(i, i ^ distance) for i in range(count)])


def gather_relative(value, axis, distance=1):
    while distance < lax.axis_size(axis):
        value = jnp.concatenate([value, from_distance(value, axis, distance)], axis=0)
        distance *= 2
    return value


def pick(flag, first, second):
    return jnp.where(flag, first, second)


def is_even(axis):
    return lax.rem(lax.axis_index(axis), 2) == 0


def write_faces(q_ref, face_refs, shape):
    count_x, count_z, count_y = shape
    za_ref, zb_ref, ya_ref, yb_ref, xa_ref = face_refs[:5]
    even_x, even_z, even_y = is_even("gx"), is_even("gz"), is_even("gy")
    low, high = q_ref[:, 0], q_ref[:, count_x - 1]
    xa_ref[...] = pick(even_x, high, low)
    for xb_ref in face_refs[5:]:
        xb_ref[...] = pick(even_x, low, high)
    for comp in range(4):
        low = q_ref[comp, :, 0, :]
        high = q_ref[comp, :, count_z - 1, :]
        za_ref[comp * count_x : (comp + 1) * count_x] = pick(even_z, high, low)
        zb_ref[comp * count_x : (comp + 1) * count_x] = pick(even_z, low, high)
    lane = lax.broadcasted_iota(jnp.int32, (count_z, 128), 1)
    low = jnp.zeros((count_z, 128), jnp.float32)
    high = jnp.zeros((count_z, 128), jnp.float32)
    for comp in range(4):
        for x in range(count_x):
            place = comp * count_x + x
            first = q_ref[comp, x, :, :128]
            last = q_ref[comp, x, :, count_y - 128 :]
            low = jnp.where(lane == place, pltpu.roll(first, place, 1), low)
            high = jnp.where(lane == place, pltpu.roll(last, (place + 1) % 128, 1), high)
    ya_ref[...] = pick(even_y, high, low)
    yb_ref[...] = pick(even_y, low, high)


def faces_body(q_ref, *face_refs, shape):
    write_faces(q_ref, face_refs, shape)


def sorted_slots(list_ref, capacity):
    slots = [list_ref[j] for j in range(capacity)]
    for first in range(capacity):
        for second in range(first + 1, capacity):
            a, b = slots[first], slots[second]
            slots[first], slots[second] = jnp.minimum(a, b), jnp.maximum(a, b)
    return slots


def masks_of(shape):
    count_z = shape[1]
    sub = lax.broadcasted_iota(jnp.int32, (count_z, 128), 0)
    lane = lax.broadcasted_iota(jnp.int32, (count_z, 128), 1)
    return sub == 0, sub == count_z - 1, lane == 0, lane == 127


def tile_update(shifts, pushed):
    diffs, laplace, centre = [], [], []
    for c, minus_x, plus_x, minus_y, plus_y, minus_z, plus_z in shifts:
        diffs.append((plus_x - minus_x, plus_y - minus_y, plus_z - minus_z))
        laplace.append((plus_x + minus_x) + (plus_y + minus_y) + (plus_z + minus_z) - 6.0 * c)
        centre.append(c)
    diagonal = diffs[0][0] * diffs[0][0] + diffs[1][1] * diffs[1][1] + diffs[2][2] * diffs[2][2]
    xy = diffs[0][1] + diffs[1][0]
    xz = diffs[0][2] + diffs[2][0]
    yz = diffs[1][2] + diffs[2][1]
    total = (diagonal + diagonal) + (xy * xy + xz * xz + yz * yz)
    root = total * lax.rsqrt(jnp.maximum(total, 1.1754944e-38))
    scale_u = time_step * viscosity + (0.5 * time_step * smag_coef**2) * root
    scale_t = time_step * diffusivity + (0.5 * time_step * smag_coef**2 / prandtl) * root
    half = [0.5 * time_step * centre[a] for a in range(3)]
    out = []
    for comp in range(4):
        d = diffs[comp]
        moved = half[0] * d[0] + half[1] * d[1] + half[2] * d[2]
        value = centre[comp] - moved + (scale_u if comp < 3 else scale_t) * laplace[comp]
        out.append(value + pushed[comp] if comp < 3 else value)
    return out


def split(value):
    high = value.astype(jnp.bfloat16)
    low = (value - high.astype(jnp.float32)).astype(jnp.bfloat16)
    return high, low


def turbine_rows(rows_ref, table_ref, slots, step, points):
    size_x, size_y = lax.axis_size("gx"), lax.axis_size("gy")
    for j, slot in enumerate(slots):
        t = jnp.minimum(slot, size_x * size_y - 1)
        place_x = lax.bitwise_xor(lax.div(t, size_y), lax.axis_index("gx"))
        place_y = lax.bitwise_xor(lax.rem(t, size_y), lax.axis_index("gy"))
        entry = place_x * size_y + place_y
        rows_ref[:, j * points : (j + 1) * points] = table_ref[entry, 8 * step : 8 * step + 8, :]
    return rows_ref[...]


def point_factors(rows, listed, shape):
    lanes = rows.shape[1]

    def factor(row, axis, count):
        start = (lax.axis_index(axis) * count).astype(jnp.float32)
        cells = lax.broadcasted_iota(jnp.int32, (count, lanes), 0).astype(jnp.float32) + start
        gap = cells - row
        return jnp.exp(-(gap * gap) / kernel_width**2)

    count_x, count_z, count_y = shape
    factor_x = factor(rows[0:1], "gx", count_x)
    factor_y = factor(rows[1:2], "gy", count_y)
    factor_z = factor(rows[2:3], "gz", count_z) * jnp.where(listed, kernel_norm, 0.0)
    weights = (factor_x[:, None, :] * factor_z[None, :, :]).reshape(count_x * count_z, lanes)
    return weights, split(factor_y)


def store_factors(rows, listed, weight_ref, right_ref, shape, along_points):
    weights, (high, low) = point_factors(rows, listed, shape)
    weight_ref[...] = weights.reshape(weight_ref.shape)
    right_ref[...] = jnp.concatenate([high, high, low], axis=1 if along_points else 0)


def push(force_ref, rows, weight_ref, right_ref, start, planes, shape):
    count_z = shape[1]
    weights = weight_ref[start : start + planes].reshape(planes * count_z, -1)
    left = []
    for comp in range(3):
        first, second = split(weights * (rows[3 + comp : 4 + comp] * time_step))
        left.append(jnp.concatenate([first, second, first], axis=1))
    left = jnp.concatenate(left, axis=0)
    pushed = lax.dot_general(left, right_ref[...], (((1,), (1,)), ((), ())), preferred_element_type=jnp.float32)
    force_ref[:, start : start + planes] = pushed.reshape((3, planes) + shape[1:])


def sample(q_ref, weight_ref, right_ref, start, planes, shape):
    count_z = shape[1]
    left = []
    for comp in range(3):
        first, second = split(q_ref[comp, start : start + planes].reshape(planes * count_z, -1))
        left.append(jnp.concatenate([first, second, first], axis=1))
    along = jnp.dot(jnp.concatenate(left, axis=0), right_ref[...], preferred_element_type=jnp.float32)
    weights = weight_ref[start : start + planes].reshape(planes * count_z, -1)
    rows = planes * count_z
    return [jnp.sum(along[k * rows : (k + 1) * rows] * weights, axis=0, keepdims=True) for k in range(3)]


def step_body(*refs, shape, points, capacity, step, steps):
    count_x, count_z, count_y = shape
    last, packs = step == steps - 1, step == steps - 2
    faces = len(face_shapes(shape))
    refs = list(refs)
    list_ref, table_ref, q_ref = refs[:3]
    za_ref, zb_ref, ya_ref, yb_ref = refs[3:7]
    x_refs, refs = refs[7 : 3 + faces], refs[3 + faces :]
    past_ref = None if step == 0 or last else refs.pop(0)
    out_ref = refs.pop(0)
    sample_ref = None
    if not last:
        face_refs, refs = refs[:faces], refs[faces:]
        sample_ref = refs.pop(0)
    else:
        far_ref, out_ref, sems = out_ref, refs.pop(0), refs.pop(0)
    force_ref, rows_ref, low_z_ref, high_z_ref, low_y_ref, high_y_ref, low_x_ref, high_x_ref = refs[:8]
    weight_ref, push_right_ref = refs[8:10]
    if not last:
        next_weight_ref, sample_right_ref = refs[10:12]
    if step == 0:
        first_right_ref = refs[12]
    slots = sorted_slots(list_ref, capacity)
    turbines = lax.axis_size("gx") * lax.axis_size("gy")
    listed = slots[0] < turbines

    if not last:
        sample_ref[...] = jnp.zeros(sample_ref.shape, jnp.float32)
        if past_ref is not None:
            sample_ref[: 3 * step + 3] = past_ref[: 3 * step + 3]

    if not last:
        rows = turbine_rows(rows_ref, table_ref, slots, step + 1, points)
        store_factors(rows, listed, next_weight_ref, sample_right_ref, shape, False)
    rows = turbine_rows(rows_ref, table_ref, slots, step, points)
    store_factors(rows, listed, weight_ref, push_right_ref, shape, True)
    if step == 0:
        high, low = point_factors(rows, listed, shape)[1]
        first_right_ref[...] = jnp.concatenate([high, high, low], axis=0)

    even_x, even_z, even_y = is_even("gx"), is_even("gz"), is_even("gy")
    index_y, index_z = lax.axis_index("gy"), lax.axis_index("gz")
    tiles = count_y // 128
    for comp in range(4):
        for tile in range(tiles):
            there = slice(comp * count_x, (comp + 1) * count_x), slice(tile * 128, tile * 128 + 128)
            first, second = za_ref[there], zb_ref[there]
            low_z_ref[comp, tile] = pick(index_z == 0, 0.0, pick(even_z, second, first))
            high_z_ref[comp, tile] = pick(index_z == lax.axis_size("gz") - 1, 0.0, pick(even_z, first, second))
    low_y_ref[...] = pick(index_y == 0, 0.0, pick(even_y, yb_ref[:count_z], ya_ref[:count_z]))
    high_y_ref[...] = pick(index_y == lax.axis_size("gy") - 1, 0.0, pick(even_y, ya_ref[:count_z], yb_ref[:count_z]))
    first = x_refs[0][...]
    second = x_refs[1][...] if len(x_refs) > 1 else 0.0
    low_x_ref[...] = pick(even_x, second, first)
    high_x_ref[...] = pick(even_x, first, second)
    first_z, last_z, first_y, last_y = masks_of(shape)

    def plane(x, minus, plus):
        centre, up, down = [], [], []
        for comp in range(4):
            row = [q_ref[comp, x, :, tile * 128 : tile * 128 + 128] for tile in range(tiles)]
            place = comp * count_x + x
            turn = (128 - place) % 128 if isinstance(place, int) else 128 - place
            centre.append(row)
            up.append([pltpu.roll(low_y_ref[...], turn, 1)] + [pltpu.roll(c, 1, 1) for c in row])
            down.append([pltpu.roll(c, 127, 1) for c in row] + [pltpu.roll(high_y_ref[...], 127 - place, 1)])
        for tile in range(tiles):
            here = slice(tile * 128, tile * 128 + 128)
            shifts = []
            for comp in range(4):
                c = centre[comp][tile]
                minus_y = jnp.where(first_y, up[comp][tile], up[comp][tile + 1])
                plus_y = jnp.where(last_y, down[comp][tile + 1], down[comp][tile])
                low_z = low_z_ref[comp, tile, pl.ds(x, 1), :]
                high_z = high_z_ref[comp, tile, pl.ds(x, 1), :]
                minus_z = jnp.where(first_z, low_z, pltpu.roll(c, 1, 0))
                plus_z = jnp.where(last_z, high_z, pltpu.roll(c, count_z - 1, 0))
                shifts.append((c, minus(comp, here), plus(comp, here), minus_y, plus_y, minus_z, plus_z))
            pushed = [force_ref[comp, x, :, here] for comp in range(3)]
            for comp, value in enumerate(tile_update(shifts, pushed)):
                out_ref[comp, x, :, here] = value

    def of_plane(x):
        return lambda comp, here: q_ref[comp, x, :, here]

    def copy_out(number, start, count):
        here = pl.ds(start, count)
        return pltpu.make_async_copy(out_ref.at[:, here], far_ref.at[:, here], sems.at[number])

    group = max(g for g in range(1, 9) if count_x % g == 0)
    groups = count_x // group
    sums = [0.0] * 3
    first_sums = [0.0] * 3
    push(force_ref, rows, weight_ref, push_right_ref, 0, group, shape)
    for number in range(groups):
        start = number * group
        if number + 1 < groups:
            push(force_ref, rows, weight_ref, push_right_ref, start + group, group, shape)
        if step == 0:
            more = sample(q_ref, weight_ref, first_right_ref, start, group, shape)
            first_sums = [a + b for a, b in zip(first_sums, more)]
        for x in range(start, start + group):
            minus = of_plane(x - 1) if x else lambda comp, here: low_x_ref[comp, :, here]
            plus = of_plane(x + 1) if x < count_x - 1 else lambda comp, here: high_x_ref[comp, :, here]
            plane(x, minus, plus)
        if last:
            copy_out(number, start, group).start()
        elif number:
            more = sample(out_ref, next_weight_ref, sample_right_ref, start - group, group, shape)
            sums = [a + b for a, b in zip(sums, more)]
    if last:
        for number in range(groups):
            copy_out(number, number * group, group).wait()
        return
    more = sample(out_ref, next_weight_ref, sample_right_ref, count_x - group, group, shape)
    for comp in range(3):
        sample_ref[3 * step + 3 + comp : 3 * step + 4 + comp] = sums[comp] + more[comp]
        if step == 0:
            sample_ref[comp : comp + 1] = first_sums[comp]
    write_faces(out_ref, face_refs, shape)

    if packs:
        count = 3 * steps + 1
        za_ref = face_refs[0]
        start = 4 * count_x
        za_ref[start:] = jnp.zeros((za_ref.shape[0] - start, count_y), jnp.float32)
        for j, slot in enumerate(slots):
            lane, row = (j % 2) * points, start + (j // 2) * count
            values = sample_ref[: count - 1, j * points : (j + 1) * points]
            za_ref[row : row + count - 1, lane : lane + points] = values
            name = jnp.where(listed, 0.5 * (slot + 1).astype(jnp.float32), 0.0)
            za_ref[row + count - 1 : row + count, lane : lane + points] = jnp.full((1, points), name)


def face_shapes(shape, extra=0):
    count_x, count_z, count_y = shape
    forms = [(4 * count_x + extra, count_y), (4 * count_x, count_y)]
    forms += [(count_z, 128)] * 2 + [(4, count_z, count_y)] * (1 if lax.axis_size("gx") == 2 else 2)
    return [jax.ShapeDtypeStruct(form, jnp.float32) for form in forms]


def vmem_specs(count):
    return [pl.BlockSpec(memory_space=pltpu.VMEM)] * count


def swap_faces(faces):
    za, zb, ya, yb = faces[:4]
    zb, za = swap_inner(zb, "gz"), swap(za, "gz", 0)
    yb, ya = swap_inner(yb, "gy"), swap(ya, "gy", 0)
    halos = [za, zb, ya, yb]
    return halos + [swap(face, "gx", first) for first, face in enumerate(faces[4:])]


def masked(halo, axis, first):
    index = lax.axis_index(axis)
    partner = index + 1 - 2 * lax.rem(index + first, 2)
    inside = jnp.logical_and(partner >= 0, partner < lax.axis_size(axis))
    return jnp.where(inside, halo, 0.0)


def true_order(pieces, axis):
    distance = 1
    while distance < pieces.shape[0]:
        swapped = pieces.reshape((-1, 2, distance) + pieces.shape[1:])[:, ::-1].reshape(pieces.shape)
        odd = lax.rem(lax.div(lax.axis_index(axis), distance), 2) == 1
        pieces = jnp.where(odd, swapped, pieces)
        distance *= 2
    return pieces


def shards(flow, positions, loads, block_list):
    capacity = block_list.shape[-1]
    steps, _, _, part = positions.shape
    shape = flow.shape[1:]
    count_x, count_z, count_y = shape
    size_x, size_y, size_z = lax.axis_size("gx"), lax.axis_size("gy"), lax.axis_size("gz")
    points = part * size_z
    lanes = capacity * points
    params = pltpu.CompilerParams(vmem_limit_bytes=vmem_limit)
    q = flow
    turbines = block_list.reshape(capacity)
    barrier = lax.optimization_barrier
    forms = face_shapes(shape)

    extra = pl.cdiv((3 * steps + 1) * pl.cdiv(capacity, 2), 8) * 8

    own = jnp.concatenate([positions.reshape(steps, 3, part), loads.reshape(steps, 3, part)], axis=1)
    table = jnp.pad(own, ((0, 0), (0, 2), (0, 0))).reshape(1, 8 * steps, part)
    table = jnp.concatenate([table, from_distance(table, "gz", 1)], axis=0)
    faces = pl.pallas_call(
        functools.partial(faces_body, shape=shape),
        out_shape=forms,
        in_specs=vmem_specs(1),
        out_specs=vmem_specs(len(forms)),
        compiler_params=params,
        name="faces",
    )(q)
    table, faces = barrier((table, list(faces)))
    za, zb, ya, yb = faces[:4]
    za = masked(swap(za, "gz", 0), "gz", 0)
    distance = 2
    while distance < size_z:
        received = from_distance(table, "gz", distance)
        received, za = barrier((received, za))
        table = jnp.concatenate([table, received], axis=0)
        distance *= 2
    table = true_order(table, "gz")
    table = jnp.concatenate([table[k] for k in range(size_z)], axis=1)
    rows = 8 * steps
    zb, yb, ya, table = barrier((zb, yb, ya, table))
    zb = masked(swap_inner(zb, "gz"), "gz", 1)
    yb = swap_inner(yb, "gy")
    ya = swap(jnp.concatenate([ya, table], axis=0), "gy", 0)
    ya, zb, yb = barrier((ya, zb, yb))
    table = jnp.concatenate([table, ya[count_z:]], axis=0).reshape(2, rows, points)
    table = gather_relative(table, "gy", 2)
    x_faces = [swap(face, "gx", first) for first, face in enumerate(faces[4:])]
    table = gather_relative(table[None], "gx").reshape(size_x * size_y, rows, points)
    halos = [za, zb, ya, yb] + x_faces

    samples = None
    for step in range(steps):
        last, packs = step == steps - 1, step == steps - 2
        shapes = [jax.ShapeDtypeStruct(q.shape, jnp.float32)]
        out_specs = vmem_specs(1)
        scratch = []
        if last:
            out_specs = [pl.BlockSpec(memory_space=pl.ANY)]
            scratch = [pltpu.VMEM(q.shape, jnp.float32), pltpu.SemaphoreType.DMA((count_x,))]
        else:
            shapes += face_shapes(shape, extra if packs else 0)
            if packs:
                scratch = [pltpu.VMEM((16, lanes), jnp.float32)]
            else:
                shapes += [jax.ShapeDtypeStruct((16, lanes), jnp.float32)]
            out_specs = vmem_specs(len(shapes))
        past = [] if step == 0 or last else [samples]
        results = pl.pallas_call(
            functools.partial(step_body, shape=shape, points=points, capacity=capacity, step=step, steps=steps),
            out_shape=shapes,
            in_specs=[pl.BlockSpec(memory_space=pltpu.SMEM)] + vmem_specs(2 + len(halos) + len(past)),
            out_specs=out_specs,
            scratch_shapes=scratch
            + [pltpu.VMEM((3,) + shape, jnp.float32), pltpu.VMEM((8, lanes), jnp.float32)]
            + [pltpu.VMEM((4, count_y // 128, count_x, 128), jnp.float32)] * 2
            + [pltpu.VMEM((count_z, 128), jnp.float32)] * 2
            + [pltpu.VMEM((4, count_z, count_y), jnp.float32)] * 2
            + [pltpu.VMEM((count_x, count_z, lanes), jnp.float32), pltpu.VMEM((count_y, 3 * lanes), jnp.bfloat16)]
            + ([] if last else [pltpu.VMEM((count_x, count_z, lanes), jnp.float32)])
            + ([] if last else [pltpu.VMEM((3 * count_y, lanes), jnp.bfloat16)])
            + ([pltpu.VMEM((3 * count_y, lanes), jnp.bfloat16)] if step == 0 else []),
            compiler_params=params,
            name="step",
        )(turbines, table, q, *halos, *past)
        q = results[0]
        if last:
            break
        faces = results[1 : 1 + len(forms)]
        if not packs:
            samples = results[-1]
            halos = swap_faces(faces)
            continue
        za, zb, ya, yb = faces[:4]
        za_in, zb_in, yb_in = swap(za, "gz", 0), swap_inner(zb, "gz"), swap_inner(yb, "gy")
        sums = za[4 * count_x :] + za_in[4 * count_x :]
        pieces = jnp.concatenate([sums[:, h * 128 : h * 128 + 128] for h in range(2)], axis=0)
        pieces, ya, zb_in, yb_in = barrier((pieces, ya, zb_in, yb_in))
        ya_in = swap(jnp.concatenate([ya, pieces], axis=0), "gy", 0)
        x_faces = [swap(face, "gx", first) for first, face in enumerate(faces[4:])]
        pieces = jnp.concatenate([pieces, ya_in[count_z:]], axis=0).reshape(2, -1, points)
        pieces, x_faces = barrier((pieces, x_faces))
        pieces = gather_relative(pieces, "gy", 2).reshape(-1, points)
        halos = [za_in, zb_in, ya_in, yb_in] + x_faces

    distance = 2
    while distance < size_z:
        pieces = pieces + from_distance(pieces, "gz", distance)
        distance *= 2
    pieces, q = barrier((pieces, q))
    mine = lax.dynamic_slice_in_dim(pieces, lax.axis_index("gz") * part, part, axis=1)[None]
    mine = gather_relative(mine, "gx").reshape(size_x * size_y, 2, extra, part)
    holder = (lax.axis_index("gx") * size_y + lax.axis_index("gy") + 1).astype(jnp.float32)
    returned = 0.0
    for j in range(capacity):
        row = (j // 2) * (3 * steps + 1)
        values = mine[:, j % 2, row : row + 3 * steps]
        match = mine[:, j % 2, row + 3 * steps :][:, :1] == holder
        returned = returned + jnp.sum(jnp.where(match, values, 0.0), axis=0)
    return q, returned.reshape(positions.shape)


def solution(mesh):
    in_specs = (
        P(None, "gx", "gz", "gy"),
        P(None, None, ("gx", "gy"), "gz"),
        P(None, None, ("gx", "gy"), "gz"),
        P("gx", "gy", "gz", None),
    )
    out_specs = (P(None, "gx", "gz", "gy"), P(None, None, ("gx", "gy"), "gz"))
    return jax.shard_map(shards, mesh=mesh, in_specs=in_specs, out_specs=out_specs, check_vma=False)
```

```python
import functools
import math

import jax
import jax.numpy as jnp
from jax import lax
from jax.experimental import pallas as pl
from jax.experimental.pallas import tpu as pltpu
from jax.sharding import PartitionSpec as P

kernel_width = 2.0
kernel_norm = 1.0 / (math.pi**1.5 * kernel_width**3)
time_step = 0.1
smag_coef = 0.17
viscosity = 0.02
diffusivity = 0.02
prandtl = 0.4
vmem_limit = 24 << 20


def swap_pairs(count, first):
    pairs = []
    for low in range(first, count - 1, 2):
        pairs += [(low, low + 1), (low + 1, low)]
    return pairs


def swap(value, axis, first):
    pairs = swap_pairs(lax.axis_size(axis), first)
    if not pairs:
        return jnp.zeros_like(value)
    return lax.ppermute(value, axis, pairs)


def swap_inner(value, axis):
    size, chips = lax.axis_size(axis), lax.axis_size("gx")
    target = {low: high for low, high in swap_pairs(size, 1)}
    pairs = []
    for x in range(chips):
        for k in range(size):
            pairs.append((x * size + k, x * size + target[k] if k in target else (x ^ 1) * size + k))
    return lax.ppermute(value, ("gx", axis), pairs)


def from_distance(value, axis, distance):
    count = lax.axis_size(axis)
    return lax.ppermute(value, axis, [(i, i ^ distance) for i in range(count)])


def gather_relative(value, axis, distance=1):
    while distance < lax.axis_size(axis):
        value = jnp.concatenate([value, from_distance(value, axis, distance)], axis=0)
        distance *= 2
    return value


def pick(flag, first, second):
    return jnp.where(flag, first, second)


def is_even(axis):
    return lax.rem(lax.axis_index(axis), 2) == 0


def write_faces(q_ref, face_refs, shape):
    count_x, count_z, count_y = shape
    za_ref, zb_ref, ya_ref, yb_ref, xa_ref = face_refs[:5]
    even_x, even_z, even_y = is_even("gx"), is_even("gz"), is_even("gy")
    low, high = q_ref[:, 0], q_ref[:, count_x - 1]
    xa_ref[...] = pick(even_x, high, low)
    for xb_ref in face_refs[5:]:
        xb_ref[...] = pick(even_x, low, high)
    for comp in range(4):
        low = q_ref[comp, :, 0, :]
        high = q_ref[comp, :, count_z - 1, :]
        za_ref[comp * count_x : (comp + 1) * count_x] = pick(even_z, high, low)
        zb_ref[comp * count_x : (comp + 1) * count_x] = pick(even_z, low, high)
    lane = lax.broadcasted_iota(jnp.int32, (count_z, 128), 1)
    low = jnp.zeros((count_z, 128), jnp.float32)
    high = jnp.zeros((count_z, 128), jnp.float32)
    for comp in range(4):
        for x in range(count_x):
            place = comp * count_x + x
            first = q_ref[comp, x, :, :128]
            last = q_ref[comp, x, :, count_y - 128 :]
            low = jnp.where(lane == place, pltpu.roll(first, place, 1), low)
            high = jnp.where(lane == place, pltpu.roll(last, (place + 1) % 128, 1), high)
    ya_ref[...] = pick(even_y, high, low)
    yb_ref[...] = pick(even_y, low, high)


def faces_body(q_ref, *face_refs, shape):
    write_faces(q_ref, face_refs, shape)


def sorted_slots(list_ref, capacity):
    slots = [list_ref[j] for j in range(capacity)]
    for first in range(capacity):
        for second in range(first + 1, capacity):
            a, b = slots[first], slots[second]
            slots[first], slots[second] = jnp.minimum(a, b), jnp.maximum(a, b)
    return slots


def masks_of(shape):
    count_z = shape[1]
    sub = lax.broadcasted_iota(jnp.int32, (count_z, 128), 0)
    lane = lax.broadcasted_iota(jnp.int32, (count_z, 128), 1)
    return sub == 0, sub == count_z - 1, lane == 0, lane == 127


def tile_update(shifts, pushed):
    diffs, laplace, centre = [], [], []
    for c, minus_x, plus_x, minus_y, plus_y, minus_z, plus_z in shifts:
        diffs.append((plus_x - minus_x, plus_y - minus_y, plus_z - minus_z))
        laplace.append((plus_x + minus_x) + (plus_y + minus_y) + (plus_z + minus_z) - 6.0 * c)
        centre.append(c)
    diagonal = diffs[0][0] * diffs[0][0] + diffs[1][1] * diffs[1][1] + diffs[2][2] * diffs[2][2]
    xy = diffs[0][1] + diffs[1][0]
    xz = diffs[0][2] + diffs[2][0]
    yz = diffs[1][2] + diffs[2][1]
    total = (diagonal + diagonal) + (xy * xy + xz * xz + yz * yz)
    root = total * lax.rsqrt(jnp.maximum(total, 1.1754944e-38))
    scale_u = time_step * viscosity + (0.5 * time_step * smag_coef**2) * root
    scale_t = time_step * diffusivity + (0.5 * time_step * smag_coef**2 / prandtl) * root
    half = [0.5 * time_step * centre[a] for a in range(3)]
    out = []
    for comp in range(4):
        d = diffs[comp]
        moved = half[0] * d[0] + half[1] * d[1] + half[2] * d[2]
        value = centre[comp] - moved + (scale_u if comp < 3 else scale_t) * laplace[comp]
        out.append(value + pushed[comp] if comp < 3 else value)
    return out


def split(value):
    high = value.astype(jnp.bfloat16)
    low = (value - high.astype(jnp.float32)).astype(jnp.bfloat16)
    return high, low


def turbine_rows(rows_ref, table_ref, slots, step, points):
    size_x, size_y = lax.axis_size("gx"), lax.axis_size("gy")
    for j, slot in enumerate(slots):
        t = jnp.minimum(slot, size_x * size_y - 1)
        place_x = lax.bitwise_xor(lax.div(t, size_y), lax.axis_index("gx"))
        place_y = lax.bitwise_xor(lax.rem(t, size_y), lax.axis_index("gy"))
        entry = place_x * size_y + place_y
        rows_ref[:, j * points : (j + 1) * points] = table_ref[entry, 8 * step : 8 * step + 8, :]
    return rows_ref[...]


def point_factors(rows, listed, shape):
    lanes = rows.shape[1]

    def factor(row, axis, count):
        start = (lax.axis_index(axis) * count).astype(jnp.float32)
        cells = lax.broadcasted_iota(jnp.int32, (count, lanes), 0).astype(jnp.float32) + start
        gap = cells - row
        return jnp.exp(-(gap * gap) / kernel_width**2)

    count_x, count_z, count_y = shape
    factor_x = factor(rows[0:1], "gx", count_x)
    factor_y = factor(rows[1:2], "gy", count_y)
    factor_z = factor(rows[2:3], "gz", count_z) * jnp.where(listed, kernel_norm, 0.0)
    weights = (factor_x[:, None, :] * factor_z[None, :, :]).reshape(count_x * count_z, lanes)
    return weights, split(factor_y)


def store_factors(rows, listed, weight_ref, right_ref, shape, along_points):
    weights, (high, low) = point_factors(rows, listed, shape)
    weight_ref[...] = weights.reshape(weight_ref.shape)
    right_ref[...] = jnp.concatenate([high, high, low], axis=1 if along_points else 0)


def push(force_ref, rows, weight_ref, right_ref, start, planes, shape):
    count_z = shape[1]
    weights = weight_ref[start : start + planes].reshape(planes * count_z, -1)
    left = []
    for comp in range(3):
        first, second = split(weights * (rows[3 + comp : 4 + comp] * time_step))
        left.append(jnp.concatenate([first, second, first], axis=1))
    left = jnp.concatenate(left, axis=0)
    pushed = lax.dot_general(left, right_ref[...], (((1,), (1,)), ((), ())), preferred_element_type=jnp.float32)
    force_ref[:, start : start + planes] = pushed.reshape((3, planes) + shape[1:])


def sample(q_ref, weight_ref, right_ref, start, planes, shape):
    count_z = shape[1]
    left = []
    for comp in range(3):
        first, second = split(q_ref[comp, start : start + planes].reshape(planes * count_z, -1))
        left.append(jnp.concatenate([first, second, first], axis=1))
    along = jnp.dot(jnp.concatenate(left, axis=0), right_ref[...], preferred_element_type=jnp.float32)
    weights = weight_ref[start : start + planes].reshape(planes * count_z, -1)
    rows = planes * count_z
    return [jnp.sum(along[k * rows : (k + 1) * rows] * weights, axis=0, keepdims=True) for k in range(3)]


def step_body(*refs, shape, points, capacity, step, steps):
    count_x, count_z, count_y = shape
    last, packs = step == steps - 1, step == steps - 2
    faces = len(face_shapes(shape))
    refs = list(refs)
    list_ref, table_ref, q_ref = refs[:3]
    za_ref, zb_ref, ya_ref, yb_ref = refs[3:7]
    x_refs, refs = refs[7 : 3 + faces], refs[3 + faces :]
    past_ref = None if step == 0 or last else refs.pop(0)
    out_ref = refs.pop(0)
    sample_ref = None
    if not last:
        face_refs, refs = refs[:faces], refs[faces:]
        sample_ref = refs.pop(0)
    else:
        far_ref, out_ref, sems = out_ref, refs.pop(0), refs.pop(0)
    force_ref, rows_ref, low_z_ref, high_z_ref, low_y_ref, high_y_ref, low_x_ref, high_x_ref = refs[:8]
    weight_ref, push_right_ref = refs[8:10]
    if not last:
        next_weight_ref, sample_right_ref = refs[10:12]
    if step == 0:
        first_right_ref = refs[12]
    slots = sorted_slots(list_ref, capacity)
    turbines = lax.axis_size("gx") * lax.axis_size("gy")
    listed = slots[0] < turbines

    if not last:
        sample_ref[...] = jnp.zeros(sample_ref.shape, jnp.float32)
        if past_ref is not None:
            sample_ref[: 3 * step + 3] = past_ref[: 3 * step + 3]

    if not last:
        rows = turbine_rows(rows_ref, table_ref, slots, step + 1, points)
        store_factors(rows, listed, next_weight_ref, sample_right_ref, shape, False)
    rows = turbine_rows(rows_ref, table_ref, slots, step, points)
    store_factors(rows, listed, weight_ref, push_right_ref, shape, True)
    if step == 0:
        high, low = point_factors(rows, listed, shape)[1]
        first_right_ref[...] = jnp.concatenate([high, high, low], axis=0)

    even_x, even_z, even_y = is_even("gx"), is_even("gz"), is_even("gy")
    index_y, index_z = lax.axis_index("gy"), lax.axis_index("gz")
    tiles = count_y // 128
    for comp in range(4):
        for tile in range(tiles):
            there = slice(comp * count_x, (comp + 1) * count_x), slice(tile * 128, tile * 128 + 128)
            first, second = za_ref[there], zb_ref[there]
            low_z_ref[comp, tile] = pick(index_z == 0, 0.0, pick(even_z, second, first))
            high_z_ref[comp, tile] = pick(index_z == lax.axis_size("gz") - 1, 0.0, pick(even_z, first, second))
    low_y_ref[...] = pick(index_y == 0, 0.0, pick(even_y, yb_ref[:count_z], ya_ref[:count_z]))
    high_y_ref[...] = pick(index_y == lax.axis_size("gy") - 1, 0.0, pick(even_y, ya_ref[:count_z], yb_ref[:count_z]))
    first = x_refs[0][...]
    second = x_refs[1][...] if len(x_refs) > 1 else 0.0
    low_x_ref[...] = pick(even_x, second, first)
    high_x_ref[...] = pick(even_x, first, second)
    first_z, last_z, first_y, last_y = masks_of(shape)

    def plane(x, minus, plus):
        centre, up, down = [], [], []
        for comp in range(4):
            row = [q_ref[comp, x, :, tile * 128 : tile * 128 + 128] for tile in range(tiles)]
            place = comp * count_x + x
            turn = (128 - place) % 128 if isinstance(place, int) else 128 - place
            centre.append(row)
            up.append([pltpu.roll(low_y_ref[...], turn, 1)] + [pltpu.roll(c, 1, 1) for c in row])
            down.append([pltpu.roll(c, 127, 1) for c in row] + [pltpu.roll(high_y_ref[...], 127 - place, 1)])
        for tile in range(tiles):
            here = slice(tile * 128, tile * 128 + 128)
            shifts = []
            for comp in range(4):
                c = centre[comp][tile]
                minus_y = jnp.where(first_y, up[comp][tile], up[comp][tile + 1])
                plus_y = jnp.where(last_y, down[comp][tile + 1], down[comp][tile])
                low_z = low_z_ref[comp, tile, pl.ds(x, 1), :]
                high_z = high_z_ref[comp, tile, pl.ds(x, 1), :]
                minus_z = jnp.where(first_z, low_z, pltpu.roll(c, 1, 0))
                plus_z = jnp.where(last_z, high_z, pltpu.roll(c, count_z - 1, 0))
                shifts.append((c, minus(comp, here), plus(comp, here), minus_y, plus_y, minus_z, plus_z))
            pushed = [force_ref[comp, x, :, here] for comp in range(3)]
            for comp, value in enumerate(tile_update(shifts, pushed)):
                out_ref[comp, x, :, here] = value

    def of_plane(x):
        return lambda comp, here: q_ref[comp, x, :, here]

    def copy_out(number, start, count):
        here = pl.ds(start, count)
        return pltpu.make_async_copy(out_ref.at[:, here], far_ref.at[:, here], sems.at[number])

    group = max(g for g in range(1, 9) if count_x % g == 0)
    groups = count_x // group
    sums = [0.0] * 3
    first_sums = [0.0] * 3
    push(force_ref, rows, weight_ref, push_right_ref, 0, group, shape)
    for number in range(groups):
        start = number * group
        if number + 1 < groups:
            push(force_ref, rows, weight_ref, push_right_ref, start + group, group, shape)
        if step == 0:
            more = sample(q_ref, weight_ref, first_right_ref, start, group, shape)
            first_sums = [a + b for a, b in zip(first_sums, more)]
        for x in range(start, start + group):
            minus = of_plane(x - 1) if x else lambda comp, here: low_x_ref[comp, :, here]
            plus = of_plane(x + 1) if x < count_x - 1 else lambda comp, here: high_x_ref[comp, :, here]
            plane(x, minus, plus)
        if last:
            copy_out(number, start, group).start()
        elif number:
            more = sample(out_ref, next_weight_ref, sample_right_ref, start - group, group, shape)
            sums = [a + b for a, b in zip(sums, more)]
    if last:
        for number in range(groups):
            copy_out(number, number * group, group).wait()
        return
    more = sample(out_ref, next_weight_ref, sample_right_ref, count_x - group, group, shape)
    for comp in range(3):
        sample_ref[3 * step + 3 + comp : 3 * step + 4 + comp] = sums[comp] + more[comp]
        if step == 0:
            sample_ref[comp : comp + 1] = first_sums[comp]
    write_faces(out_ref, face_refs, shape)

    if packs:
        count = 3 * steps + 1
        za_ref = face_refs[0]
        start = 4 * count_x
        za_ref[start:] = jnp.zeros((za_ref.shape[0] - start, count_y), jnp.float32)
        for j, slot in enumerate(slots):
            lane, row = (j % 2) * points, start + (j // 2) * count
            values = sample_ref[: count - 1, j * points : (j + 1) * points]
            za_ref[row : row + count - 1, lane : lane + points] = values
            name = jnp.where(listed, 0.5 * (slot + 1).astype(jnp.float32), 0.0)
            za_ref[row + count - 1 : row + count, lane : lane + points] = jnp.full((1, points), name)


def face_shapes(shape, extra=0):
    count_x, count_z, count_y = shape
    forms = [(4 * count_x + extra, count_y), (4 * count_x, count_y)]
    forms += [(count_z, 128)] * 2 + [(4, count_z, count_y)] * (1 if lax.axis_size("gx") == 2 else 2)
    return [jax.ShapeDtypeStruct(form, jnp.float32) for form in forms]


def vmem_specs(count):
    return [pl.BlockSpec(memory_space=pltpu.VMEM)] * count


def swap_faces(faces):
    za, zb, ya, yb = faces[:4]
    zb, za = swap_inner(zb, "gz"), swap(za, "gz", 0)
    yb, ya = swap_inner(yb, "gy"), swap(ya, "gy", 0)
    halos = [za, zb, ya, yb]
    return halos + [swap(face, "gx", first) for first, face in enumerate(faces[4:])]


def masked(halo, axis, first):
    index = lax.axis_index(axis)
    partner = index + 1 - 2 * lax.rem(index + first, 2)
    inside = jnp.logical_and(partner >= 0, partner < lax.axis_size(axis))
    return jnp.where(inside, halo, 0.0)


def true_order(pieces, axis):
    distance = 1
    while distance < pieces.shape[0]:
        swapped = pieces.reshape((-1, 2, distance) + pieces.shape[1:])[:, ::-1].reshape(pieces.shape)
        odd = lax.rem(lax.div(lax.axis_index(axis), distance), 2) == 1
        pieces = jnp.where(odd, swapped, pieces)
        distance *= 2
    return pieces


def shards(flow, positions, loads, block_list):
    capacity = block_list.shape[-1]
    steps, _, _, part = positions.shape
    shape = flow.shape[1:]
    count_x, count_z, count_y = shape
    size_x, size_y, size_z = lax.axis_size("gx"), lax.axis_size("gy"), lax.axis_size("gz")
    points = part * size_z
    lanes = capacity * points
    params = pltpu.CompilerParams(vmem_limit_bytes=vmem_limit)
    q = flow
    turbines = block_list.reshape(capacity)
    barrier = lax.optimization_barrier
    forms = face_shapes(shape)

    extra = pl.cdiv((3 * steps + 1) * pl.cdiv(capacity, 2), 8) * 8

    own = jnp.concatenate([positions.reshape(steps, 3, part), loads.reshape(steps, 3, part)], axis=1)
    table = jnp.pad(own, ((0, 0), (0, 2), (0, 0))).reshape(1, 8 * steps, part)
    table = jnp.concatenate([table, from_distance(table, "gz", 1)], axis=0)
    faces = pl.pallas_call(
        functools.partial(faces_body, shape=shape),
        out_shape=forms,
        in_specs=vmem_specs(1),
        out_specs=vmem_specs(len(forms)),
        compiler_params=params,
        name="faces",
    )(q)
    table, faces = barrier((table, list(faces)))
    za, zb, ya, yb = faces[:4]
    za = masked(swap(za, "gz", 0), "gz", 0)
    distance = 2
    while distance < size_z:
        received = from_distance(table, "gz", distance)
        received, za = barrier((received, za))
        table = jnp.concatenate([table, received], axis=0)
        distance *= 2
    table = true_order(table, "gz")
    table = jnp.concatenate([table[k] for k in range(size_z)], axis=1)
    rows = 8 * steps
    zb, ya, table = barrier((zb, ya, table))
    zb = masked(swap_inner(zb, "gz"), "gz", 1)
    ya = swap(jnp.concatenate([ya, table], axis=0), "gy", 0)
    ya, zb, yb = barrier((ya, zb, yb))
    table = jnp.concatenate([table, ya[count_z:]], axis=0).reshape(2, rows, points)
    table = gather_relative(table, "gy", 2)
    yb = swap_inner(yb, "gy")
    table, yb = barrier((table, yb))
    x_faces = [swap(face, "gx", first) for first, face in enumerate(faces[4:])]
    table = gather_relative(table[None], "gx").reshape(size_x * size_y, rows, points)
    halos = [za, zb, ya, yb] + x_faces

    samples = None
    for step in range(steps):
        last, packs = step == steps - 1, step == steps - 2
        shapes = [jax.ShapeDtypeStruct(q.shape, jnp.float32)]
        out_specs = vmem_specs(1)
        scratch = []
        if last:
            out_specs = [pl.BlockSpec(memory_space=pl.ANY)]
            scratch = [pltpu.VMEM(q.shape, jnp.float32), pltpu.SemaphoreType.DMA((count_x,))]
        else:
            shapes += face_shapes(shape, extra if packs else 0)
            if packs:
                scratch = [pltpu.VMEM((16, lanes), jnp.float32)]
            else:
                shapes += [jax.ShapeDtypeStruct((16, lanes), jnp.float32)]
            out_specs = vmem_specs(len(shapes))
        past = [] if step == 0 or last else [samples]
        results = pl.pallas_call(
            functools.partial(step_body, shape=shape, points=points, capacity=capacity, step=step, steps=steps),
            out_shape=shapes,
            in_specs=[pl.BlockSpec(memory_space=pltpu.SMEM)] + vmem_specs(2 + len(halos) + len(past)),
            out_specs=out_specs,
            scratch_shapes=scratch
            + [pltpu.VMEM((3,) + shape, jnp.float32), pltpu.VMEM((8, lanes), jnp.float32)]
            + [pltpu.VMEM((4, count_y // 128, count_x, 128), jnp.float32)] * 2
            + [pltpu.VMEM((count_z, 128), jnp.float32)] * 2
            + [pltpu.VMEM((4, count_z, count_y), jnp.float32)] * 2
            + [pltpu.VMEM((count_x, count_z, lanes), jnp.float32), pltpu.VMEM((count_y, 3 * lanes), jnp.bfloat16)]
            + ([] if last else [pltpu.VMEM((count_x, count_z, lanes), jnp.float32)])
            + ([] if last else [pltpu.VMEM((3 * count_y, lanes), jnp.bfloat16)])
            + ([pltpu.VMEM((3 * count_y, lanes), jnp.bfloat16)] if step == 0 else []),
            compiler_params=params,
            name="step",
        )(turbines, table, q, *halos, *past)
        q = results[0]
        if last:
            break
        faces = results[1 : 1 + len(forms)]
        if not packs:
            samples = results[-1]
            halos = swap_faces(faces)
            continue
        za, zb, ya, yb = faces[:4]
        za_in, zb_in = swap(za, "gz", 0), swap_inner(zb, "gz")
        sums = za[4 * count_x :] + za_in[4 * count_x :]
        pieces = jnp.concatenate([sums[:, h * 128 : h * 128 + 128] for h in range(2)], axis=0)
        pieces, ya, zb_in = barrier((pieces, ya, zb_in))
        ya_in = swap(jnp.concatenate([ya, pieces], axis=0), "gy", 0)
        x_faces = [swap(face, "gx", first) for first, face in enumerate(faces[4:])]
        pieces = jnp.concatenate([pieces, ya_in[count_z:]], axis=0).reshape(2, -1, points)
        pieces, yb, x_faces = barrier((pieces, yb, x_faces))
        pieces = gather_relative(pieces, "gy", 2).reshape(-1, points)
        yb_in = swap_inner(yb, "gy")
        pieces, yb_in = barrier((pieces, yb_in))
        halos = [za_in, zb_in, ya_in, yb_in] + x_faces

    distance = 2
    while distance < size_z:
        pieces = pieces + from_distance(pieces, "gz", distance)
        distance *= 2
    pieces, q = barrier((pieces, q))
    mine = lax.dynamic_slice_in_dim(pieces, lax.axis_index("gz") * part, part, axis=1)[None]
    mine = gather_relative(mine, "gx").reshape(size_x * size_y, 2, extra, part)
    holder = (lax.axis_index("gx") * size_y + lax.axis_index("gy") + 1).astype(jnp.float32)
    returned = 0.0
    for j in range(capacity):
        row = (j // 2) * (3 * steps + 1)
        values = mine[:, j % 2, row : row + 3 * steps]
        match = mine[:, j % 2, row + 3 * steps :][:, :1] == holder
        returned = returned + jnp.sum(jnp.where(match, values, 0.0), axis=0)
    return q, returned.reshape(positions.shape)


def solution(mesh):
    in_specs = (
        P(None, "gx", "gz", "gy"),
        P(None, None, ("gx", "gy"), "gz"),
        P(None, None, ("gx", "gy"), "gz"),
        P("gx", "gy", "gz", None),
    )
    out_specs = (P(None, "gx", "gz", "gy"), P(None, None, ("gx", "gy"), "gz"))
    return jax.shard_map(shards, mesh=mesh, in_specs=in_specs, out_specs=out_specs, check_vma=False)
```

```python
import functools
import math

import jax
import jax.numpy as jnp
from jax import lax
from jax.experimental import pallas as pl
from jax.experimental.pallas import tpu as pltpu
from jax.sharding import PartitionSpec as P

kernel_width = 2.0
kernel_norm = 1.0 / (math.pi**1.5 * kernel_width**3)
time_step = 0.1
smag_coef = 0.17
viscosity = 0.02
diffusivity = 0.02
prandtl = 0.4
vmem_limit = 24 << 20


def swap_pairs(count, first):
    pairs = []
    for low in range(first, count - 1, 2):
        pairs += [(low, low + 1), (low + 1, low)]
    return pairs


def swap(value, axis, first):
    pairs = swap_pairs(lax.axis_size(axis), first)
    if not pairs:
        return jnp.zeros_like(value)
    return lax.ppermute(value, axis, pairs)


def swap_inner(value, axis):
    size, chips = lax.axis_size(axis), lax.axis_size("gx")
    target = {low: high for low, high in swap_pairs(size, 1)}
    pairs = []
    for x in range(chips):
        for k in range(size):
            pairs.append((x * size + k, x * size + target[k] if k in target else (x ^ 1) * size + k))
    return lax.ppermute(value, ("gx", axis), pairs)


def from_distance(value, axis, distance):
    count = lax.axis_size(axis)
    return lax.ppermute(value, axis, [(i, i ^ distance) for i in range(count)])


def gather_relative(value, axis, distance=1):
    while distance < lax.axis_size(axis):
        value = jnp.concatenate([value, from_distance(value, axis, distance)], axis=0)
        distance *= 2
    return value


def pick(flag, first, second):
    return jnp.where(flag, first, second)


def is_even(axis):
    return lax.rem(lax.axis_index(axis), 2) == 0


def write_faces(q_ref, face_refs, shape):
    count_x, count_z, count_y = shape
    za_ref, zb_ref, ya_ref, yb_ref, xa_ref = face_refs[:5]
    even_x, even_z, even_y = is_even("gx"), is_even("gz"), is_even("gy")
    low, high = q_ref[:, 0], q_ref[:, count_x - 1]
    xa_ref[...] = pick(even_x, high, low)
    for xb_ref in face_refs[5:]:
        xb_ref[...] = pick(even_x, low, high)
    for comp in range(4):
        low = q_ref[comp, :, 0, :]
        high = q_ref[comp, :, count_z - 1, :]
        za_ref[comp * count_x : (comp + 1) * count_x] = pick(even_z, high, low)
        zb_ref[comp * count_x : (comp + 1) * count_x] = pick(even_z, low, high)
    lane = lax.broadcasted_iota(jnp.int32, (count_z, 128), 1)
    low = jnp.zeros((count_z, 128), jnp.float32)
    high = jnp.zeros((count_z, 128), jnp.float32)
    for comp in range(4):
        for x in range(count_x):
            place = comp * count_x + x
            first = q_ref[comp, x, :, :128]
            last = q_ref[comp, x, :, count_y - 128 :]
            low = jnp.where(lane == place, pltpu.roll(first, place, 1), low)
            high = jnp.where(lane == place, pltpu.roll(last, (place + 1) % 128, 1), high)
    ya_ref[...] = pick(even_y, high, low)
    yb_ref[...] = pick(even_y, low, high)


def faces_body(q_ref, *face_refs, shape):
    write_faces(q_ref, face_refs, shape)


def sorted_slots(list_ref, capacity):
    slots = [list_ref[j] for j in range(capacity)]
    for first in range(capacity):
        for second in range(first + 1, capacity):
            a, b = slots[first], slots[second]
            slots[first], slots[second] = jnp.minimum(a, b), jnp.maximum(a, b)
    return slots


def masks_of(shape):
    count_z = shape[1]
    sub = lax.broadcasted_iota(jnp.int32, (count_z, 128), 0)
    lane = lax.broadcasted_iota(jnp.int32, (count_z, 128), 1)
    return sub == 0, sub == count_z - 1, lane == 0, lane == 127


def tile_update(shifts, pushed):
    diffs, laplace, centre = [], [], []
    for c, minus_x, plus_x, minus_y, plus_y, minus_z, plus_z in shifts:
        diffs.append((plus_x - minus_x, plus_y - minus_y, plus_z - minus_z))
        laplace.append((plus_x + minus_x) + (plus_y + minus_y) + (plus_z + minus_z) - 6.0 * c)
        centre.append(c)
    diagonal = diffs[0][0] * diffs[0][0] + diffs[1][1] * diffs[1][1] + diffs[2][2] * diffs[2][2]
    xy = diffs[0][1] + diffs[1][0]
    xz = diffs[0][2] + diffs[2][0]
    yz = diffs[1][2] + diffs[2][1]
    total = (diagonal + diagonal) + (xy * xy + xz * xz + yz * yz)
    root = total * lax.rsqrt(jnp.maximum(total, 1.1754944e-38))
    scale_u = time_step * viscosity + (0.5 * time_step * smag_coef**2) * root
    scale_t = time_step * diffusivity + (0.5 * time_step * smag_coef**2 / prandtl) * root
    half = [0.5 * time_step * centre[a] for a in range(3)]
    out = []
    for comp in range(4):
        d = diffs[comp]
        moved = half[0] * d[0] + half[1] * d[1] + half[2] * d[2]
        value = centre[comp] - moved + (scale_u if comp < 3 else scale_t) * laplace[comp]
        out.append(value + pushed[comp] if comp < 3 else value)
    return out


def split(value):
    high = value.astype(jnp.bfloat16)
    low = (value - high.astype(jnp.float32)).astype(jnp.bfloat16)
    return high, low


def turbine_rows(rows_ref, table_ref, slots, step, points):
    size_x, size_y = lax.axis_size("gx"), lax.axis_size("gy")
    for j, slot in enumerate(slots):
        t = jnp.minimum(slot, size_x * size_y - 1)
        place_x = lax.bitwise_xor(lax.div(t, size_y), lax.axis_index("gx"))
        place_y = lax.bitwise_xor(lax.rem(t, size_y), lax.axis_index("gy"))
        entry = place_x * size_y + lax.bitwise_xor(place_y, lax.div(place_y, 2))
        rows_ref[:, j * points : (j + 1) * points] = table_ref[entry, 8 * step : 8 * step + 8, :]
    return rows_ref[...]


def point_factors(rows, listed, shape):
    lanes = rows.shape[1]

    def factor(row, axis, count):
        start = (lax.axis_index(axis) * count).astype(jnp.float32)
        cells = lax.broadcasted_iota(jnp.int32, (count, lanes), 0).astype(jnp.float32) + start
        gap = cells - row
        return jnp.exp(-(gap * gap) / kernel_width**2)

    count_x, count_z, count_y = shape
    factor_x = factor(rows[0:1], "gx", count_x)
    factor_y = factor(rows[1:2], "gy", count_y)
    factor_z = factor(rows[2:3], "gz", count_z) * jnp.where(listed, kernel_norm, 0.0)
    weights = (factor_x[:, None, :] * factor_z[None, :, :]).reshape(count_x * count_z, lanes)
    return weights, split(factor_y)


def store_factors(rows, listed, weight_ref, right_ref, shape, along_points):
    weights, (high, low) = point_factors(rows, listed, shape)
    weight_ref[...] = weights.reshape(weight_ref.shape)
    right_ref[...] = jnp.concatenate([high, high, low], axis=1 if along_points else 0)


def push(force_ref, rows, weight_ref, right_ref, start, planes, shape):
    count_z = shape[1]
    weights = weight_ref[start : start + planes].reshape(planes * count_z, -1)
    left = []
    for comp in range(3):
        first, second = split(weights * (rows[3 + comp : 4 + comp] * time_step))
        left.append(jnp.concatenate([first, second, first], axis=1))
    left = jnp.concatenate(left, axis=0)
    pushed = lax.dot_general(left, right_ref[...], (((1,), (1,)), ((), ())), preferred_element_type=jnp.float32)
    force_ref[:, start : start + planes] = pushed.reshape((3, planes) + shape[1:])


def sample(q_ref, weight_ref, right_ref, start, planes, shape):
    count_z = shape[1]
    left = []
    for comp in range(3):
        first, second = split(q_ref[comp, start : start + planes].reshape(planes * count_z, -1))
        left.append(jnp.concatenate([first, second, first], axis=1))
    along = jnp.dot(jnp.concatenate(left, axis=0), right_ref[...], preferred_element_type=jnp.float32)
    weights = weight_ref[start : start + planes].reshape(planes * count_z, -1)
    rows = planes * count_z
    return [jnp.sum(along[k * rows : (k + 1) * rows] * weights, axis=0, keepdims=True) for k in range(3)]


def step_body(*refs, shape, points, capacity, step, steps):
    count_x, count_z, count_y = shape
    last, packs = step == steps - 1, step == steps - 2
    faces = len(face_shapes(shape))
    refs = list(refs)
    list_ref, table_ref, q_ref = refs[:3]
    za_ref, zb_ref, ya_ref, yb_ref = refs[3:7]
    x_refs, refs = refs[7 : 3 + faces], refs[3 + faces :]
    past_ref = None if step == 0 or last else refs.pop(0)
    out_ref = refs.pop(0)
    sample_ref = None
    if not last:
        face_refs, refs = refs[:faces], refs[faces:]
        sample_ref = refs.pop(0)
    else:
        far_ref, out_ref, sems = out_ref, refs.pop(0), refs.pop(0)
    force_ref, rows_ref, low_z_ref, high_z_ref, low_y_ref, high_y_ref, low_x_ref, high_x_ref = refs[:8]
    weight_ref, push_right_ref = refs[8:10]
    if not last:
        next_weight_ref, sample_right_ref = refs[10:12]
    if step == 0:
        first_right_ref = refs[12]
    slots = sorted_slots(list_ref, capacity)
    turbines = lax.axis_size("gx") * lax.axis_size("gy")
    listed = slots[0] < turbines

    if not last:
        sample_ref[...] = jnp.zeros(sample_ref.shape, jnp.float32)
        if past_ref is not None:
            sample_ref[: 3 * step + 3] = past_ref[: 3 * step + 3]

    if not last:
        rows = turbine_rows(rows_ref, table_ref, slots, step + 1, points)
        store_factors(rows, listed, next_weight_ref, sample_right_ref, shape, False)
    rows = turbine_rows(rows_ref, table_ref, slots, step, points)
    store_factors(rows, listed, weight_ref, push_right_ref, shape, True)
    if step == 0:
        high, low = point_factors(rows, listed, shape)[1]
        first_right_ref[...] = jnp.concatenate([high, high, low], axis=0)

    even_x, even_z, even_y = is_even("gx"), is_even("gz"), is_even("gy")
    index_y, index_z = lax.axis_index("gy"), lax.axis_index("gz")
    tiles = count_y // 128
    for comp in range(4):
        for tile in range(tiles):
            there = slice(comp * count_x, (comp + 1) * count_x), slice(tile * 128, tile * 128 + 128)
            first, second = za_ref[there], zb_ref[there]
            low_z_ref[comp, tile] = pick(index_z == 0, 0.0, pick(even_z, second, first))
            high_z_ref[comp, tile] = pick(index_z == lax.axis_size("gz") - 1, 0.0, pick(even_z, first, second))
    low_y_ref[...] = pick(index_y == 0, 0.0, pick(even_y, yb_ref[:count_z], ya_ref[:count_z]))
    high_y_ref[...] = pick(index_y == lax.axis_size("gy") - 1, 0.0, pick(even_y, ya_ref[:count_z], yb_ref[:count_z]))
    first = x_refs[0][...]
    second = x_refs[1][...] if len(x_refs) > 1 else 0.0
    low_x_ref[...] = pick(even_x, second, first)
    high_x_ref[...] = pick(even_x, first, second)
    first_z, last_z, first_y, last_y = masks_of(shape)

    def plane(x, minus, plus):
        centre, up, down = [], [], []
        for comp in range(4):
            row = [q_ref[comp, x, :, tile * 128 : tile * 128 + 128] for tile in range(tiles)]
            place = comp * count_x + x
            turn = (128 - place) % 128 if isinstance(place, int) else 128 - place
            centre.append(row)
            up.append([pltpu.roll(low_y_ref[...], turn, 1)] + [pltpu.roll(c, 1, 1) for c in row])
            down.append([pltpu.roll(c, 127, 1) for c in row] + [pltpu.roll(high_y_ref[...], 127 - place, 1)])
        for tile in range(tiles):
            here = slice(tile * 128, tile * 128 + 128)
            shifts = []
            for comp in range(4):
                c = centre[comp][tile]
                minus_y = jnp.where(first_y, up[comp][tile], up[comp][tile + 1])
                plus_y = jnp.where(last_y, down[comp][tile + 1], down[comp][tile])
                low_z = low_z_ref[comp, tile, pl.ds(x, 1), :]
                high_z = high_z_ref[comp, tile, pl.ds(x, 1), :]
                minus_z = jnp.where(first_z, low_z, pltpu.roll(c, 1, 0))
                plus_z = jnp.where(last_z, high_z, pltpu.roll(c, count_z - 1, 0))
                shifts.append((c, minus(comp, here), plus(comp, here), minus_y, plus_y, minus_z, plus_z))
            pushed = [force_ref[comp, x, :, here] for comp in range(3)]
            for comp, value in enumerate(tile_update(shifts, pushed)):
                out_ref[comp, x, :, here] = value

    def of_plane(x):
        return lambda comp, here: q_ref[comp, x, :, here]

    def copy_out(number, start, count):
        here = pl.ds(start, count)
        return pltpu.make_async_copy(out_ref.at[:, here], far_ref.at[:, here], sems.at[number])

    group = max(g for g in range(1, 9) if count_x % g == 0)
    groups = count_x // group
    sums = [0.0] * 3
    first_sums = [0.0] * 3
    push(force_ref, rows, weight_ref, push_right_ref, 0, group, shape)
    for number in range(groups):
        start = number * group
        if number + 1 < groups:
            push(force_ref, rows, weight_ref, push_right_ref, start + group, group, shape)
        if step == 0:
            more = sample(q_ref, weight_ref, first_right_ref, start, group, shape)
            first_sums = [a + b for a, b in zip(first_sums, more)]
        for x in range(start, start + group):
            minus = of_plane(x - 1) if x else lambda comp, here: low_x_ref[comp, :, here]
            plus = of_plane(x + 1) if x < count_x - 1 else lambda comp, here: high_x_ref[comp, :, here]
            plane(x, minus, plus)
        if last:
            copy_out(number, start, group).start()
        elif number:
            more = sample(out_ref, next_weight_ref, sample_right_ref, start - group, group, shape)
            sums = [a + b for a, b in zip(sums, more)]
    if last:
        for number in range(groups):
            copy_out(number, number * group, group).wait()
        return
    more = sample(out_ref, next_weight_ref, sample_right_ref, count_x - group, group, shape)
    for comp in range(3):
        sample_ref[3 * step + 3 + comp : 3 * step + 4 + comp] = sums[comp] + more[comp]
        if step == 0:
            sample_ref[comp : comp + 1] = first_sums[comp]
    write_faces(out_ref, face_refs, shape)

    if packs:
        count = 3 * steps + 1
        za_ref = face_refs[0]
        start = 4 * count_x
        za_ref[start:] = jnp.zeros((za_ref.shape[0] - start, count_y), jnp.float32)
        for j, slot in enumerate(slots):
            lane, row = (j % 2) * points, start + (j // 2) * count
            values = sample_ref[: count - 1, j * points : (j + 1) * points]
            za_ref[row : row + count - 1, lane : lane + points] = values
            name = jnp.where(listed, 0.5 * (slot + 1).astype(jnp.float32), 0.0)
            za_ref[row + count - 1 : row + count, lane : lane + points] = jnp.full((1, points), name)


def face_shapes(shape, extra=0):
    count_x, count_z, count_y = shape
    forms = [(4 * count_x + extra, count_y), (4 * count_x, count_y)]
    forms += [(count_z, 128)] * 2 + [(4, count_z, count_y)] * (1 if lax.axis_size("gx") == 2 else 2)
    return [jax.ShapeDtypeStruct(form, jnp.float32) for form in forms]


def vmem_specs(count):
    return [pl.BlockSpec(memory_space=pltpu.VMEM)] * count


def swap_faces(faces):
    za, zb, ya, yb = faces[:4]
    zb, za = swap_inner(zb, "gz"), swap(za, "gz", 0)
    yb, ya = swap_inner(yb, "gy"), swap(ya, "gy", 0)
    halos = [za, zb, ya, yb]
    return halos + [swap(face, "gx", first) for first, face in enumerate(faces[4:])]


def masked(halo, axis, first):
    index = lax.axis_index(axis)
    partner = index + 1 - 2 * lax.rem(index + first, 2)
    inside = jnp.logical_and(partner >= 0, partner < lax.axis_size(axis))
    return jnp.where(inside, halo, 0.0)


def true_order(pieces, axis):
    distance = 1
    while distance < pieces.shape[0]:
        swapped = pieces.reshape((-1, 2, distance) + pieces.shape[1:])[:, ::-1].reshape(pieces.shape)
        odd = lax.rem(lax.div(lax.axis_index(axis), distance), 2) == 1
        pieces = jnp.where(odd, swapped, pieces)
        distance *= 2
    return pieces


def shards(flow, positions, loads, block_list):
    capacity = block_list.shape[-1]
    steps, _, _, part = positions.shape
    shape = flow.shape[1:]
    count_x, count_z, count_y = shape
    size_x, size_y, size_z = lax.axis_size("gx"), lax.axis_size("gy"), lax.axis_size("gz")
    points = part * size_z
    lanes = capacity * points
    params = pltpu.CompilerParams(vmem_limit_bytes=vmem_limit)
    q = flow
    turbines = block_list.reshape(capacity)
    barrier = lax.optimization_barrier
    forms = face_shapes(shape)

    extra = pl.cdiv((3 * steps + 1) * pl.cdiv(capacity, 2), 8) * 8

    own = jnp.concatenate([positions.reshape(steps, 3, part), loads.reshape(steps, 3, part)], axis=1)
    table = jnp.pad(own, ((0, 0), (0, 2), (0, 0))).reshape(1, 8 * steps, part)
    table = jnp.concatenate([table, from_distance(table, "gz", 1)], axis=0)
    faces = pl.pallas_call(
        functools.partial(faces_body, shape=shape),
        out_shape=forms,
        in_specs=vmem_specs(1),
        out_specs=vmem_specs(len(forms)),
        compiler_params=params,
        name="faces",
    )(q)
    table, faces = barrier((table, list(faces)))
    za, zb, ya, yb = faces[:4]
    za = masked(swap(za, "gz", 0), "gz", 0)
    distance = 2
    while distance < size_z:
        received = from_distance(table, "gz", distance)
        received, za = barrier((received, za))
        table = jnp.concatenate([table, received], axis=0)
        distance *= 2
    table = true_order(table, "gz")
    table = jnp.concatenate([table[k] for k in range(size_z)], axis=1)
    rows = 8 * steps
    zb, ya, table = barrier((zb, ya, table))
    zb = masked(swap_inner(zb, "gz"), "gz", 1)
    ya = swap(jnp.concatenate([ya, table], axis=0), "gy", 0)
    ya, zb = barrier((ya, zb))
    table = jnp.concatenate([table, ya[count_z:]], axis=0)
    yb = from_distance(jnp.concatenate([yb, table], axis=0), "gy", 3)
    x_faces = [swap(face, "gx", first) for first, face in enumerate(faces[4:])]
    table = jnp.concatenate([table, yb[count_z:]], axis=0)
    table = gather_relative(table[None], "gx").reshape(size_x * size_y, rows, points)
    halos = [za, zb, ya, yb] + x_faces

    samples = None
    for step in range(steps):
        last, packs = step == steps - 1, step == steps - 2
        shapes = [jax.ShapeDtypeStruct(q.shape, jnp.float32)]
        out_specs = vmem_specs(1)
        scratch = []
        if last:
            out_specs = [pl.BlockSpec(memory_space=pl.ANY)]
            scratch = [pltpu.VMEM(q.shape, jnp.float32), pltpu.SemaphoreType.DMA((count_x,))]
        else:
            shapes += face_shapes(shape, extra if packs else 0)
            if packs:
                scratch = [pltpu.VMEM((16, lanes), jnp.float32)]
            else:
                shapes += [jax.ShapeDtypeStruct((16, lanes), jnp.float32)]
            out_specs = vmem_specs(len(shapes))
        past = [] if step == 0 or last else [samples]
        results = pl.pallas_call(
            functools.partial(step_body, shape=shape, points=points, capacity=capacity, step=step, steps=steps),
            out_shape=shapes,
            in_specs=[pl.BlockSpec(memory_space=pltpu.SMEM)] + vmem_specs(2 + len(halos) + len(past)),
            out_specs=out_specs,
            scratch_shapes=scratch
            + [pltpu.VMEM((3,) + shape, jnp.float32), pltpu.VMEM((8, lanes), jnp.float32)]
            + [pltpu.VMEM((4, count_y // 128, count_x, 128), jnp.float32)] * 2
            + [pltpu.VMEM((count_z, 128), jnp.float32)] * 2
            + [pltpu.VMEM((4, count_z, count_y), jnp.float32)] * 2
            + [pltpu.VMEM((count_x, count_z, lanes), jnp.float32), pltpu.VMEM((count_y, 3 * lanes), jnp.bfloat16)]
            + ([] if last else [pltpu.VMEM((count_x, count_z, lanes), jnp.float32)])
            + ([] if last else [pltpu.VMEM((3 * count_y, lanes), jnp.bfloat16)])
            + ([pltpu.VMEM((3 * count_y, lanes), jnp.bfloat16)] if step == 0 else []),
            compiler_params=params,
            name="step",
        )(turbines, table, q, *halos, *past)
        q = results[0]
        if last:
            break
        faces = results[1 : 1 + len(forms)]
        if not packs:
            samples = results[-1]
            halos = swap_faces(faces)
            continue
        za, zb, ya, yb = faces[:4]
        za_in, zb_in = swap(za, "gz", 0), swap_inner(zb, "gz")
        sums = za[4 * count_x :] + za_in[4 * count_x :]
        pieces = jnp.concatenate([sums[:, h * 128 : h * 128 + 128] for h in range(2)], axis=0)
        pieces, ya, zb_in = barrier((pieces, ya, zb_in))
        ya_in = swap(jnp.concatenate([ya, pieces], axis=0), "gy", 0)
        x_faces = [swap(face, "gx", first) for first, face in enumerate(faces[4:])]
        pieces = jnp.concatenate([pieces, ya_in[count_z:]], axis=0).reshape(2, -1, points)
        pieces, yb, x_faces = barrier((pieces, yb, x_faces))
        pieces = gather_relative(pieces, "gy", 2).reshape(-1, points)
        yb_in = swap_inner(yb, "gy")
        pieces, yb_in = barrier((pieces, yb_in))
        halos = [za_in, zb_in, ya_in, yb_in] + x_faces

    distance = 2
    while distance < size_z:
        pieces = pieces + from_distance(pieces, "gz", distance)
        distance *= 2
    pieces, q = barrier((pieces, q))
    mine = lax.dynamic_slice_in_dim(pieces, lax.axis_index("gz") * part, part, axis=1)[None]
    mine = gather_relative(mine, "gx").reshape(size_x * size_y, 2, extra, part)
    holder = (lax.axis_index("gx") * size_y + lax.axis_index("gy") + 1).astype(jnp.float32)
    returned = 0.0
    for j in range(capacity):
        row = (j // 2) * (3 * steps + 1)
        values = mine[:, j % 2, row : row + 3 * steps]
        match = mine[:, j % 2, row + 3 * steps :][:, :1] == holder
        returned = returned + jnp.sum(jnp.where(match, values, 0.0), axis=0)
    return q, returned.reshape(positions.shape)


def solution(mesh):
    in_specs = (
        P(None, "gx", "gz", "gy"),
        P(None, None, ("gx", "gy"), "gz"),
        P(None, None, ("gx", "gy"), "gz"),
        P("gx", "gy", "gz", None),
    )
    out_specs = (P(None, "gx", "gz", "gy"), P(None, None, ("gx", "gy"), "gz"))
    return jax.shard_map(shards, mesh=mesh, in_specs=in_specs, out_specs=out_specs, check_vma=False)
```

```python
import functools
import math

import jax
import jax.numpy as jnp
from jax import lax
from jax.experimental import pallas as pl
from jax.experimental.pallas import tpu as pltpu
from jax.sharding import PartitionSpec as P

kernel_width = 2.0
kernel_norm = 1.0 / (math.pi**1.5 * kernel_width**3)
time_step = 0.1
smag_coef = 0.17
viscosity = 0.02
diffusivity = 0.02
prandtl = 0.4
vmem_limit = 24 << 20


def swap_pairs(count, first):
    pairs = []
    for low in range(first, count - 1, 2):
        pairs += [(low, low + 1), (low + 1, low)]
    return pairs


def swap(value, axis, first):
    pairs = swap_pairs(lax.axis_size(axis), first)
    if not pairs:
        return jnp.zeros_like(value)
    return lax.ppermute(value, axis, pairs)


def swap_inner(value, axis):
    size, chips = lax.axis_size(axis), lax.axis_size("gx")
    target = {low: high for low, high in swap_pairs(size, 1)}
    pairs = []
    for x in range(chips):
        for k in range(size):
            pairs.append((x * size + k, x * size + target[k] if k in target else (x ^ 1) * size + k))
    return lax.ppermute(value, ("gx", axis), pairs)


def from_distance(value, axis, distance):
    count = lax.axis_size(axis)
    return lax.ppermute(value, axis, [(i, i ^ distance) for i in range(count)])


def gather_relative(value, axis, distance=1):
    while distance < lax.axis_size(axis):
        value = jnp.concatenate([value, from_distance(value, axis, distance)], axis=0)
        distance *= 2
    return value


def pick(flag, first, second):
    return jnp.where(flag, first, second)


def is_even(axis):
    return lax.rem(lax.axis_index(axis), 2) == 0


def write_faces(q_ref, face_refs, shape):
    count_x, count_z, count_y = shape
    za_ref, zb_ref, ya_ref, yb_ref, xa_ref = face_refs[:5]
    even_x, even_z, even_y = is_even("gx"), is_even("gz"), is_even("gy")
    low, high = q_ref[:, 0], q_ref[:, count_x - 1]
    xa_ref[...] = pick(even_x, high, low)
    for xb_ref in face_refs[5:]:
        xb_ref[...] = pick(even_x, low, high)
    for comp in range(4):
        low = q_ref[comp, :, 0, :]
        high = q_ref[comp, :, count_z - 1, :]
        za_ref[comp * count_x : (comp + 1) * count_x] = pick(even_z, high, low)
        zb_ref[comp * count_x : (comp + 1) * count_x] = pick(even_z, low, high)
    lane = lax.broadcasted_iota(jnp.int32, (count_z, 128), 1)
    low = jnp.zeros((count_z, 128), jnp.float32)
    high = jnp.zeros((count_z, 128), jnp.float32)
    for comp in range(4):
        for x in range(count_x):
            place = comp * count_x + x
            first = q_ref[comp, x, :, :128]
            last = q_ref[comp, x, :, count_y - 128 :]
            low = jnp.where(lane == place, pltpu.roll(first, place, 1), low)
            high = jnp.where(lane == place, pltpu.roll(last, (place + 1) % 128, 1), high)
    ya_ref[...] = pick(even_y, high, low)
    yb_ref[...] = pick(even_y, low, high)


def faces_body(q_ref, *face_refs, shape):
    write_faces(q_ref, face_refs, shape)


def sorted_slots(list_ref, capacity):
    slots = [list_ref[j] for j in range(capacity)]
    for first in range(capacity):
        for second in range(first + 1, capacity):
            a, b = slots[first], slots[second]
            slots[first], slots[second] = jnp.minimum(a, b), jnp.maximum(a, b)
    return slots


def masks_of(shape):
    count_z = shape[1]
    sub = lax.broadcasted_iota(jnp.int32, (count_z, 128), 0)
    lane = lax.broadcasted_iota(jnp.int32, (count_z, 128), 1)
    return sub == 0, sub == count_z - 1, lane == 0, lane == 127


def tile_update(shifts, pushed):
    diffs, laplace, centre = [], [], []
    for c, minus_x, plus_x, minus_y, plus_y, minus_z, plus_z in shifts:
        diffs.append((plus_x - minus_x, plus_y - minus_y, plus_z - minus_z))
        laplace.append((plus_x + minus_x) + (plus_y + minus_y) + (plus_z + minus_z) - 6.0 * c)
        centre.append(c)
    diagonal = diffs[0][0] * diffs[0][0] + diffs[1][1] * diffs[1][1] + diffs[2][2] * diffs[2][2]
    xy = diffs[0][1] + diffs[1][0]
    xz = diffs[0][2] + diffs[2][0]
    yz = diffs[1][2] + diffs[2][1]
    total = (diagonal + diagonal) + (xy * xy + xz * xz + yz * yz)
    root = total * lax.rsqrt(jnp.maximum(total, 1.1754944e-38))
    scale_u = time_step * viscosity + (0.5 * time_step * smag_coef**2) * root
    scale_t = time_step * diffusivity + (0.5 * time_step * smag_coef**2 / prandtl) * root
    half = [0.5 * time_step * centre[a] for a in range(3)]
    out = []
    for comp in range(4):
        d = diffs[comp]
        moved = half[0] * d[0] + half[1] * d[1] + half[2] * d[2]
        value = centre[comp] - moved + (scale_u if comp < 3 else scale_t) * laplace[comp]
        out.append(value + pushed[comp] if comp < 3 else value)
    return out


def split(value):
    high = value.astype(jnp.bfloat16)
    low = (value - high.astype(jnp.float32)).astype(jnp.bfloat16)
    return high, low


def turbine_rows(rows_ref, table_ref, slots, step, points):
    size_x, size_y = lax.axis_size("gx"), lax.axis_size("gy")
    for j, slot in enumerate(slots):
        t = jnp.minimum(slot, size_x * size_y - 1)
        place_x = lax.bitwise_xor(lax.div(t, size_y), lax.axis_index("gx"))
        place_y = lax.bitwise_xor(lax.rem(t, size_y), lax.axis_index("gy"))
        entry = place_x * size_y + lax.bitwise_xor(place_y, lax.div(place_y, 2))
        rows_ref[:, j * points : (j + 1) * points] = table_ref[entry, 8 * step : 8 * step + 8, :]
    return rows_ref[...]


def point_factors(rows, listed, shape):
    lanes = rows.shape[1]

    def factor(row, axis, count):
        start = (lax.axis_index(axis) * count).astype(jnp.float32)
        cells = lax.broadcasted_iota(jnp.int32, (count, lanes), 0).astype(jnp.float32) + start
        gap = cells - row
        return jnp.exp(-(gap * gap) / kernel_width**2)

    count_x, count_z, count_y = shape
    factor_x = factor(rows[0:1], "gx", count_x)
    factor_y = factor(rows[1:2], "gy", count_y)
    factor_z = factor(rows[2:3], "gz", count_z) * jnp.where(listed, kernel_norm, 0.0)
    weights = (factor_x[:, None, :] * factor_z[None, :, :]).reshape(count_x * count_z, lanes)
    return weights, split(factor_y)


def store_factors(rows, listed, weight_ref, right_refs, shape):
    weights, (high, low) = point_factors(rows, listed, shape)
    weight_ref[...] = weights.reshape(weight_ref.shape)
    for axis, right_ref in right_refs.items():
        right_ref[...] = jnp.concatenate([high, high, low], axis=axis)


def push(force_ref, rows, weight_ref, right_ref, start, planes, shape):
    count_z = shape[1]
    weights = weight_ref[start : start + planes].reshape(planes * count_z, -1)
    left = []
    for comp in range(3):
        first, second = split(weights * (rows[3 + comp : 4 + comp] * time_step))
        left.append(jnp.concatenate([first, second, first], axis=1))
    left = jnp.concatenate(left, axis=0)
    pushed = lax.dot_general(left, right_ref[...], (((1,), (1,)), ((), ())), preferred_element_type=jnp.float32)
    force_ref[:, start : start + planes] = pushed.reshape((3, planes) + shape[1:])


def sample(q_ref, weight_ref, right_ref, start, planes, shape):
    count_z = shape[1]
    left = []
    for comp in range(3):
        first, second = split(q_ref[comp, start : start + planes].reshape(planes * count_z, -1))
        left.append(jnp.concatenate([first, second, first], axis=1))
    along = jnp.dot(jnp.concatenate(left, axis=0), right_ref[...], preferred_element_type=jnp.float32)
    weights = weight_ref[start : start + planes].reshape(planes * count_z, -1)
    rows = planes * count_z
    return [jnp.sum(along[k * rows : (k + 1) * rows] * weights, axis=0, keepdims=True) for k in range(3)]


def step_body(*refs, shape, points, capacity, step, steps):
    count_x, count_z, count_y = shape
    last, packs = step == steps - 1, step == steps - 2
    faces = len(face_shapes(shape))
    refs = list(refs)
    list_ref, table_ref, q_ref = refs[:3]
    za_ref, zb_ref, ya_ref, yb_ref = refs[3:7]
    x_refs, refs = refs[7 : 3 + faces], refs[3 + faces :]
    past_ref = None if step == 0 or last else refs.pop(0)
    out_ref = refs.pop(0)
    sample_ref = None
    if not last:
        face_refs, refs = refs[:faces], refs[faces:]
        sample_ref = refs.pop(0)
    else:
        far_ref, out_ref, sems = out_ref, refs.pop(0), refs.pop(0)
    force_ref, rows_ref, low_z_ref, high_z_ref, low_y_ref, high_y_ref, low_x_ref, high_x_ref = refs[:8]
    weight_ref, push_right_ref = refs[8:10]
    if not last:
        next_weight_ref, sample_right_ref = refs[10:12]
    if step == 0:
        first_right_ref = refs[12]
    slots = sorted_slots(list_ref, capacity)
    turbines = lax.axis_size("gx") * lax.axis_size("gy")
    listed = slots[0] < turbines

    if not last:
        sample_ref[...] = jnp.zeros(sample_ref.shape, jnp.float32)
        if past_ref is not None:
            sample_ref[: 3 * step + 3] = past_ref[: 3 * step + 3]

    rows = turbine_rows(rows_ref, table_ref, slots, step, points)
    store_factors(rows, listed, weight_ref, {1: push_right_ref, 0: first_right_ref} if step == 0 else {1: push_right_ref}, shape)

    even_x, even_z, even_y = is_even("gx"), is_even("gz"), is_even("gy")
    index_y, index_z = lax.axis_index("gy"), lax.axis_index("gz")
    tiles = count_y // 128
    for comp in range(4):
        for tile in range(tiles):
            there = slice(comp * count_x, (comp + 1) * count_x), slice(tile * 128, tile * 128 + 128)
            first, second = za_ref[there], zb_ref[there]
            low_z_ref[comp, tile] = pick(index_z == 0, 0.0, pick(even_z, second, first))
            high_z_ref[comp, tile] = pick(index_z == lax.axis_size("gz") - 1, 0.0, pick(even_z, first, second))
    low_y_ref[...] = pick(index_y == 0, 0.0, pick(even_y, yb_ref[:count_z], ya_ref[:count_z]))
    high_y_ref[...] = pick(index_y == lax.axis_size("gy") - 1, 0.0, pick(even_y, ya_ref[:count_z], yb_ref[:count_z]))
    first = x_refs[0][...]
    second = x_refs[1][...] if len(x_refs) > 1 else 0.0
    low_x_ref[...] = pick(even_x, second, first)
    high_x_ref[...] = pick(even_x, first, second)
    first_z, last_z, first_y, last_y = masks_of(shape)

    def plane(x, minus, plus):
        centre, up, down = [], [], []
        for comp in range(4):
            row = [q_ref[comp, x, :, tile * 128 : tile * 128 + 128] for tile in range(tiles)]
            place = comp * count_x + x
            turn = (128 - place) % 128 if isinstance(place, int) else 128 - place
            centre.append(row)
            up.append([pltpu.roll(low_y_ref[...], turn, 1)] + [pltpu.roll(c, 1, 1) for c in row])
            down.append([pltpu.roll(c, 127, 1) for c in row] + [pltpu.roll(high_y_ref[...], 127 - place, 1)])
        for tile in range(tiles):
            here = slice(tile * 128, tile * 128 + 128)
            shifts = []
            for comp in range(4):
                c = centre[comp][tile]
                minus_y = jnp.where(first_y, up[comp][tile], up[comp][tile + 1])
                plus_y = jnp.where(last_y, down[comp][tile + 1], down[comp][tile])
                low_z = low_z_ref[comp, tile, pl.ds(x, 1), :]
                high_z = high_z_ref[comp, tile, pl.ds(x, 1), :]
                minus_z = jnp.where(first_z, low_z, pltpu.roll(c, 1, 0))
                plus_z = jnp.where(last_z, high_z, pltpu.roll(c, count_z - 1, 0))
                shifts.append((c, minus(comp, here), plus(comp, here), minus_y, plus_y, minus_z, plus_z))
            pushed = [force_ref[comp, x, :, here] for comp in range(3)]
            for comp, value in enumerate(tile_update(shifts, pushed)):
                out_ref[comp, x, :, here] = value

    def of_plane(x):
        return lambda comp, here: q_ref[comp, x, :, here]

    def copy_out(number, start, count):
        here = pl.ds(start, count)
        return pltpu.make_async_copy(out_ref.at[:, here], far_ref.at[:, here], sems.at[number])

    group = max(g for g in range(1, 9) if count_x % g == 0)
    groups = count_x // group
    sums = [0.0] * 3
    first_sums = [0.0] * 3
    push(force_ref, rows, weight_ref, push_right_ref, 0, group, shape)
    for number in range(groups):
        start = number * group
        if number + 1 < groups:
            push(force_ref, rows, weight_ref, push_right_ref, start + group, group, shape)
        if step == 0:
            more = sample(q_ref, weight_ref, first_right_ref, start, group, shape)
            first_sums = [a + b for a, b in zip(first_sums, more)]
        for x in range(start, start + group):
            minus = of_plane(x - 1) if x else lambda comp, here: low_x_ref[comp, :, here]
            plus = of_plane(x + 1) if x < count_x - 1 else lambda comp, here: high_x_ref[comp, :, here]
            plane(x, minus, plus)
        if not last and not number:
            next_rows = turbine_rows(rows_ref, table_ref, slots, step + 1, points)
            store_factors(next_rows, listed, next_weight_ref, {0: sample_right_ref}, shape)
        if last:
            copy_out(number, start, group).start()
        elif number:
            more = sample(out_ref, next_weight_ref, sample_right_ref, start - group, group, shape)
            sums = [a + b for a, b in zip(sums, more)]
    if last:
        for number in range(groups):
            copy_out(number, number * group, group).wait()
        return
    write_faces(out_ref, face_refs, shape)
    more = sample(out_ref, next_weight_ref, sample_right_ref, count_x - group, group, shape)
    for comp in range(3):
        sample_ref[3 * step + 3 + comp : 3 * step + 4 + comp] = sums[comp] + more[comp]
        if step == 0:
            sample_ref[comp : comp + 1] = first_sums[comp]

    if packs:
        count = 3 * steps + 1
        za_ref = face_refs[0]
        start = 4 * count_x
        za_ref[start:] = jnp.zeros((za_ref.shape[0] - start, count_y), jnp.float32)
        for j, slot in enumerate(slots):
            lane, row = (j % 2) * points, start + (j // 2) * count
            values = sample_ref[: count - 1, j * points : (j + 1) * points]
            za_ref[row : row + count - 1, lane : lane + points] = values
            name = jnp.where(listed, 0.5 * (slot + 1).astype(jnp.float32), 0.0)
            za_ref[row + count - 1 : row + count, lane : lane + points] = jnp.full((1, points), name)


def face_shapes(shape, extra=0):
    count_x, count_z, count_y = shape
    forms = [(4 * count_x + extra, count_y), (4 * count_x, count_y)]
    forms += [(count_z, 128)] * 2 + [(4, count_z, count_y)] * (1 if lax.axis_size("gx") == 2 else 2)
    return [jax.ShapeDtypeStruct(form, jnp.float32) for form in forms]


def vmem_specs(count):
    return [pl.BlockSpec(memory_space=pltpu.VMEM)] * count


def swap_faces(faces):
    za, zb, ya, yb = faces[:4]
    zb, za = swap_inner(zb, "gz"), swap(za, "gz", 0)
    yb, ya = swap_inner(yb, "gy"), swap(ya, "gy", 0)
    halos = [za, zb, ya, yb]
    return halos + [swap(face, "gx", first) for first, face in enumerate(faces[4:])]


def masked(halo, axis, first):
    index = lax.axis_index(axis)
    partner = index + 1 - 2 * lax.rem(index + first, 2)
    inside = jnp.logical_and(partner >= 0, partner < lax.axis_size(axis))
    return jnp.where(inside, halo, 0.0)


def true_order(pieces, axis):
    distance = 1
    while distance < pieces.shape[0]:
        swapped = pieces.reshape((-1, 2, distance) + pieces.shape[1:])[:, ::-1].reshape(pieces.shape)
        odd = lax.rem(lax.div(lax.axis_index(axis), distance), 2) == 1
        pieces = jnp.where(odd, swapped, pieces)
        distance *= 2
    return pieces


def shards(flow, positions, loads, block_list):
    capacity = block_list.shape[-1]
    steps, _, _, part = positions.shape
    shape = flow.shape[1:]
    count_x, count_z, count_y = shape
    size_x, size_y, size_z = lax.axis_size("gx"), lax.axis_size("gy"), lax.axis_size("gz")
    points = part * size_z
    lanes = capacity * points
    params = pltpu.CompilerParams(vmem_limit_bytes=vmem_limit)
    q = flow
    turbines = block_list.reshape(capacity)
    barrier = lax.optimization_barrier
    forms = face_shapes(shape)

    extra = pl.cdiv((3 * steps + 1) * pl.cdiv(capacity, 2), 8) * 8

    own = jnp.concatenate([positions.reshape(steps, 3, part), loads.reshape(steps, 3, part)], axis=1)
    table = jnp.pad(own, ((0, 0), (0, 2), (0, 0))).reshape(1, 8 * steps, part)
    table = jnp.concatenate([table, from_distance(table, "gz", 1)], axis=0)
    faces = pl.pallas_call(
        functools.partial(faces_body, shape=shape),
        out_shape=forms,
        in_specs=vmem_specs(1),
        out_specs=vmem_specs(len(forms)),
        compiler_params=params,
        name="faces",
    )(q)
    table, faces = barrier((table, list(faces)))
    za, zb, ya, yb = faces[:4]
    za = masked(swap(za, "gz", 0), "gz", 0)
    distance = 2
    while distance < size_z:
        received = from_distance(table, "gz", distance)
        received, za = barrier((received, za))
        table = jnp.concatenate([table, received], axis=0)
        distance *= 2
    table = true_order(table, "gz")
    table = jnp.concatenate([table[k] for k in range(size_z)], axis=1)
    rows = 8 * steps
    zb, ya, table = barrier((zb, ya, table))
    zb = masked(swap_inner(zb, "gz"), "gz", 1)
    ya = swap(jnp.concatenate([ya, table], axis=0), "gy", 0)
    ya, zb = barrier((ya, zb))
    table = jnp.concatenate([table, ya[count_z:]], axis=0)
    yb = from_distance(jnp.concatenate([yb, table], axis=0), "gy", 3)
    x_faces = [swap(face, "gx", first) for first, face in enumerate(faces[4:])]
    table = jnp.concatenate([table, yb[count_z:]], axis=0)
    table = gather_relative(table[None], "gx").reshape(size_x * size_y, rows, points)
    halos = [za, zb, ya, yb] + x_faces

    samples = None
    for step in range(steps):
        last, packs = step == steps - 1, step == steps - 2
        shapes = [jax.ShapeDtypeStruct(q.shape, jnp.float32)]
        out_specs = vmem_specs(1)
        scratch = []
        if last:
            out_specs = [pl.BlockSpec(memory_space=pl.ANY)]
            scratch = [pltpu.VMEM(q.shape, jnp.float32), pltpu.SemaphoreType.DMA((count_x,))]
        else:
            shapes += face_shapes(shape, extra if packs else 0)
            if packs:
                scratch = [pltpu.VMEM((16, lanes), jnp.float32)]
            else:
                shapes += [jax.ShapeDtypeStruct((16, lanes), jnp.float32)]
            out_specs = vmem_specs(len(shapes))
        past = [] if step == 0 or last else [samples]
        results = pl.pallas_call(
            functools.partial(step_body, shape=shape, points=points, capacity=capacity, step=step, steps=steps),
            out_shape=shapes,
            in_specs=[pl.BlockSpec(memory_space=pltpu.SMEM)] + vmem_specs(2 + len(halos) + len(past)),
            out_specs=out_specs,
            scratch_shapes=scratch
            + [pltpu.VMEM((3,) + shape, jnp.float32), pltpu.VMEM((8, lanes), jnp.float32)]
            + [pltpu.VMEM((4, count_y // 128, count_x, 128), jnp.float32)] * 2
            + [pltpu.VMEM((count_z, 128), jnp.float32)] * 2
            + [pltpu.VMEM((4, count_z, count_y), jnp.float32)] * 2
            + [pltpu.VMEM((count_x, count_z, lanes), jnp.float32), pltpu.VMEM((count_y, 3 * lanes), jnp.bfloat16)]
            + ([] if last else [pltpu.VMEM((count_x, count_z, lanes), jnp.float32)])
            + ([] if last else [pltpu.VMEM((3 * count_y, lanes), jnp.bfloat16)])
            + ([pltpu.VMEM((3 * count_y, lanes), jnp.bfloat16)] if step == 0 else []),
            compiler_params=params,
            name="step",
        )(turbines, table, q, *halos, *past)
        q = results[0]
        if last:
            break
        faces = results[1 : 1 + len(forms)]
        if not packs:
            samples = results[-1]
            halos = swap_faces(faces)
            continue
        za, zb, ya, yb = faces[:4]
        za_in, zb_in = swap(za, "gz", 0), swap_inner(zb, "gz")
        sums = za[4 * count_x :] + za_in[4 * count_x :]
        pieces = jnp.concatenate([sums[:, h * 128 : h * 128 + 128] for h in range(2)], axis=0)
        pieces, ya, zb_in = barrier((pieces, ya, zb_in))
        ya_in = swap(jnp.concatenate([ya, pieces], axis=0), "gy", 0)
        x_faces = [swap(face, "gx", first) for first, face in enumerate(faces[4:])]
        pieces = jnp.concatenate([pieces, ya_in[count_z:]], axis=0).reshape(2, -1, points)
        pieces, yb, x_faces = barrier((pieces, yb, x_faces))
        pieces = gather_relative(pieces, "gy", 2).reshape(-1, points)
        yb_in = swap_inner(yb, "gy")
        pieces, yb_in = barrier((pieces, yb_in))
        halos = [za_in, zb_in, ya_in, yb_in] + x_faces

    distance = 2
    while distance < size_z:
        pieces = pieces + from_distance(pieces, "gz", distance)
        distance *= 2
    pieces, q = barrier((pieces, q))
    mine = lax.dynamic_slice_in_dim(pieces, lax.axis_index("gz") * part, part, axis=1)[None]
    mine = gather_relative(mine, "gx").reshape(size_x * size_y, 2, extra, part)
    holder = (lax.axis_index("gx") * size_y + lax.axis_index("gy") + 1).astype(jnp.float32)
    returned = 0.0
    for j in range(capacity):
        row = (j // 2) * (3 * steps + 1)
        values = mine[:, j % 2, row : row + 3 * steps]
        match = mine[:, j % 2, row + 3 * steps :][:, :1] == holder
        returned = returned + jnp.sum(jnp.where(match, values, 0.0), axis=0)
    return q, returned.reshape(positions.shape)


def solution(mesh):
    in_specs = (
        P(None, "gx", "gz", "gy"),
        P(None, None, ("gx", "gy"), "gz"),
        P(None, None, ("gx", "gy"), "gz"),
        P("gx", "gy", "gz", None),
    )
    out_specs = (P(None, "gx", "gz", "gy"), P(None, None, ("gx", "gy"), "gz"))
    return jax.shard_map(shards, mesh=mesh, in_specs=in_specs, out_specs=out_specs, check_vma=False)
```

```python
import functools
import math

import jax
import jax.numpy as jnp
from jax import lax
from jax.experimental import pallas as pl
from jax.experimental.pallas import tpu as pltpu
from jax.sharding import PartitionSpec as P

kernel_width = 2.0
kernel_norm = 1.0 / (math.pi**1.5 * kernel_width**3)
time_step = 0.1
smag_coef = 0.17
viscosity = 0.02
diffusivity = 0.02
prandtl = 0.4
vmem_limit = 24 << 20


def swap_pairs(count, first):
    pairs = []
    for low in range(first, count - 1, 2):
        pairs += [(low, low + 1), (low + 1, low)]
    return pairs


def swap(value, axis, first):
    pairs = swap_pairs(lax.axis_size(axis), first)
    if not pairs:
        return jnp.zeros_like(value)
    return lax.ppermute(value, axis, pairs)


def swap_inner(value, axis):
    size, chips = lax.axis_size(axis), lax.axis_size("gx")
    target = {low: high for low, high in swap_pairs(size, 1)}
    pairs = []
    for x in range(chips):
        for k in range(size):
            pairs.append((x * size + k, x * size + target[k] if k in target else (x ^ 1) * size + k))
    return lax.ppermute(value, ("gx", axis), pairs)


def from_distance(value, axis, distance):
    count = lax.axis_size(axis)
    return lax.ppermute(value, axis, [(i, i ^ distance) for i in range(count)])


def gather_relative(value, axis, distance=1):
    while distance < lax.axis_size(axis):
        value = jnp.concatenate([value, from_distance(value, axis, distance)], axis=0)
        distance *= 2
    return value


def pick(flag, first, second):
    return jnp.where(flag, first, second)


def is_even(axis):
    return lax.rem(lax.axis_index(axis), 2) == 0


def write_faces(q_ref, face_refs, shape, await_component=None):
    count_x, count_z, count_y = shape
    za_ref, zb_ref, ya_ref, yb_ref, xa_ref = face_refs[:5]
    even_x, even_z, even_y = is_even("gx"), is_even("gz"), is_even("gy")
    lane = lax.broadcasted_iota(jnp.int32, (count_z, 128), 1)
    low_y = jnp.zeros((count_z, 128), jnp.float32)
    high_y = jnp.zeros((count_z, 128), jnp.float32)
    for comp in range(4):
        if await_component is not None:
            await_component(comp)
        low, high = q_ref[comp, 0], q_ref[comp, count_x - 1]
        xa_ref[comp] = pick(even_x, high, low)
        for xb_ref in face_refs[5:]:
            xb_ref[comp] = pick(even_x, low, high)
        low = q_ref[comp, :, 0, :]
        high = q_ref[comp, :, count_z - 1, :]
        za_ref[comp * count_x : (comp + 1) * count_x] = pick(even_z, high, low)
        zb_ref[comp * count_x : (comp + 1) * count_x] = pick(even_z, low, high)
        for x in range(count_x):
            place = comp * count_x + x
            first = q_ref[comp, x, :, :128]
            last = q_ref[comp, x, :, count_y - 128 :]
            low_y = jnp.where(lane == place, pltpu.roll(first, place, 1), low_y)
            high_y = jnp.where(lane == place, pltpu.roll(last, (place + 1) % 128, 1), high_y)
    ya_ref[...] = pick(even_y, high_y, low_y)
    yb_ref[...] = pick(even_y, low_y, high_y)


def faces_body(far_ref, *refs, shape):
    face_refs, q_ref, sems = refs[:-2], refs[-2], refs[-1]
    copies = [pltpu.make_async_copy(far_ref.at[comp], q_ref.at[comp], sems.at[comp]) for comp in range(4)]
    for copy in copies:
        copy.start()
    write_faces(q_ref, face_refs, shape, lambda comp: copies[comp].wait())


def sorted_slots(list_ref, capacity):
    slots = [list_ref[j] for j in range(capacity)]
    for first in range(capacity):
        for second in range(first + 1, capacity):
            a, b = slots[first], slots[second]
            slots[first], slots[second] = jnp.minimum(a, b), jnp.maximum(a, b)
    return slots


def masks_of(shape):
    count_z = shape[1]
    sub = lax.broadcasted_iota(jnp.int32, (count_z, 128), 0)
    lane = lax.broadcasted_iota(jnp.int32, (count_z, 128), 1)
    return sub == 0, sub == count_z - 1, lane == 0, lane == 127


def tile_update(shifts, pushed):
    diffs, laplace, centre = [], [], []
    for c, minus_x, plus_x, minus_y, plus_y, minus_z, plus_z in shifts:
        diffs.append((plus_x - minus_x, plus_y - minus_y, plus_z - minus_z))
        laplace.append((plus_x + minus_x) + (plus_y + minus_y) + (plus_z + minus_z) - 6.0 * c)
        centre.append(c)
    diagonal = diffs[0][0] * diffs[0][0] + diffs[1][1] * diffs[1][1] + diffs[2][2] * diffs[2][2]
    xy = diffs[0][1] + diffs[1][0]
    xz = diffs[0][2] + diffs[2][0]
    yz = diffs[1][2] + diffs[2][1]
    total = (diagonal + diagonal) + (xy * xy + xz * xz + yz * yz)
    root = total * lax.rsqrt(jnp.maximum(total, 1.1754944e-38))
    scale_u = time_step * viscosity + (0.5 * time_step * smag_coef**2) * root
    scale_t = time_step * diffusivity + (0.5 * time_step * smag_coef**2 / prandtl) * root
    half = [0.5 * time_step * centre[a] for a in range(3)]
    out = []
    for comp in range(4):
        d = diffs[comp]
        moved = half[0] * d[0] + half[1] * d[1] + half[2] * d[2]
        value = centre[comp] - moved + (scale_u if comp < 3 else scale_t) * laplace[comp]
        out.append(value + pushed[comp] if comp < 3 else value)
    return out


def split(value):
    high = value.astype(jnp.bfloat16)
    low = (value - high.astype(jnp.float32)).astype(jnp.bfloat16)
    return high, low


def turbine_rows(rows_ref, table_ref, slots, step, points):
    size_x, size_y = lax.axis_size("gx"), lax.axis_size("gy")
    for j, slot in enumerate(slots):
        t = jnp.minimum(slot, size_x * size_y - 1)
        place_x = lax.bitwise_xor(lax.div(t, size_y), lax.axis_index("gx"))
        place_y = lax.bitwise_xor(lax.rem(t, size_y), lax.axis_index("gy"))
        entry = place_x * size_y + lax.bitwise_xor(place_y, lax.div(place_y, 2))
        rows_ref[:, j * points : (j + 1) * points] = table_ref[entry, 8 * step : 8 * step + 8, :]
    return rows_ref[...]


def point_factors(rows, listed, shape):
    lanes = rows.shape[1]

    def factor(row, axis, count):
        start = (lax.axis_index(axis) * count).astype(jnp.float32)
        cells = lax.broadcasted_iota(jnp.int32, (count, lanes), 0).astype(jnp.float32) + start
        gap = cells - row
        return jnp.exp(-(gap * gap) / kernel_width**2)

    count_x, count_z, count_y = shape
    factor_x = factor(rows[0:1], "gx", count_x)
    factor_y = factor(rows[1:2], "gy", count_y)
    factor_z = factor(rows[2:3], "gz", count_z) * jnp.where(listed, kernel_norm, 0.0)
    weights = (factor_x[:, None, :] * factor_z[None, :, :]).reshape(count_x * count_z, lanes)
    return weights, split(factor_y)


def store_factors(rows, listed, weight_ref, right_refs, shape):
    weights, (high, low) = point_factors(rows, listed, shape)
    weight_ref[...] = weights.reshape(weight_ref.shape)
    for axis, right_ref in right_refs.items():
        right_ref[...] = jnp.concatenate([high, high, low], axis=axis)


def push(force_ref, rows, weight_ref, right_ref, start, planes, shape):
    count_z = shape[1]
    weights = weight_ref[start : start + planes].reshape(planes * count_z, -1)
    left = []
    for comp in range(3):
        first, second = split(weights * (rows[3 + comp : 4 + comp] * time_step))
        left.append(jnp.concatenate([first, second, first], axis=1))
    left = jnp.concatenate(left, axis=0)
    pushed = lax.dot_general(left, right_ref[...], (((1,), (1,)), ((), ())), preferred_element_type=jnp.float32)
    force_ref[:, start : start + planes] = pushed.reshape((3, planes) + shape[1:])


def sample(q_ref, weight_ref, right_ref, start, planes, shape):
    count_z = shape[1]
    left = []
    for comp in range(3):
        first, second = split(q_ref[comp, start : start + planes].reshape(planes * count_z, -1))
        left.append(jnp.concatenate([first, second, first], axis=1))
    along = jnp.dot(jnp.concatenate(left, axis=0), right_ref[...], preferred_element_type=jnp.float32)
    weights = weight_ref[start : start + planes].reshape(planes * count_z, -1)
    rows = planes * count_z
    return [jnp.sum(along[k * rows : (k + 1) * rows] * weights, axis=0, keepdims=True) for k in range(3)]


def step_body(*refs, shape, points, capacity, step, steps):
    count_x, count_z, count_y = shape
    last, packs = step == steps - 1, step == steps - 2
    faces = len(face_shapes(shape))
    refs = list(refs)
    list_ref, table_ref, q_ref = refs[:3]
    za_ref, zb_ref, ya_ref, yb_ref = refs[3:7]
    x_refs, refs = refs[7 : 3 + faces], refs[3 + faces :]
    past_ref = None if step == 0 or last else refs.pop(0)
    out_ref = refs.pop(0)
    sample_ref = None
    if not last:
        face_refs, refs = refs[:faces], refs[faces:]
        sample_ref = refs.pop(0)
    else:
        far_ref, out_ref, sems = out_ref, refs.pop(0), refs.pop(0)
    force_ref, rows_ref, low_z_ref, high_z_ref, low_y_ref, high_y_ref, low_x_ref, high_x_ref = refs[:8]
    weight_ref, push_right_ref = refs[8:10]
    if not last:
        next_weight_ref, sample_right_ref = refs[10:12]
    if step == 0:
        first_right_ref = refs[12]
    slots = sorted_slots(list_ref, capacity)
    turbines = lax.axis_size("gx") * lax.axis_size("gy")
    listed = slots[0] < turbines

    if not last:
        sample_ref[...] = jnp.zeros(sample_ref.shape, jnp.float32)
        if past_ref is not None:
            sample_ref[: 3 * step + 3] = past_ref[: 3 * step + 3]

    rows = turbine_rows(rows_ref, table_ref, slots, step, points)
    store_factors(rows, listed, weight_ref, {1: push_right_ref, 0: first_right_ref} if step == 0 else {1: push_right_ref}, shape)

    even_x, even_z, even_y = is_even("gx"), is_even("gz"), is_even("gy")
    index_y, index_z = lax.axis_index("gy"), lax.axis_index("gz")
    tiles = count_y // 128
    for comp in range(4):
        for tile in range(tiles):
            there = slice(comp * count_x, (comp + 1) * count_x), slice(tile * 128, tile * 128 + 128)
            first, second = za_ref[there], zb_ref[there]
            low_z_ref[comp, tile] = pick(index_z == 0, 0.0, pick(even_z, second, first))
            high_z_ref[comp, tile] = pick(index_z == lax.axis_size("gz") - 1, 0.0, pick(even_z, first, second))
    low_y_ref[...] = pick(index_y == 0, 0.0, pick(even_y, yb_ref[:count_z], ya_ref[:count_z]))
    high_y_ref[...] = pick(index_y == lax.axis_size("gy") - 1, 0.0, pick(even_y, ya_ref[:count_z], yb_ref[:count_z]))
    first = x_refs[0][...]
    second = x_refs[1][...] if len(x_refs) > 1 else 0.0
    low_x_ref[...] = pick(even_x, second, first)
    high_x_ref[...] = pick(even_x, first, second)
    first_z, last_z, first_y, last_y = masks_of(shape)

    def plane(x, minus, plus):
        centre, up, down = [], [], []
        for comp in range(4):
            row = [q_ref[comp, x, :, tile * 128 : tile * 128 + 128] for tile in range(tiles)]
            place = comp * count_x + x
            turn = (128 - place) % 128 if isinstance(place, int) else 128 - place
            centre.append(row)
            up.append([pltpu.roll(low_y_ref[...], turn, 1)] + [pltpu.roll(c, 1, 1) for c in row])
            down.append([pltpu.roll(c, 127, 1) for c in row] + [pltpu.roll(high_y_ref[...], 127 - place, 1)])
        for tile in range(tiles):
            here = slice(tile * 128, tile * 128 + 128)
            shifts = []
            for comp in range(4):
                c = centre[comp][tile]
                minus_y = jnp.where(first_y, up[comp][tile], up[comp][tile + 1])
                plus_y = jnp.where(last_y, down[comp][tile + 1], down[comp][tile])
                low_z = low_z_ref[comp, tile, pl.ds(x, 1), :]
                high_z = high_z_ref[comp, tile, pl.ds(x, 1), :]
                minus_z = jnp.where(first_z, low_z, pltpu.roll(c, 1, 0))
                plus_z = jnp.where(last_z, high_z, pltpu.roll(c, count_z - 1, 0))
                shifts.append((c, minus(comp, here), plus(comp, here), minus_y, plus_y, minus_z, plus_z))
            pushed = [force_ref[comp, x, :, here] for comp in range(3)]
            for comp, value in enumerate(tile_update(shifts, pushed)):
                out_ref[comp, x, :, here] = value

    def of_plane(x):
        return lambda comp, here: q_ref[comp, x, :, here]

    def copy_out(number, start, count):
        here = pl.ds(start, count)
        return pltpu.make_async_copy(out_ref.at[:, here], far_ref.at[:, here], sems.at[number])

    group = max(g for g in range(1, 9) if count_x % g == 0)
    groups = count_x // group
    sums = [0.0] * 3
    first_sums = [0.0] * 3
    push(force_ref, rows, weight_ref, push_right_ref, 0, group, shape)
    for number in range(groups):
        start = number * group
        if number + 1 < groups:
            push(force_ref, rows, weight_ref, push_right_ref, start + group, group, shape)
        if step == 0:
            more = sample(q_ref, weight_ref, first_right_ref, start, group, shape)
            first_sums = [a + b for a, b in zip(first_sums, more)]
        for x in range(start, start + group):
            minus = of_plane(x - 1) if x else lambda comp, here: low_x_ref[comp, :, here]
            plus = of_plane(x + 1) if x < count_x - 1 else lambda comp, here: high_x_ref[comp, :, here]
            plane(x, minus, plus)
        if not last and not number:
            next_rows = turbine_rows(rows_ref, table_ref, slots, step + 1, points)
            store_factors(next_rows, listed, next_weight_ref, {0: sample_right_ref}, shape)
        if last:
            copy_out(number, start, group).start()
        elif number:
            more = sample(out_ref, next_weight_ref, sample_right_ref, start - group, group, shape)
            sums = [a + b for a, b in zip(sums, more)]
    if last:
        for number in range(groups):
            copy_out(number, number * group, group).wait()
        return
    write_faces(out_ref, face_refs, shape)
    more = sample(out_ref, next_weight_ref, sample_right_ref, count_x - group, group, shape)
    for comp in range(3):
        sample_ref[3 * step + 3 + comp : 3 * step + 4 + comp] = sums[comp] + more[comp]
        if step == 0:
            sample_ref[comp : comp + 1] = first_sums[comp]

    if packs:
        count = 3 * steps + 1
        za_ref = face_refs[0]
        start = 4 * count_x
        za_ref[start:] = jnp.zeros((za_ref.shape[0] - start, count_y), jnp.float32)
        for j, slot in enumerate(slots):
            lane, row = (j % 2) * points, start + (j // 2) * count
            values = sample_ref[: count - 1, j * points : (j + 1) * points]
            za_ref[row : row + count - 1, lane : lane + points] = values
            name = jnp.where(listed, 0.5 * (slot + 1).astype(jnp.float32), 0.0)
            za_ref[row + count - 1 : row + count, lane : lane + points] = jnp.full((1, points), name)


def face_shapes(shape, extra=0):
    count_x, count_z, count_y = shape
    forms = [(4 * count_x + extra, count_y), (4 * count_x, count_y)]
    forms += [(count_z, 128)] * 2 + [(4, count_z, count_y)] * (1 if lax.axis_size("gx") == 2 else 2)
    return [jax.ShapeDtypeStruct(form, jnp.float32) for form in forms]


def vmem_specs(count):
    return [pl.BlockSpec(memory_space=pltpu.VMEM)] * count


def swap_faces(faces):
    za, zb, ya, yb = faces[:4]
    zb, za = swap_inner(zb, "gz"), swap(za, "gz", 0)
    yb, ya = swap_inner(yb, "gy"), swap(ya, "gy", 0)
    halos = [za, zb, ya, yb]
    return halos + [swap(face, "gx", first) for first, face in enumerate(faces[4:])]


def masked(halo, axis, first):
    index = lax.axis_index(axis)
    partner = index + 1 - 2 * lax.rem(index + first, 2)
    inside = jnp.logical_and(partner >= 0, partner < lax.axis_size(axis))
    return jnp.where(inside, halo, 0.0)


def true_order(pieces, axis):
    distance = 1
    while distance < pieces.shape[0]:
        swapped = pieces.reshape((-1, 2, distance) + pieces.shape[1:])[:, ::-1].reshape(pieces.shape)
        odd = lax.rem(lax.div(lax.axis_index(axis), distance), 2) == 1
        pieces = jnp.where(odd, swapped, pieces)
        distance *= 2
    return pieces


def shards(flow, positions, loads, block_list):
    capacity = block_list.shape[-1]
    steps, _, _, part = positions.shape
    shape = flow.shape[1:]
    count_x, count_z, count_y = shape
    size_x, size_y, size_z = lax.axis_size("gx"), lax.axis_size("gy"), lax.axis_size("gz")
    points = part * size_z
    lanes = capacity * points
    params = pltpu.CompilerParams(vmem_limit_bytes=vmem_limit)
    q = flow
    turbines = block_list.reshape(capacity)
    barrier = lax.optimization_barrier
    forms = face_shapes(shape)

    extra = pl.cdiv((3 * steps + 1) * pl.cdiv(capacity, 2), 8) * 8

    own = jnp.concatenate([positions.reshape(steps, 3, part), loads.reshape(steps, 3, part)], axis=1)
    table = jnp.pad(own, ((0, 0), (0, 2), (0, 0))).reshape(1, 8 * steps, part)
    table = jnp.concatenate([table, from_distance(table, "gz", 1)], axis=0)
    faces = pl.pallas_call(
        functools.partial(faces_body, shape=shape),
        out_shape=forms,
        in_specs=[pl.BlockSpec(memory_space=pl.ANY)],
        out_specs=vmem_specs(len(forms)),
        scratch_shapes=[pltpu.VMEM(q.shape, jnp.float32), pltpu.SemaphoreType.DMA((4,))],
        compiler_params=params,
        name="faces",
    )(q)
    table, faces = barrier((table, list(faces)))
    za, zb, ya, yb = faces[:4]
    za = masked(swap(za, "gz", 0), "gz", 0)
    distance = 2
    while distance < size_z:
        received = from_distance(table, "gz", distance)
        received, za = barrier((received, za))
        table = jnp.concatenate([table, received], axis=0)
        distance *= 2
    table = true_order(table, "gz")
    table = jnp.concatenate([table[k] for k in range(size_z)], axis=1)
    rows = 8 * steps
    zb, ya, table = barrier((zb, ya, table))
    zb = masked(swap_inner(zb, "gz"), "gz", 1)
    ya = swap(jnp.concatenate([ya, table], axis=0), "gy", 0)
    ya, zb = barrier((ya, zb))
    table = jnp.concatenate([table, ya[count_z:]], axis=0)
    yb = from_distance(jnp.concatenate([yb, table], axis=0), "gy", 3)
    x_faces = [swap(face, "gx", first) for first, face in enumerate(faces[4:])]
    table = jnp.concatenate([table, yb[count_z:]], axis=0)
    table = gather_relative(table[None], "gx").reshape(size_x * size_y, rows, points)
    halos = [za, zb, ya, yb] + x_faces

    samples = None
    for step in range(steps):
        last, packs = step == steps - 1, step == steps - 2
        shapes = [jax.ShapeDtypeStruct(q.shape, jnp.float32)]
        out_specs = vmem_specs(1)
        scratch = []
        if last:
            out_specs = [pl.BlockSpec(memory_space=pl.ANY)]
            scratch = [pltpu.VMEM(q.shape, jnp.float32), pltpu.SemaphoreType.DMA((count_x,))]
        else:
            shapes += face_shapes(shape, extra if packs else 0)
            if packs:
                scratch = [pltpu.VMEM((16, lanes), jnp.float32)]
            else:
                shapes += [jax.ShapeDtypeStruct((16, lanes), jnp.float32)]
            out_specs = vmem_specs(len(shapes))
        past = [] if step == 0 or last else [samples]
        results = pl.pallas_call(
            functools.partial(step_body, shape=shape, points=points, capacity=capacity, step=step, steps=steps),
            out_shape=shapes,
            in_specs=[pl.BlockSpec(memory_space=pltpu.SMEM)] + vmem_specs(2 + len(halos) + len(past)),
            out_specs=out_specs,
            scratch_shapes=scratch
            + [pltpu.VMEM((3,) + shape, jnp.float32), pltpu.VMEM((8, lanes), jnp.float32)]
            + [pltpu.VMEM((4, count_y // 128, count_x, 128), jnp.float32)] * 2
            + [pltpu.VMEM((count_z, 128), jnp.float32)] * 2
            + [pltpu.VMEM((4, count_z, count_y), jnp.float32)] * 2
            + [pltpu.VMEM((count_x, count_z, lanes), jnp.float32), pltpu.VMEM((count_y, 3 * lanes), jnp.bfloat16)]
            + ([] if last else [pltpu.VMEM((count_x, count_z, lanes), jnp.float32)])
            + ([] if last else [pltpu.VMEM((3 * count_y, lanes), jnp.bfloat16)])
            + ([pltpu.VMEM((3 * count_y, lanes), jnp.bfloat16)] if step == 0 else []),
            compiler_params=params,
            name="step",
        )(turbines, table, q, *halos, *past)
        q = results[0]
        if last:
            break
        faces = results[1 : 1 + len(forms)]
        if not packs:
            samples = results[-1]
            halos = swap_faces(faces)
            continue
        za, zb, ya, yb = faces[:4]
        za_in, zb_in = swap(za, "gz", 0), swap_inner(zb, "gz")
        sums = za[4 * count_x :] + za_in[4 * count_x :]
        pieces = jnp.concatenate([sums[:, h * 128 : h * 128 + 128] for h in range(2)], axis=0)
        pieces, ya, zb_in = barrier((pieces, ya, zb_in))
        ya_in = swap(jnp.concatenate([ya, pieces], axis=0), "gy", 0)
        x_faces = [swap(face, "gx", first) for first, face in enumerate(faces[4:])]
        pieces = jnp.concatenate([pieces, ya_in[count_z:]], axis=0).reshape(2, -1, points)
        pieces, yb, x_faces = barrier((pieces, yb, x_faces))
        pieces = gather_relative(pieces, "gy", 2).reshape(-1, points)
        yb_in = swap_inner(yb, "gy")
        pieces, yb_in = barrier((pieces, yb_in))
        halos = [za_in, zb_in, ya_in, yb_in] + x_faces

    distance = 2
    while distance < size_z:
        pieces = pieces + from_distance(pieces, "gz", distance)
        distance *= 2
    pieces, q = barrier((pieces, q))
    mine = lax.dynamic_slice_in_dim(pieces, lax.axis_index("gz") * part, part, axis=1)[None]
    mine = gather_relative(mine, "gx").reshape(size_x * size_y, 2, extra, part)
    holder = (lax.axis_index("gx") * size_y + lax.axis_index("gy") + 1).astype(jnp.float32)
    returned = 0.0
    for j in range(capacity):
        row = (j // 2) * (3 * steps + 1)
        values = mine[:, j % 2, row : row + 3 * steps]
        match = mine[:, j % 2, row + 3 * steps :][:, :1] == holder
        returned = returned + jnp.sum(jnp.where(match, values, 0.0), axis=0)
    return q, returned.reshape(positions.shape)


def solution(mesh):
    in_specs = (
        P(None, "gx", "gz", "gy"),
        P(None, None, ("gx", "gy"), "gz"),
        P(None, None, ("gx", "gy"), "gz"),
        P("gx", "gy", "gz", None),
    )
    out_specs = (P(None, "gx", "gz", "gy"), P(None, None, ("gx", "gy"), "gz"))
    return jax.shard_map(shards, mesh=mesh, in_specs=in_specs, out_specs=out_specs, check_vma=False)
```

```python
import functools
import math

import jax
import jax.numpy as jnp
from jax import lax
from jax.experimental import pallas as pl
from jax.experimental.pallas import tpu as pltpu
from jax.sharding import PartitionSpec as P

kernel_width = 2.0
kernel_norm = 1.0 / (math.pi**1.5 * kernel_width**3)
time_step = 0.1
smag_coef = 0.17
viscosity = 0.02
diffusivity = 0.02
prandtl = 0.4
vmem_limit = 24 << 20


def swap_pairs(count, first):
    pairs = []
    for low in range(first, count - 1, 2):
        pairs += [(low, low + 1), (low + 1, low)]
    return pairs


def swap(value, axis, first):
    pairs = swap_pairs(lax.axis_size(axis), first)
    if not pairs:
        return jnp.zeros_like(value)
    return lax.ppermute(value, axis, pairs)


def swap_inner(value, axis):
    size, chips = lax.axis_size(axis), lax.axis_size("gx")
    target = {low: high for low, high in swap_pairs(size, 1)}
    pairs = []
    for x in range(chips):
        for k in range(size):
            pairs.append((x * size + k, x * size + target[k] if k in target else (x ^ 1) * size + k))
    return lax.ppermute(value, ("gx", axis), pairs)


def from_distance(value, axis, distance):
    count = lax.axis_size(axis)
    return lax.ppermute(value, axis, [(i, i ^ distance) for i in range(count)])


def gather_relative(value, axis, distance=1):
    while distance < lax.axis_size(axis):
        value = jnp.concatenate([value, from_distance(value, axis, distance)], axis=0)
        distance *= 2
    return value


def pick(flag, first, second):
    return jnp.where(flag, first, second)


def is_even(axis):
    return lax.rem(lax.axis_index(axis), 2) == 0


def write_faces(q_ref, face_refs, shape, await_component=None):
    count_x, count_z, count_y = shape
    za_ref, zb_ref, ya_ref, yb_ref, xa_ref = face_refs[:5]
    even_x, even_z, even_y = is_even("gx"), is_even("gz"), is_even("gy")
    lane = lax.broadcasted_iota(jnp.int32, (count_z, 128), 1)
    low_y = jnp.zeros((count_z, 128), jnp.float32)
    high_y = jnp.zeros((count_z, 128), jnp.float32)
    for comp in range(4):
        if await_component is not None:
            await_component(comp)
        low, high = q_ref[comp, 0], q_ref[comp, count_x - 1]
        xa_ref[comp] = pick(even_x, high, low)
        for xb_ref in face_refs[5:]:
            xb_ref[comp] = pick(even_x, low, high)
        low = q_ref[comp, :, 0, :]
        high = q_ref[comp, :, count_z - 1, :]
        za_ref[comp * count_x : (comp + 1) * count_x] = pick(even_z, high, low)
        zb_ref[comp * count_x : (comp + 1) * count_x] = pick(even_z, low, high)
        for x in range(count_x):
            place = comp * count_x + x
            first = q_ref[comp, x, :, :128]
            last = q_ref[comp, x, :, count_y - 128 :]
            low_y = jnp.where(lane == place, pltpu.roll(first, place, 1), low_y)
            high_y = jnp.where(lane == place, pltpu.roll(last, (place + 1) % 128, 1), high_y)
    ya_ref[...] = pick(even_y, high_y, low_y)
    yb_ref[...] = pick(even_y, low_y, high_y)


def faces_body(far_ref, *refs, shape):
    face_refs, q_ref, sems = refs[:-2], refs[-2], refs[-1]
    copies = [pltpu.make_async_copy(far_ref.at[comp], q_ref.at[comp], sems.at[comp]) for comp in range(4)]
    for copy in copies:
        copy.start()
    write_faces(q_ref, face_refs, shape, lambda comp: copies[comp].wait())


def sorted_slots(list_ref, capacity):
    slots = [list_ref[j] for j in range(capacity)]
    for first in range(capacity):
        for second in range(first + 1, capacity):
            a, b = slots[first], slots[second]
            slots[first], slots[second] = jnp.minimum(a, b), jnp.maximum(a, b)
    return slots


def masks_of(shape):
    count_z = shape[1]
    sub = lax.broadcasted_iota(jnp.int32, (count_z, 128), 0)
    lane = lax.broadcasted_iota(jnp.int32, (count_z, 128), 1)
    return sub == 0, sub == count_z - 1, lane == 0, lane == 127


def tile_update(shifts, pushed):
    diffs, laplace, centre = [], [], []
    for c, minus_x, plus_x, minus_y, plus_y, minus_z, plus_z in shifts:
        diffs.append((plus_x - minus_x, plus_y - minus_y, plus_z - minus_z))
        laplace.append((plus_x + minus_x) + (plus_y + minus_y) + (plus_z + minus_z) - 6.0 * c)
        centre.append(c)
    diagonal = diffs[0][0] * diffs[0][0] + diffs[1][1] * diffs[1][1] + diffs[2][2] * diffs[2][2]
    xy = diffs[0][1] + diffs[1][0]
    xz = diffs[0][2] + diffs[2][0]
    yz = diffs[1][2] + diffs[2][1]
    total = (diagonal + diagonal) + (xy * xy + xz * xz + yz * yz)
    root = total * lax.rsqrt(jnp.maximum(total, 1.1754944e-38))
    scale_u = time_step * viscosity + (0.5 * time_step * smag_coef**2) * root
    scale_t = time_step * diffusivity + (0.5 * time_step * smag_coef**2 / prandtl) * root
    half = [0.5 * time_step * centre[a] for a in range(3)]
    out = []
    for comp in range(4):
        d = diffs[comp]
        moved = half[0] * d[0] + half[1] * d[1] + half[2] * d[2]
        value = centre[comp] - moved + (scale_u if comp < 3 else scale_t) * laplace[comp]
        out.append(value + pushed[comp] if comp < 3 else value)
    return out


def split(value):
    high = value.astype(jnp.bfloat16)
    low = (value - high.astype(jnp.float32)).astype(jnp.bfloat16)
    return high, low


def turbine_rows(rows_ref, table_ref, slots, step, points):
    size_x, size_y = lax.axis_size("gx"), lax.axis_size("gy")
    for j, slot in enumerate(slots):
        t = jnp.minimum(slot, size_x * size_y - 1)
        place_x = lax.bitwise_xor(lax.div(t, size_y), lax.axis_index("gx"))
        place_y = lax.bitwise_xor(lax.rem(t, size_y), lax.axis_index("gy"))
        entry = place_x * size_y + lax.bitwise_xor(place_y, lax.div(place_y, 2))
        rows_ref[:, j * points : (j + 1) * points] = table_ref[entry, 8 * step : 8 * step + 8, :]
    return rows_ref[...]


def point_factors(rows, listed, shape):
    lanes = rows.shape[1]

    def factor(row, axis, count):
        start = (lax.axis_index(axis) * count).astype(jnp.float32)
        cells = lax.broadcasted_iota(jnp.int32, (count, lanes), 0).astype(jnp.float32) + start
        gap = cells - row
        return jnp.exp(-(gap * gap) / kernel_width**2)

    count_x, count_z, count_y = shape
    factor_x = factor(rows[0:1], "gx", count_x)
    factor_y = factor(rows[1:2], "gy", count_y)
    factor_z = factor(rows[2:3], "gz", count_z) * jnp.where(listed, kernel_norm, 0.0)
    weights = (factor_x[:, None, :] * factor_z[None, :, :]).reshape(count_x * count_z, lanes)
    return weights, split(factor_y)


def store_factors(rows, listed, weight_ref, right_refs, shape):
    weights, (high, low) = point_factors(rows, listed, shape)
    weight_ref[...] = weights.reshape(weight_ref.shape)
    for axis, right_ref in right_refs.items():
        right_ref[...] = jnp.concatenate([high, high, low], axis=axis)


def push(force_ref, rows, weight_ref, right_ref, start, planes, shape):
    count_z = shape[1]
    weights = weight_ref[start : start + planes].reshape(planes * count_z, -1)
    left = []
    for comp in range(3):
        first, second = split(weights * (rows[3 + comp : 4 + comp] * time_step))
        left.append(jnp.concatenate([first, second, first], axis=1))
    left = jnp.concatenate(left, axis=0)
    pushed = lax.dot_general(left, right_ref[...], (((1,), (1,)), ((), ())), preferred_element_type=jnp.float32)
    force_ref[:, start : start + planes] = pushed.reshape((3, planes) + shape[1:])


def sample(q_ref, weight_ref, right_ref, start, planes, shape):
    count_z = shape[1]
    left = []
    for comp in range(3):
        first, second = split(q_ref[comp, start : start + planes].reshape(planes * count_z, -1))
        left.append(jnp.concatenate([first, second, first], axis=1))
    along = jnp.dot(jnp.concatenate(left, axis=0), right_ref[...], preferred_element_type=jnp.float32)
    weights = weight_ref[start : start + planes].reshape(planes * count_z, -1)
    rows = planes * count_z
    return [jnp.sum(along[k * rows : (k + 1) * rows] * weights, axis=0, keepdims=True) for k in range(3)]


def step_body(*refs, shape, points, capacity, step, steps):
    count_x, count_z, count_y = shape
    last, packs = step == steps - 1, step == steps - 2
    faces = len(face_shapes(shape))
    refs = list(refs)
    list_ref, table_ref, q_ref = refs[:3]
    za_ref, zb_ref, ya_ref, yb_ref = refs[3:7]
    x_refs, refs = refs[7 : 3 + faces], refs[3 + faces :]
    past_ref = None if step == 0 or last else refs.pop(0)
    out_ref = refs.pop(0)
    sample_ref = None
    if not last:
        face_refs, refs = refs[:faces], refs[faces:]
        sample_ref = refs.pop(0)
    else:
        far_ref, out_ref, sems = out_ref, refs.pop(0), refs.pop(0)
    force_ref, rows_ref, low_z_ref, high_z_ref, low_y_ref, high_y_ref, low_x_ref, high_x_ref = refs[:8]
    weight_ref, push_right_ref = refs[8:10]
    if not last:
        next_weight_ref, sample_right_ref = refs[10:12]
    if step == 0:
        first_right_ref = refs[12]
    slots = sorted_slots(list_ref, capacity)
    turbines = lax.axis_size("gx") * lax.axis_size("gy")
    listed = slots[0] < turbines

    if not last:
        sample_ref[...] = jnp.zeros(sample_ref.shape, jnp.float32)
        if past_ref is not None:
            sample_ref[: 3 * step + 3] = past_ref[: 3 * step + 3]

    rows = turbine_rows(rows_ref, table_ref, slots, step, points)
    store_factors(rows, listed, weight_ref, {1: push_right_ref, 0: first_right_ref} if step == 0 else {1: push_right_ref}, shape)

    even_x, even_z, even_y = is_even("gx"), is_even("gz"), is_even("gy")
    index_y, index_z = lax.axis_index("gy"), lax.axis_index("gz")
    tiles = count_y // 128
    for comp in range(4):
        for tile in range(tiles):
            there = slice(comp * count_x, (comp + 1) * count_x), slice(tile * 128, tile * 128 + 128)
            first, second = za_ref[there], zb_ref[there]
            low_z_ref[comp, tile] = pick(index_z == 0, 0.0, pick(even_z, second, first))
            high_z_ref[comp, tile] = pick(index_z == lax.axis_size("gz") - 1, 0.0, pick(even_z, first, second))
    low_y_ref[...] = pick(index_y == 0, 0.0, pick(even_y, yb_ref[:count_z], ya_ref[:count_z]))
    high_y_ref[...] = pick(index_y == lax.axis_size("gy") - 1, 0.0, pick(even_y, ya_ref[:count_z], yb_ref[:count_z]))
    first = x_refs[0][...]
    second = x_refs[1][...] if len(x_refs) > 1 else 0.0
    low_x_ref[...] = pick(even_x, second, first)
    high_x_ref[...] = pick(even_x, first, second)
    first_z, last_z, first_y, last_y = masks_of(shape)

    def plane(x, minus, plus):
        centre, up, down = [], [], []
        for comp in range(4):
            row = [q_ref[comp, x, :, tile * 128 : tile * 128 + 128] for tile in range(tiles)]
            place = comp * count_x + x
            turn = (128 - place) % 128 if isinstance(place, int) else 128 - place
            centre.append(row)
            up.append([pltpu.roll(low_y_ref[...], turn, 1)] + [pltpu.roll(c, 1, 1) for c in row])
            down.append([pltpu.roll(c, 127, 1) for c in row] + [pltpu.roll(high_y_ref[...], 127 - place, 1)])
        for tile in range(tiles):
            here = slice(tile * 128, tile * 128 + 128)
            shifts = []
            for comp in range(4):
                c = centre[comp][tile]
                minus_y = jnp.where(first_y, up[comp][tile], up[comp][tile + 1])
                plus_y = jnp.where(last_y, down[comp][tile + 1], down[comp][tile])
                low_z = low_z_ref[comp, tile, pl.ds(x, 1), :]
                high_z = high_z_ref[comp, tile, pl.ds(x, 1), :]
                minus_z = jnp.where(first_z, low_z, pltpu.roll(c, 1, 0))
                plus_z = jnp.where(last_z, high_z, pltpu.roll(c, count_z - 1, 0))
                shifts.append((c, minus(comp, here), plus(comp, here), minus_y, plus_y, minus_z, plus_z))
            pushed = [force_ref[comp, x, :, here] for comp in range(3)]
            for comp, value in enumerate(tile_update(shifts, pushed)):
                out_ref[comp, x, :, here] = value

    def of_plane(x):
        return lambda comp, here: q_ref[comp, x, :, here]

    def copy_out(number, start, count):
        here = pl.ds(start, count)
        return pltpu.make_async_copy(out_ref.at[:, here], far_ref.at[:, here], sems.at[number])

    group = max(g for g in range(1, 9) if count_x % g == 0)
    groups = count_x // group
    sums = [0.0] * 3
    first_sums = [0.0] * 3
    push(force_ref, rows, weight_ref, push_right_ref, 0, group, shape)
    for number in range(groups):
        start = number * group
        if number + 1 < groups:
            push(force_ref, rows, weight_ref, push_right_ref, start + group, group, shape)
        if step == 0:
            more = sample(q_ref, weight_ref, first_right_ref, start, group, shape)
            first_sums = [a + b for a, b in zip(first_sums, more)]
        for x in range(start, start + group):
            minus = of_plane(x - 1) if x else lambda comp, here: low_x_ref[comp, :, here]
            plus = of_plane(x + 1) if x < count_x - 1 else lambda comp, here: high_x_ref[comp, :, here]
            plane(x, minus, plus)
        if not last and not number:
            next_rows = turbine_rows(rows_ref, table_ref, slots, step + 1, points)
            store_factors(next_rows, listed, next_weight_ref, {0: sample_right_ref}, shape)
        if last:
            copy_out(number, start, group).start()
        elif number:
            more = sample(out_ref, next_weight_ref, sample_right_ref, start - group, group, shape)
            sums = [a + b for a, b in zip(sums, more)]
    if last:
        for number in range(groups):
            copy_out(number, number * group, group).wait()
        return
    write_faces(out_ref, face_refs, shape)
    more = sample(out_ref, next_weight_ref, sample_right_ref, count_x - group, group, shape)
    for comp in range(3):
        sample_ref[3 * step + 3 + comp : 3 * step + 4 + comp] = sums[comp] + more[comp]
        if step == 0:
            sample_ref[comp : comp + 1] = first_sums[comp]

    if packs:
        count = 3 * steps + 1
        za_ref = face_refs[0]
        start = 4 * count_x
        za_ref[start:] = jnp.zeros((za_ref.shape[0] - start, count_y), jnp.float32)
        for j, slot in enumerate(slots):
            lane, row = (j % 2) * points, start + (j // 2) * count
            values = sample_ref[: count - 1, j * points : (j + 1) * points]
            za_ref[row : row + count - 1, lane : lane + points] = values
            name = jnp.where(listed, 0.5 * (slot + 1).astype(jnp.float32), 0.0)
            za_ref[row + count - 1 : row + count, lane : lane + points] = jnp.full((1, points), name)


def face_shapes(shape, extra=0):
    count_x, count_z, count_y = shape
    forms = [(4 * count_x + extra, count_y), (4 * count_x, count_y)]
    forms += [(count_z, 128)] * 2 + [(4, count_z, count_y)] * (1 if lax.axis_size("gx") == 2 else 2)
    return [jax.ShapeDtypeStruct(form, jnp.float32) for form in forms]


def vmem_specs(count):
    return [pl.BlockSpec(memory_space=pltpu.VMEM)] * count


def swap_faces(faces):
    za, zb, ya, yb = faces[:4]
    zb, za = swap_inner(zb, "gz"), swap(za, "gz", 0)
    yb, ya = swap_inner(yb, "gy"), swap(ya, "gy", 0)
    halos = [za, zb, ya, yb]
    return halos + [swap(face, "gx", first) for first, face in enumerate(faces[4:])]


def masked(halo, axis, first):
    index = lax.axis_index(axis)
    partner = index + 1 - 2 * lax.rem(index + first, 2)
    inside = jnp.logical_and(partner >= 0, partner < lax.axis_size(axis))
    return jnp.where(inside, halo, 0.0)


def true_order(pieces, axis):
    distance = 1
    while distance < pieces.shape[0]:
        swapped = pieces.reshape((-1, 2, distance) + pieces.shape[1:])[:, ::-1].reshape(pieces.shape)
        odd = lax.rem(lax.div(lax.axis_index(axis), distance), 2) == 1
        pieces = jnp.where(odd, swapped, pieces)
        distance *= 2
    return pieces


def shards(flow, positions, loads, block_list):
    capacity = block_list.shape[-1]
    steps, _, _, part = positions.shape
    shape = flow.shape[1:]
    count_x, count_z, count_y = shape
    size_x, size_y, size_z = lax.axis_size("gx"), lax.axis_size("gy"), lax.axis_size("gz")
    points = part * size_z
    lanes = capacity * points
    params = pltpu.CompilerParams(vmem_limit_bytes=vmem_limit)
    q = flow
    turbines = block_list.reshape(capacity)
    barrier = lax.optimization_barrier
    forms = face_shapes(shape)

    extra = pl.cdiv((3 * steps + 1) * pl.cdiv(capacity, 2), 8) * 8

    own = jnp.concatenate([positions.reshape(steps, 3, part), loads.reshape(steps, 3, part)], axis=1)
    table = jnp.pad(own, ((0, 0), (0, 2), (0, 0))).reshape(1, 8 * steps, part)
    table = jnp.concatenate([table, from_distance(table, "gz", 1)], axis=0)
    faces = pl.pallas_call(
        functools.partial(faces_body, shape=shape),
        out_shape=forms,
        in_specs=[pl.BlockSpec(memory_space=pltpu.HBM)],
        out_specs=vmem_specs(len(forms)),
        scratch_shapes=[pltpu.VMEM(q.shape, jnp.float32), pltpu.SemaphoreType.DMA((4,))],
        compiler_params=params,
        name="faces",
    )(pltpu.with_memory_space_constraint(q, pltpu.HBM))
    table, faces = barrier((table, list(faces)))
    za, zb, ya, yb = faces[:4]
    za = masked(swap(za, "gz", 0), "gz", 0)
    distance = 2
    while distance < size_z:
        received = from_distance(table, "gz", distance)
        received, za = barrier((received, za))
        table = jnp.concatenate([table, received], axis=0)
        distance *= 2
    table = true_order(table, "gz")
    table = jnp.concatenate([table[k] for k in range(size_z)], axis=1)
    rows = 8 * steps
    zb, ya, table = barrier((zb, ya, table))
    zb = masked(swap_inner(zb, "gz"), "gz", 1)
    ya = swap(jnp.concatenate([ya, table], axis=0), "gy", 0)
    ya, zb = barrier((ya, zb))
    table = jnp.concatenate([table, ya[count_z:]], axis=0)
    yb = from_distance(jnp.concatenate([yb, table], axis=0), "gy", 3)
    x_faces = [swap(face, "gx", first) for first, face in enumerate(faces[4:])]
    table = jnp.concatenate([table, yb[count_z:]], axis=0)
    table = gather_relative(table[None], "gx").reshape(size_x * size_y, rows, points)
    halos = [za, zb, ya, yb] + x_faces

    samples = None
    for step in range(steps):
        last, packs = step == steps - 1, step == steps - 2
        shapes = [jax.ShapeDtypeStruct(q.shape, jnp.float32)]
        out_specs = vmem_specs(1)
        scratch = []
        if last:
            out_specs = [pl.BlockSpec(memory_space=pl.ANY)]
            scratch = [pltpu.VMEM(q.shape, jnp.float32), pltpu.SemaphoreType.DMA((count_x,))]
        else:
            shapes += face_shapes(shape, extra if packs else 0)
            if packs:
                scratch = [pltpu.VMEM((16, lanes), jnp.float32)]
            else:
                shapes += [jax.ShapeDtypeStruct((16, lanes), jnp.float32)]
            out_specs = vmem_specs(len(shapes))
        past = [] if step == 0 or last else [samples]
        results = pl.pallas_call(
            functools.partial(step_body, shape=shape, points=points, capacity=capacity, step=step, steps=steps),
            out_shape=shapes,
            in_specs=[pl.BlockSpec(memory_space=pltpu.SMEM)] + vmem_specs(2 + len(halos) + len(past)),
            out_specs=out_specs,
            scratch_shapes=scratch
            + [pltpu.VMEM((3,) + shape, jnp.float32), pltpu.VMEM((8, lanes), jnp.float32)]
            + [pltpu.VMEM((4, count_y // 128, count_x, 128), jnp.float32)] * 2
            + [pltpu.VMEM((count_z, 128), jnp.float32)] * 2
            + [pltpu.VMEM((4, count_z, count_y), jnp.float32)] * 2
            + [pltpu.VMEM((count_x, count_z, lanes), jnp.float32), pltpu.VMEM((count_y, 3 * lanes), jnp.bfloat16)]
            + ([] if last else [pltpu.VMEM((count_x, count_z, lanes), jnp.float32)])
            + ([] if last else [pltpu.VMEM((3 * count_y, lanes), jnp.bfloat16)])
            + ([pltpu.VMEM((3 * count_y, lanes), jnp.bfloat16)] if step == 0 else []),
            compiler_params=params,
            name="step",
        )(turbines, table, q, *halos, *past)
        q = results[0]
        if last:
            break
        faces = results[1 : 1 + len(forms)]
        if not packs:
            samples = results[-1]
            halos = swap_faces(faces)
            continue
        za, zb, ya, yb = faces[:4]
        za_in, zb_in = swap(za, "gz", 0), swap_inner(zb, "gz")
        sums = za[4 * count_x :] + za_in[4 * count_x :]
        pieces = jnp.concatenate([sums[:, h * 128 : h * 128 + 128] for h in range(2)], axis=0)
        pieces, ya, zb_in = barrier((pieces, ya, zb_in))
        ya_in = swap(jnp.concatenate([ya, pieces], axis=0), "gy", 0)
        x_faces = [swap(face, "gx", first) for first, face in enumerate(faces[4:])]
        pieces = jnp.concatenate([pieces, ya_in[count_z:]], axis=0).reshape(2, -1, points)
        pieces, yb, x_faces = barrier((pieces, yb, x_faces))
        pieces = gather_relative(pieces, "gy", 2).reshape(-1, points)
        yb_in = swap_inner(yb, "gy")
        pieces, yb_in = barrier((pieces, yb_in))
        halos = [za_in, zb_in, ya_in, yb_in] + x_faces

    distance = 2
    while distance < size_z:
        pieces = pieces + from_distance(pieces, "gz", distance)
        distance *= 2
    pieces, q = barrier((pieces, q))
    mine = lax.dynamic_slice_in_dim(pieces, lax.axis_index("gz") * part, part, axis=1)[None]
    mine = gather_relative(mine, "gx").reshape(size_x * size_y, 2, extra, part)
    holder = (lax.axis_index("gx") * size_y + lax.axis_index("gy") + 1).astype(jnp.float32)
    returned = 0.0
    for j in range(capacity):
        row = (j // 2) * (3 * steps + 1)
        values = mine[:, j % 2, row : row + 3 * steps]
        match = mine[:, j % 2, row + 3 * steps :][:, :1] == holder
        returned = returned + jnp.sum(jnp.where(match, values, 0.0), axis=0)
    return q, returned.reshape(positions.shape)


def solution(mesh):
    in_specs = (
        P(None, "gx", "gz", "gy"),
        P(None, None, ("gx", "gy"), "gz"),
        P(None, None, ("gx", "gy"), "gz"),
        P("gx", "gy", "gz", None),
    )
    out_specs = (P(None, "gx", "gz", "gy"), P(None, None, ("gx", "gy"), "gz"))
    return jax.shard_map(shards, mesh=mesh, in_specs=in_specs, out_specs=out_specs, check_vma=False)
```

```python
import functools
import math

import jax
import jax.numpy as jnp
from jax import lax
from jax.experimental import pallas as pl
from jax.experimental.pallas import tpu as pltpu
from jax.sharding import PartitionSpec as P

kernel_width = 2.0
kernel_norm = 1.0 / (math.pi**1.5 * kernel_width**3)
time_step = 0.1
smag_coef = 0.17
viscosity = 0.02
diffusivity = 0.02
prandtl = 0.4
vmem_limit = 24 << 20


def swap_pairs(count, first):
    pairs = []
    for low in range(first, count - 1, 2):
        pairs += [(low, low + 1), (low + 1, low)]
    return pairs


def swap(value, axis, first):
    pairs = swap_pairs(lax.axis_size(axis), first)
    if not pairs:
        return jnp.zeros_like(value)
    return lax.ppermute(value, axis, pairs)


def swap_inner(value, axis):
    size, chips = lax.axis_size(axis), lax.axis_size("gx")
    target = {low: high for low, high in swap_pairs(size, 1)}
    pairs = []
    for x in range(chips):
        for k in range(size):
            pairs.append((x * size + k, x * size + target[k] if k in target else (x ^ 1) * size + k))
    return lax.ppermute(value, ("gx", axis), pairs)


def from_distance(value, axis, distance):
    count = lax.axis_size(axis)
    return lax.ppermute(value, axis, [(i, i ^ distance) for i in range(count)])


def gather_relative(value, axis, distance=1):
    while distance < lax.axis_size(axis):
        value = jnp.concatenate([value, from_distance(value, axis, distance)], axis=0)
        distance *= 2
    return value


def pick(flag, first, second):
    return jnp.where(flag, first, second)


def is_even(axis):
    return lax.rem(lax.axis_index(axis), 2) == 0


def write_faces(q_ref, face_refs, shape):
    count_x, count_z, count_y = shape
    za_ref, zb_ref, ya_ref, yb_ref, xa_ref = face_refs[:5]
    even_x, even_z, even_y = is_even("gx"), is_even("gz"), is_even("gy")
    low, high = q_ref[:, 0], q_ref[:, count_x - 1]
    xa_ref[...] = pick(even_x, high, low)
    for xb_ref in face_refs[5:]:
        xb_ref[...] = pick(even_x, low, high)
    for comp in range(4):
        low = q_ref[comp, :, 0, :]
        high = q_ref[comp, :, count_z - 1, :]
        za_ref[comp * count_x : (comp + 1) * count_x] = pick(even_z, high, low)
        zb_ref[comp * count_x : (comp + 1) * count_x] = pick(even_z, low, high)
    lane = lax.broadcasted_iota(jnp.int32, (count_z, 128), 1)
    low = jnp.zeros((count_z, 128), jnp.float32)
    high = jnp.zeros((count_z, 128), jnp.float32)
    for comp in range(4):
        for x in range(count_x):
            place = comp * count_x + x
            first = q_ref[comp, x, :, :128]
            last = q_ref[comp, x, :, count_y - 128 :]
            low = jnp.where(lane == place, pltpu.roll(first, place, 1), low)
            high = jnp.where(lane == place, pltpu.roll(last, (place + 1) % 128, 1), high)
    ya_ref[...] = pick(even_y, high, low)
    yb_ref[...] = pick(even_y, low, high)


def faces_body(q_ref, *face_refs, shape):
    write_faces(q_ref, face_refs, shape)


def sorted_slots(list_ref, capacity):
    slots = [list_ref[j] for j in range(capacity)]
    for first in range(capacity):
        for second in range(first + 1, capacity):
            a, b = slots[first], slots[second]
            slots[first], slots[second] = jnp.minimum(a, b), jnp.maximum(a, b)
    return slots


def masks_of(shape):
    count_z = shape[1]
    sub = lax.broadcasted_iota(jnp.int32, (count_z, 128), 0)
    lane = lax.broadcasted_iota(jnp.int32, (count_z, 128), 1)
    return sub == 0, sub == count_z - 1, lane == 0, lane == 127


def tile_update(shifts, pushed):
    diffs, laplace, centre = [], [], []
    for c, minus_x, plus_x, minus_y, plus_y, minus_z, plus_z in shifts:
        diffs.append((plus_x - minus_x, plus_y - minus_y, plus_z - minus_z))
        laplace.append((plus_x + minus_x) + (plus_y + minus_y) + (plus_z + minus_z) - 6.0 * c)
        centre.append(c)
    diagonal = diffs[0][0] * diffs[0][0] + diffs[1][1] * diffs[1][1] + diffs[2][2] * diffs[2][2]
    xy = diffs[0][1] + diffs[1][0]
    xz = diffs[0][2] + diffs[2][0]
    yz = diffs[1][2] + diffs[2][1]
    total = (diagonal + diagonal) + (xy * xy + xz * xz + yz * yz)
    root = total * lax.rsqrt(jnp.maximum(total, 1.1754944e-38))
    scale_u = time_step * viscosity + (0.5 * time_step * smag_coef**2) * root
    scale_t = time_step * diffusivity + (0.5 * time_step * smag_coef**2 / prandtl) * root
    half = [0.5 * time_step * centre[a] for a in range(3)]
    out = []
    for comp in range(4):
        d = diffs[comp]
        moved = half[0] * d[0] + half[1] * d[1] + half[2] * d[2]
        value = centre[comp] - moved + (scale_u if comp < 3 else scale_t) * laplace[comp]
        out.append(value + pushed[comp] if comp < 3 else value)
    return out


def split(value):
    high = value.astype(jnp.bfloat16)
    low = (value - high.astype(jnp.float32)).astype(jnp.bfloat16)
    return high, low


def turbine_rows(rows_ref, table_ref, slots, step, points):
    size_x, size_y = lax.axis_size("gx"), lax.axis_size("gy")
    for j, slot in enumerate(slots):
        t = jnp.minimum(slot, size_x * size_y - 1)
        place_x = lax.bitwise_xor(lax.div(t, size_y), lax.axis_index("gx"))
        place_y = lax.bitwise_xor(lax.rem(t, size_y), lax.axis_index("gy"))
        entry = place_x * size_y + lax.bitwise_xor(place_y, lax.div(place_y, 2))
        rows_ref[:, j * points : (j + 1) * points] = table_ref[entry, 8 * step : 8 * step + 8, :]
    return rows_ref[...]


def point_factors(rows, listed, shape):
    lanes = rows.shape[1]

    def factor(row, axis, count):
        start = (lax.axis_index(axis) * count).astype(jnp.float32)
        cells = lax.broadcasted_iota(jnp.int32, (count, lanes), 0).astype(jnp.float32) + start
        gap = cells - row
        return jnp.exp(-(gap * gap) / kernel_width**2)

    count_x, count_z, count_y = shape
    factor_x = factor(rows[0:1], "gx", count_x)
    factor_y = factor(rows[1:2], "gy", count_y)
    factor_z = factor(rows[2:3], "gz", count_z) * jnp.where(listed, kernel_norm, 0.0)
    weights = (factor_x[:, None, :] * factor_z[None, :, :]).reshape(count_x * count_z, lanes)
    return weights, split(factor_y)


def store_factors(rows, listed, weight_ref, right_refs, shape):
    weights, (high, low) = point_factors(rows, listed, shape)
    weight_ref[...] = weights.reshape(weight_ref.shape)
    for axis, right_ref in right_refs.items():
        right_ref[...] = jnp.concatenate([high, high, low], axis=axis)


def push(force_ref, rows, weight_ref, right_ref, start, planes, shape):
    count_z = shape[1]
    weights = weight_ref[start : start + planes].reshape(planes * count_z, -1)
    left = []
    for comp in range(3):
        first, second = split(weights * (rows[3 + comp : 4 + comp] * time_step))
        left.append(jnp.concatenate([first, second, first], axis=1))
    left = jnp.concatenate(left, axis=0)
    pushed = lax.dot_general(left, right_ref[...], (((1,), (1,)), ((), ())), preferred_element_type=jnp.float32)
    force_ref[:, start : start + planes] = pushed.reshape((3, planes) + shape[1:])


def sample(q_ref, weight_ref, right_ref, start, planes, shape):
    count_z = shape[1]
    left = []
    for comp in range(3):
        first, second = split(q_ref[comp, start : start + planes].reshape(planes * count_z, -1))
        left.append(jnp.concatenate([first, second, first], axis=1))
    along = jnp.dot(jnp.concatenate(left, axis=0), right_ref[...], preferred_element_type=jnp.float32)
    weights = weight_ref[start : start + planes].reshape(planes * count_z, -1)
    rows = planes * count_z
    return [jnp.sum(along[k * rows : (k + 1) * rows] * weights, axis=0, keepdims=True) for k in range(3)]


def step_body(*refs, shape, points, capacity, step, steps):
    count_x, count_z, count_y = shape
    last, packs = step == steps - 1, step == steps - 2
    faces = len(face_shapes(shape))
    refs = list(refs)
    list_ref, table_ref, q_ref = refs[:3]
    za_ref, zb_ref, ya_ref, yb_ref = refs[3:7]
    x_refs, refs = refs[7 : 3 + faces], refs[3 + faces :]
    past_ref = None if step == 0 or last else refs.pop(0)
    out_ref = refs.pop(0)
    sample_ref = None
    if not last:
        face_refs, refs = refs[:faces], refs[faces:]
        sample_ref = refs.pop(0)
    else:
        far_ref, out_ref, sems = out_ref, refs.pop(0), refs.pop(0)
    force_ref, rows_ref, low_z_ref, high_z_ref, low_y_ref, high_y_ref, low_x_ref, high_x_ref = refs[:8]
    weight_ref, push_right_ref = refs[8:10]
    if not last:
        next_weight_ref, sample_right_ref = refs[10:12]
    if step == 0:
        first_right_ref = refs[12]
    slots = sorted_slots(list_ref, capacity)
    turbines = lax.axis_size("gx") * lax.axis_size("gy")
    listed = slots[0] < turbines

    if not last:
        sample_ref[...] = jnp.zeros(sample_ref.shape, jnp.float32)
        if past_ref is not None:
            sample_ref[: 3 * step + 3] = past_ref[: 3 * step + 3]

    rows = turbine_rows(rows_ref, table_ref, slots, step, points)
    store_factors(rows, listed, weight_ref, {1: push_right_ref, 0: first_right_ref} if step == 0 else {1: push_right_ref}, shape)

    even_x, even_z, even_y = is_even("gx"), is_even("gz"), is_even("gy")
    index_y, index_z = lax.axis_index("gy"), lax.axis_index("gz")
    tiles = count_y // 128
    for comp in range(4):
        for tile in range(tiles):
            there = slice(comp * count_x, (comp + 1) * count_x), slice(tile * 128, tile * 128 + 128)
            first, second = za_ref[there], zb_ref[there]
            low_z_ref[comp, tile] = pick(index_z == 0, 0.0, pick(even_z, second, first))
            high_z_ref[comp, tile] = pick(index_z == lax.axis_size("gz") - 1, 0.0, pick(even_z, first, second))
    low_y_ref[...] = pick(index_y == 0, 0.0, pick(even_y, yb_ref[:count_z], ya_ref[:count_z]))
    high_y_ref[...] = pick(index_y == lax.axis_size("gy") - 1, 0.0, pick(even_y, ya_ref[:count_z], yb_ref[:count_z]))
    first = x_refs[0][...]
    second = x_refs[1][...] if len(x_refs) > 1 else 0.0
    low_x_ref[...] = pick(even_x, second, first)
    high_x_ref[...] = pick(even_x, first, second)
    first_z, last_z, first_y, last_y = masks_of(shape)

    def plane(x, minus, plus):
        centre, up, down = [], [], []
        for comp in range(4):
            row = [q_ref[comp, x, :, tile * 128 : tile * 128 + 128] for tile in range(tiles)]
            place = comp * count_x + x
            turn = (128 - place) % 128 if isinstance(place, int) else 128 - place
            centre.append(row)
            up.append([pltpu.roll(low_y_ref[...], turn, 1)] + [pltpu.roll(c, 1, 1) for c in row])
            down.append([pltpu.roll(c, 127, 1) for c in row] + [pltpu.roll(high_y_ref[...], 127 - place, 1)])
        for tile in range(tiles):
            here = slice(tile * 128, tile * 128 + 128)
            shifts = []
            for comp in range(4):
                c = centre[comp][tile]
                minus_y = jnp.where(first_y, up[comp][tile], up[comp][tile + 1])
                plus_y = jnp.where(last_y, down[comp][tile + 1], down[comp][tile])
                low_z = low_z_ref[comp, tile, pl.ds(x, 1), :]
                high_z = high_z_ref[comp, tile, pl.ds(x, 1), :]
                minus_z = jnp.where(first_z, low_z, pltpu.roll(c, 1, 0))
                plus_z = jnp.where(last_z, high_z, pltpu.roll(c, count_z - 1, 0))
                shifts.append((c, minus(comp, here), plus(comp, here), minus_y, plus_y, minus_z, plus_z))
            pushed = [force_ref[comp, x, :, here] for comp in range(3)]
            for comp, value in enumerate(tile_update(shifts, pushed)):
                out_ref[comp, x, :, here] = value

    def of_plane(x):
        return lambda comp, here: q_ref[comp, x, :, here]

    def copy_out(number, start, count):
        here = pl.ds(start, count)
        return pltpu.make_async_copy(out_ref.at[:, here], far_ref.at[:, here], sems.at[number])

    group = max(g for g in range(1, 9) if count_x % g == 0)
    groups = count_x // group
    sums = [0.0] * 3
    first_sums = [0.0] * 3
    push(force_ref, rows, weight_ref, push_right_ref, 0, group, shape)
    for number in range(groups):
        start = number * group
        if number + 1 < groups:
            push(force_ref, rows, weight_ref, push_right_ref, start + group, group, shape)
        if step == 0:
            more = sample(q_ref, weight_ref, first_right_ref, start, group, shape)
            first_sums = [a + b for a, b in zip(first_sums, more)]
        for x in range(start, start + group):
            minus = of_plane(x - 1) if x else lambda comp, here: low_x_ref[comp, :, here]
            plus = of_plane(x + 1) if x < count_x - 1 else lambda comp, here: high_x_ref[comp, :, here]
            plane(x, minus, plus)
        if not last and not number:
            next_rows = turbine_rows(rows_ref, table_ref, slots, step + 1, points)
            store_factors(next_rows, listed, next_weight_ref, {0: sample_right_ref}, shape)
        if last:
            copy_out(number, start, group).start()
        elif number:
            more = sample(out_ref, next_weight_ref, sample_right_ref, start - group, group, shape)
            sums = [a + b for a, b in zip(sums, more)]
    if last:
        for number in range(groups):
            copy_out(number, number * group, group).wait()
        return
    write_faces(out_ref, face_refs, shape)
    more = sample(out_ref, next_weight_ref, sample_right_ref, count_x - group, group, shape)
    for comp in range(3):
        sample_ref[3 * step + 3 + comp : 3 * step + 4 + comp] = sums[comp] + more[comp]
        if step == 0:
            sample_ref[comp : comp + 1] = first_sums[comp]

    if packs:
        count = 3 * steps + 1
        za_ref = face_refs[0]
        start = 4 * count_x
        za_ref[start:] = jnp.zeros((za_ref.shape[0] - start, count_y), jnp.float32)
        for j, slot in enumerate(slots):
            lane, row = (j % 2) * points, start + (j // 2) * count
            values = sample_ref[: count - 1, j * points : (j + 1) * points]
            za_ref[row : row + count - 1, lane : lane + points] = values
            name = jnp.where(listed, 0.5 * (slot + 1).astype(jnp.float32), 0.0)
            za_ref[row + count - 1 : row + count, lane : lane + points] = jnp.full((1, points), name)


def face_shapes(shape, extra=0):
    count_x, count_z, count_y = shape
    forms = [(4 * count_x + extra, count_y), (4 * count_x, count_y)]
    forms += [(count_z, 128)] * 2 + [(4, count_z, count_y)] * (1 if lax.axis_size("gx") == 2 else 2)
    return [jax.ShapeDtypeStruct(form, jnp.float32) for form in forms]


def vmem_specs(count):
    return [pl.BlockSpec(memory_space=pltpu.VMEM)] * count


def swap_faces(faces):
    za, zb, ya, yb = faces[:4]
    zb, za = swap_inner(zb, "gz"), swap(za, "gz", 0)
    yb, ya = swap_inner(yb, "gy"), swap(ya, "gy", 0)
    halos = [za, zb, ya, yb]
    return halos + [swap(face, "gx", first) for first, face in enumerate(faces[4:])]


def masked(halo, axis, first):
    index = lax.axis_index(axis)
    partner = index + 1 - 2 * lax.rem(index + first, 2)
    inside = jnp.logical_and(partner >= 0, partner < lax.axis_size(axis))
    return jnp.where(inside, halo, 0.0)


def true_order(pieces, axis):
    distance = 1
    while distance < pieces.shape[0]:
        swapped = pieces.reshape((-1, 2, distance) + pieces.shape[1:])[:, ::-1].reshape(pieces.shape)
        odd = lax.rem(lax.div(lax.axis_index(axis), distance), 2) == 1
        pieces = jnp.where(odd, swapped, pieces)
        distance *= 2
    return pieces


def shards(flow, positions, loads, block_list):
    capacity = block_list.shape[-1]
    steps, _, _, part = positions.shape
    shape = flow.shape[1:]
    count_x, count_z, count_y = shape
    size_x, size_y, size_z = lax.axis_size("gx"), lax.axis_size("gy"), lax.axis_size("gz")
    points = part * size_z
    lanes = capacity * points
    params = pltpu.CompilerParams(vmem_limit_bytes=vmem_limit)
    q = flow
    turbines = block_list.reshape(capacity)
    barrier = lax.optimization_barrier
    forms = face_shapes(shape)

    extra = pl.cdiv((3 * steps + 1) * pl.cdiv(capacity, 2), 8) * 8

    own = jnp.concatenate([positions.reshape(steps, 3, part), loads.reshape(steps, 3, part)], axis=1)
    table = jnp.pad(own, ((0, 0), (0, 2), (0, 0))).reshape(1, 8 * steps, part)
    table = jnp.concatenate([table, from_distance(table, "gz", 1)], axis=0)
    faces = pl.pallas_call(
        functools.partial(faces_body, shape=shape),
        out_shape=forms,
        in_specs=vmem_specs(1),
        out_specs=vmem_specs(len(forms)),
        compiler_params=params,
        name="faces",
    )(q)
    table, faces = barrier((table, list(faces)))
    za, zb, ya, yb = faces[:4]
    za = masked(swap(za, "gz", 0), "gz", 0)
    distance = 2
    while distance < size_z:
        received = from_distance(table, "gz", distance)
        received, za = barrier((received, za))
        table = jnp.concatenate([table, received], axis=0)
        distance *= 2
    table = true_order(table, "gz")
    table = jnp.concatenate([table[k] for k in range(size_z)], axis=1)
    rows = 8 * steps
    zb, ya, table = barrier((zb, ya, table))
    zb = masked(swap_inner(zb, "gz"), "gz", 1)
    ya = swap(jnp.concatenate([ya, table], axis=0), "gy", 0)
    ya, zb = barrier((ya, zb))
    table = jnp.concatenate([table, ya[count_z:]], axis=0)
    yb = from_distance(jnp.concatenate([yb, table], axis=0), "gy", 3)
    x_faces = [swap(face, "gx", first) for first, face in enumerate(faces[4:])]
    table = jnp.concatenate([table, yb[count_z:]], axis=0)
    table = gather_relative(table[None], "gx").reshape(size_x * size_y, rows, points)
    halos = [za, zb, ya, yb] + x_faces

    samples = None
    for step in range(steps):
        last, packs = step == steps - 1, step == steps - 2
        shapes = [jax.ShapeDtypeStruct(q.shape, jnp.float32)]
        out_specs = vmem_specs(1)
        scratch = []
        if last:
            out_specs = [pl.BlockSpec(memory_space=pl.ANY)]
            scratch = [pltpu.VMEM(q.shape, jnp.float32), pltpu.SemaphoreType.DMA((count_x,))]
        else:
            shapes += face_shapes(shape, extra if packs else 0)
            if packs:
                scratch = [pltpu.VMEM((16, lanes), jnp.float32)]
            else:
                shapes += [jax.ShapeDtypeStruct((16, lanes), jnp.float32)]
            out_specs = vmem_specs(len(shapes))
        past = [] if step == 0 or last else [samples]
        results = pl.pallas_call(
            functools.partial(step_body, shape=shape, points=points, capacity=capacity, step=step, steps=steps),
            out_shape=shapes,
            in_specs=[pl.BlockSpec(memory_space=pltpu.SMEM)] + vmem_specs(2 + len(halos) + len(past)),
            out_specs=out_specs,
            scratch_shapes=scratch
            + [pltpu.VMEM((3,) + shape, jnp.float32), pltpu.VMEM((8, lanes), jnp.float32)]
            + [pltpu.VMEM((4, count_y // 128, count_x, 128), jnp.float32)] * 2
            + [pltpu.VMEM((count_z, 128), jnp.float32)] * 2
            + [pltpu.VMEM((4, count_z, count_y), jnp.float32)] * 2
            + [pltpu.VMEM((count_x, count_z, lanes), jnp.float32), pltpu.VMEM((count_y, 3 * lanes), jnp.bfloat16)]
            + ([] if last else [pltpu.VMEM((count_x, count_z, lanes), jnp.float32)])
            + ([] if last else [pltpu.VMEM((3 * count_y, lanes), jnp.bfloat16)])
            + ([pltpu.VMEM((3 * count_y, lanes), jnp.bfloat16)] if step == 0 else []),
            compiler_params=params,
            name="step",
        )(turbines, table, q, *halos, *past)
        q = results[0]
        if last:
            break
        faces = results[1 : 1 + len(forms)]
        if not packs:
            samples = results[-1]
            halos = swap_faces(faces)
            continue
        za, zb, ya, yb = faces[:4]
        zb_in = swap_inner(zb, "gz")
        za_in = swap(za, "gz", 0)
        sums = za[4 * count_x :] + za_in[4 * count_x :]
        pieces = jnp.concatenate([sums[:, h * 128 : h * 128 + 128] for h in range(2)], axis=0)
        zb_in = masked(zb_in, "gz", 1)
        pieces, ya, zb_in = barrier((pieces, ya, zb_in))
        ya_in = swap(jnp.concatenate([ya, pieces], axis=0), "gy", 0)
        x_faces = [swap(face, "gx", first) for first, face in enumerate(faces[4:])]
        pieces = jnp.concatenate([pieces, ya_in[count_z:]], axis=0).reshape(2, -1, points)
        pieces, yb, x_faces = barrier((pieces, yb, x_faces))
        pieces = gather_relative(pieces, "gy", 2).reshape(-1, points)
        yb_in = swap_inner(yb, "gy")
        pieces, yb_in = barrier((pieces, yb_in))
        halos = [za_in, zb_in, ya_in, yb_in] + x_faces

    distance = 2
    while distance < size_z:
        pieces = pieces + from_distance(pieces, "gz", distance)
        distance *= 2
    pieces, q = barrier((pieces, q))
    mine = lax.dynamic_slice_in_dim(pieces, lax.axis_index("gz") * part, part, axis=1)[None]
    mine = gather_relative(mine, "gx").reshape(size_x * size_y, 2, extra, part)
    holder = (lax.axis_index("gx") * size_y + lax.axis_index("gy") + 1).astype(jnp.float32)
    returned = 0.0
    for j in range(capacity):
        row = (j // 2) * (3 * steps + 1)
        values = mine[:, j % 2, row : row + 3 * steps]
        match = mine[:, j % 2, row + 3 * steps :][:, :1] == holder
        returned = returned + jnp.sum(jnp.where(match, values, 0.0), axis=0)
    return q, returned.reshape(positions.shape)


def solution(mesh):
    in_specs = (
        P(None, "gx", "gz", "gy"),
        P(None, None, ("gx", "gy"), "gz"),
        P(None, None, ("gx", "gy"), "gz"),
        P("gx", "gy", "gz", None),
    )
    out_specs = (P(None, "gx", "gz", "gy"), P(None, None, ("gx", "gy"), "gz"))
    return jax.shard_map(shards, mesh=mesh, in_specs=in_specs, out_specs=out_specs, check_vma=False)
```
